512 devices in a mesh: section: 16 (over x_hi, y), fsdp: 32 (over x_lo, z, core).
Axes of the slice: x: 4 (x_hi: 2, x_lo: 2; x = x_hi * 2 + x_lo), y: 8, z: 8, core: 2. Of those that a mesh axis runs over, the one named last changes fastest.
Arguments:
- inputs: bfloat16 [16, 8, 1024, 4096], P('section', None, 'fsdp'), may hold values from -6 to 6
- upstream: bfloat16 [8, 1024, 4096], P(None, 'fsdp'), may hold values from -6 to 6
- weights: bfloat16 [16, 4096, 512], P('section', 'fsdp')
- gain: bfloat16 [16, 4096], P('section', 'fsdp'), may hold values from 0.5 to 1.5
Outputs:
- weight_grad: float32 [16, 4096, 512], P('section', 'fsdp')
- gain_grad: float32 [16, 4096], P('section')
The draws below stay inside these ranges and needn't reach their ends.
All inputs are finite; a program needn't handle non-finite values.
Results may differ from the reference program's by a relative error of at most 0.035.
Values may be sent and summed in bfloat16 or wider, within the bound.
No kernel may reach another device: no remote copies, remote signals or barrier semaphores. Data moves between devices by JAX's collectives and lax.ppermute only.
A program may use at most 128 MiB of HBM per device.

```python
import jax
import jax.numpy as jnp
from jax import lax

D = 4096
HD = 128
TMB = 32
MB = 8
SECTIONS = 16
TOKENS = 1024
N_FSDP = 32


def draw_weights(key, part):
    layout = (SECTIONS, D, 4 * HD)
    return (jax.random.normal(key, layout, jnp.float32) * D ** (-0.5)).astype(jnp.bfloat16)


def shard_levels(own_key, extent, split, least, largest):
    def one(axis_at, blocks):
        steps = jax.random.uniform(jax.random.fold_in(jax.random.fold_in(own_key, 6), axis_at), (blocks,), jnp.float32, least / len(split), largest / len(split))
        return jnp.repeat(jnp.exp(steps), extent[axis_at] // blocks).reshape((-1,) + (1,) * (len(extent) - axis_at - 1))

    loudness = one(*split[0])
    for cut in split[1:]:
        loudness = loudness * one(*cut)
    return loudness


def centred(own_key, shape, scale, bound, split=(), kind=jnp.bfloat16):
    factor_of = shard_levels(own_key, shape, split, -0.22, 0.18) if split else 1.0
    values = jax.random.normal(own_key, shape, jnp.float32) * scale * factor_of
    return jnp.minimum(jnp.maximum(values, -bound), bound).astype(kind)


def setup_inputs(seed: int = 0) -> dict:
    key_of = jax.random.split(jax.random.key(seed), 5)
    inputs = centred(key_of[0], (SECTIONS, MB, TOKENS, D), 1.0, 6.0, ((0, 16), (2, 32)))
    upstream = centred(key_of[1], (MB, TOKENS, D), 1.0, 6.0, ((1, 32),))
    weights = draw_weights(jax.random.fold_in(key_of[4], 71), 0)
    gain = jnp.clip(0.5 + 1.0 * jax.random.uniform(key_of[3], (SECTIONS, D), jnp.float32) ** shard_levels(key_of[3], (SECTIONS, D), ((0, 16), (1, 32)), -0.2, 0.2), 0.5, 1.5).astype(jnp.bfloat16)
    return {"inputs": inputs, "upstream": upstream, "weights": weights, "gain": gain}


def rope_tables(length, head):
    half_head = head // 2
    position = jnp.arange(length, dtype=jnp.float32)
    freq = jnp.power(500000.0, -2.0 * jnp.arange(half_head, dtype=jnp.float32) / head)
    angle = position[:, None] * freq[None, :]
    return (jnp.cos(angle), jnp.sin(angle))

def rotate(value_rows, cosine, sine_table):
    half_head = value_rows.shape[-1] // 2
    first = value_rows[..., :half_head]
    second = value_rows[..., half_head:]
    return jnp.concatenate([first * cosine - second * sine_table, second * cosine + first * sine_table], axis=-1)

def unrotate(value_rows, cosine, sine_table):
    half_head = value_rows.shape[-1] // 2
    first = value_rows[..., :half_head]
    second = value_rows[..., half_head:]
    return jnp.concatenate([first * cosine + second * sine_table, second * cosine - first * sine_table], axis=-1)

def section_pass(inputs_m, weight, gain_row, grad_in):
    seqs, length, width = inputs_m.shape
    head = weight.shape[1] // 4
    cosine, sine_table = rope_tables(length, head)
    xfloat = inputs_m.astype(jnp.float32)
    inv_rms = lax.rsqrt(lax.optimization_barrier(jnp.mean(xfloat * xfloat, axis=-1, keepdims=True)) + 1e-05)
    normed = xfloat * inv_rms
    wide_gain = gain_row.astype(jnp.float32)
    hidden = (normed * wide_gain).astype(jnp.bfloat16)
    proj = jnp.dot(hidden.reshape(-1, width), weight[:, :3 * head], preferred_element_type=jnp.float32)
    proj = proj.reshape(seqs, length, 3 * head)
    query_rows = rotate(proj[..., :head], cosine, sine_table).astype(jnp.bfloat16)
    key_rows = rotate(proj[..., head:2 * head], cosine, sine_table).astype(jnp.bfloat16)
    value_rows = proj[..., 2 * head:].astype(jnp.bfloat16)
    score_scale = head ** (-0.5)
    score_matrix = jnp.einsum('onr,oir->oni', query_rows.astype(jnp.float32), key_rows.astype(jnp.float32)) * score_scale
    causal = jnp.arange(length)[:, None] >= jnp.arange(length)[None, :]
    score_matrix = jnp.where(causal, score_matrix, -1e+30)
    probs = jax.nn.softmax(score_matrix, axis=-1)
    probability_matrix = probs.astype(jnp.bfloat16)
    attended_output = jnp.einsum('wfx,wxh->wfh', probability_matrix.astype(jnp.float32), value_rows.astype(jnp.float32)).astype(jnp.bfloat16)
    attention_gradient = jnp.dot(grad_in.reshape(-1, width), weight[:, 3 * head:], preferred_element_type=jnp.float32)
    attention_gradient = attention_gradient.reshape(seqs, length, head).astype(jnp.bfloat16)
    probability_gradient = jnp.einsum('onr,oir->oni', attention_gradient.astype(jnp.float32), value_rows.astype(jnp.float32))
    score_gradient = probs * (probability_gradient - lax.optimization_barrier(jnp.sum(probability_gradient * probs, axis=-1, keepdims=True))) * score_scale
    score_gradient = score_gradient.astype(jnp.bfloat16).astype(jnp.float32)
    query_gradient = jnp.einsum('wfx,wxh->wfh', score_gradient, key_rows.astype(jnp.float32))
    key_gradient = jnp.einsum('cof,cod->cfd', score_gradient, query_rows.astype(jnp.float32))
    value_gradient = jnp.einsum('cof,cod->cfd', probability_matrix.astype(jnp.float32), attention_gradient.astype(jnp.float32))
    grad_proj = jnp.concatenate([unrotate(query_gradient, cosine, sine_table), unrotate(key_gradient, cosine, sine_table), value_gradient], axis=-1).astype(jnp.bfloat16)
    grad_hidden = lax.dot_general(grad_proj.reshape(-1, 3 * head), weight[:, :3 * head], (((1,), (1,)), ((), ())), preferred_element_type=jnp.float32)
    grad_hidden = grad_hidden.reshape(seqs, length, width)
    gain_term = lax.optimization_barrier(jnp.sum(grad_hidden * normed, axis=(0, 1)))
    grad_normed = grad_hidden * wide_gain
    grad_x = inv_rms * (grad_normed - normed * lax.optimization_barrier(jnp.mean(grad_normed * normed, axis=-1, keepdims=True)))
    grad_out = (grad_in.astype(jnp.float32) + grad_x).astype(jnp.bfloat16)
    return (grad_out, gain_term, hidden, grad_proj, attended_output)

def group_major(stacked):
    micro_count, seqs, length, cols = stacked.shape
    return jnp.transpose(stacked, (1, 0, 2, 3)).reshape(seqs, micro_count * length, cols)

def device_sum(hidden_all, proj_all, grad_all, att_all):
    width = hidden_all.shape[2]
    cols = proj_all.shape[2] + att_all.shape[2]

    def add_one(total, pieces):
        hid, prj, grd, att = pieces
        term = jnp.concatenate([lax.dot_general(hid, prj, (((0,), (0,)), ((), ())), preferred_element_type=jnp.float32), lax.dot_general(grd, att, (((0,), (0,)), ((), ())), preferred_element_type=jnp.float32)], axis=1)
        rounded = lax.optimization_barrier(term.astype(jnp.bfloat16))
        return (total + rounded.astype(jnp.float32), None)
    total, unused = lax.scan(add_one, jnp.zeros((width, cols), jnp.float32), (hidden_all, proj_all, grad_all, att_all))
    return total

def reference(inputs, upstream, weights, gain):
    grads = [upstream[micro].reshape(N_FSDP, TMB, D) for micro in range(MB)]
    weight_list = [None] * SECTIONS
    gain_list = [None] * SECTIONS
    for section in reversed(range(SECTIONS)):
        new_grads, gain_sum, hid_l, prj_l, grd_l, att_l = ([], jnp.zeros((D,), jnp.float32), [], [], [], [])
        for micro in range(MB):
            grad_out, gain_term, hidden, grad_proj, attended_output = section_pass(inputs[section, micro].reshape(N_FSDP, TMB, D), weights[section], gain[section], grads[micro])
            new_grads.append(grad_out)
            gain_sum = gain_sum + gain_term
            hid_l.append(hidden)
            prj_l.append(grad_proj)
            grd_l.append(grads[micro])
            att_l.append(attended_output)
        weight_list[section] = device_sum(group_major(jnp.stack(hid_l)), group_major(jnp.stack(prj_l)), group_major(jnp.stack(grd_l)), group_major(jnp.stack(att_l)))
        gain_list[section] = gain_sum
        grads = new_grads
    return (jnp.stack(weight_list), jnp.stack(gain_list))
```

```python
import jax
import jax.numpy as jnp
from jax import lax
from jax.sharding import PartitionSpec as P


def passed_along(value, axis, steps):
    count = lax.axis_size(axis)
    leading, last = (max(0, -steps), min(count, count - steps))
    return lax.ppermute(value, axis, [(source, source + steps) for source in range(leading, last)])


def rope_tables(length, head):
    half_head = head // 2
    position = lax.iota(jnp.float32, length)
    freq = jnp.power(500000.0, -2.0 * lax.iota(jnp.float32, half_head) / head)
    angle = position[:, None] * freq[None, :]
    return (jnp.cos(angle), jnp.sin(angle))


def rotate(value_rows, cosine, sine_table):
    half_head = value_rows.shape[-1] // 2
    first = value_rows[..., :half_head]
    second = value_rows[..., half_head:]
    return jnp.concatenate(
        [first * cosine - second * sine_table, second * cosine + first * sine_table], axis=-1
    )


def unrotate(value_rows, cosine, sine_table):
    half_head = value_rows.shape[-1] // 2
    first = value_rows[..., :half_head]
    second = value_rows[..., half_head:]
    return jnp.concatenate(
        [first * cosine + second * sine_table, second * cosine - first * sine_table], axis=-1
    )


def contract_rows(left, right):
    return lax.dot_general(
        left, right, (((0,), (0,)), ((), ())), preferred_element_type=jnp.float32
    )


def contract_cols(left, right):
    return lax.dot_general(
        left, right, (((1,), (1,)), ((), ())), preferred_element_type=jnp.float32
    )


def on_device(inputs, upstream, weights, gain):
    sections = lax.axis_size("section")
    here = lax.axis_index("section")
    micro_count = inputs.shape[1]
    length = inputs.shape[2]
    width = inputs.shape[3]
    head = weights.shape[2] // 4
    rows_here = weights.shape[1]
    groups = lax.axis_size("fsdp")

    gain_rows = jnp.zeros((16, weights.shape[2]), jnp.bfloat16)
    gain_rows = lax.dynamic_update_slice(gain_rows, gain[0][None, :], (0, 0))
    packed = jnp.concatenate([weights[0], gain_rows], axis=0)
    gathered = lax.all_gather(packed, "fsdp", axis=0, tiled=True).reshape(
        groups, rows_here + 16, weights.shape[2]
    )
    w_full = gathered[:, :rows_here, :].reshape(groups * rows_here, weights.shape[2])
    gain_full = gathered[:, rows_here, :rows_here].reshape(groups * rows_here)
    wide_gain = gain_full.astype(jnp.float32)
    w_proj = w_full[:, : 3 * head]
    w_back = w_full[:, 3 * head :]

    xfloat = inputs[0].astype(jnp.float32)
    inv_rms = lax.rsqrt(jnp.mean(xfloat * xfloat, axis=-1, keepdims=True) + 1e-05)
    normed = xfloat * inv_rms
    hidden = (normed * wide_gain).astype(jnp.bfloat16)
    proj = jnp.dot(
        hidden.reshape(micro_count * length, width), w_proj, preferred_element_type=jnp.float32
    ).reshape(micro_count, length, 3 * head)
    cosine, sine_table = rope_tables(length, head)
    query_rows = rotate(proj[..., :head], cosine, sine_table).astype(jnp.bfloat16)
    key_rows = rotate(proj[..., head : 2 * head], cosine, sine_table).astype(jnp.bfloat16)
    value_rows = proj[..., 2 * head :].astype(jnp.bfloat16)
    score_scale = head ** (-0.5)
    causal = lax.broadcasted_iota(jnp.int32, (length, length), 0) >= lax.broadcasted_iota(
        jnp.int32, (length, length), 1
    )
    scores = jnp.einsum(
        "mqh,mkh->mqk", query_rows, key_rows, preferred_element_type=jnp.float32
    ) * score_scale
    probs = jax.nn.softmax(jnp.where(causal[None], scores, -1e30), axis=-1)
    probs_b = probs.astype(jnp.bfloat16)
    attended = jnp.einsum(
        "mqk,mkh->mqh", probs_b, value_rows, preferred_element_type=jnp.float32
    ).astype(jnp.bfloat16)

    def tick(tick_no, received, state):
        grad_store, proj_store, gain_acc = state
        micro = tick_no - (sections - 1 - here)
        active = jnp.logical_and(micro >= 0, micro < micro_count)
        clipped = jnp.clip(micro, 0, micro_count - 1)
        slot = jnp.clip(micro, -1, micro_count) + 1
        top_grad = lax.dynamic_index_in_dim(upstream, clipped, 0, keepdims=False)
        grad_in = jnp.where(here == sections - 1, top_grad, received)
        query_m = lax.dynamic_index_in_dim(query_rows, clipped, 0, keepdims=False)
        keys_m = lax.dynamic_index_in_dim(key_rows, clipped, 0, keepdims=False)
        values_m = lax.dynamic_index_in_dim(value_rows, clipped, 0, keepdims=False)
        probs_m = lax.dynamic_index_in_dim(probs, clipped, 0, keepdims=False)
        probs_bm = lax.dynamic_index_in_dim(probs_b, clipped, 0, keepdims=False)
        normed_m = lax.dynamic_index_in_dim(normed, clipped, 0, keepdims=False)
        inv_m = lax.dynamic_index_in_dim(inv_rms, clipped, 0, keepdims=False)
        attention_gradient = jnp.dot(
            grad_in, w_back, preferred_element_type=jnp.float32
        ).astype(jnp.bfloat16)
        probability_gradient = contract_cols(attention_gradient, values_m)
        score_gradient = (
            probs_m
            * (probability_gradient - jnp.sum(probability_gradient * probs_m, axis=-1, keepdims=True))
            * score_scale
        ).astype(jnp.bfloat16)
        query_gradient = jnp.dot(score_gradient, keys_m, preferred_element_type=jnp.float32)
        key_gradient = contract_rows(score_gradient, query_m)
        value_gradient = contract_rows(probs_bm, attention_gradient)
        grad_proj = jnp.concatenate(
            [
                unrotate(query_gradient, cosine, sine_table),
                unrotate(key_gradient, cosine, sine_table),
                value_gradient,
            ],
            axis=-1,
        ).astype(jnp.bfloat16)
        grad_hidden = contract_cols(grad_proj, w_proj)
        gain_term = jnp.sum(grad_hidden * normed_m, axis=0)
        grad_normed = grad_hidden * wide_gain
        grad_x = inv_m * (
            grad_normed - normed_m * jnp.mean(grad_normed * normed_m, axis=-1, keepdims=True)
        )
        grad_out = (grad_in.astype(jnp.float32) + grad_x).astype(jnp.bfloat16)
        grad_store = lax.dynamic_update_index_in_dim(grad_store, grad_in, slot, 0)
        proj_store = lax.dynamic_update_index_in_dim(proj_store, grad_proj, slot, 0)
        gain_acc = gain_acc + jnp.where(active, gain_term, 0.0)
        return grad_out, (grad_store, proj_store, gain_acc)

    def step_loop(tick_no, carry):
        received, state = carry
        sent, state = tick(tick_no, received, state)
        received = passed_along(sent, "section", -1)
        return (received, state)

    state_start = (
        jnp.zeros((micro_count + 2, length, width), jnp.bfloat16),
        jnp.zeros((micro_count + 2, length, 3 * head), jnp.bfloat16),
        jnp.zeros((width,), jnp.float32),
    )
    total_ticks = sections + micro_count - 1
    received, state = lax.fori_loop(
        0, total_ticks - 1, step_loop, (jnp.zeros((length, width), jnp.bfloat16), state_start)
    )
    leftover, state = tick(total_ticks - 1, received, state)
    grad_store, proj_store, gain_acc = state
    tokens_all = micro_count * length
    grad_flat = grad_store[1 : micro_count + 1].reshape(tokens_all, width)
    proj_flat = proj_store[1 : micro_count + 1].reshape(tokens_all, 3 * head)
    att_flat = attended.reshape(tokens_all, head)
    shard = lax.psum_scatter(
        jnp.concatenate(
            [
                contract_rows(hidden.reshape(tokens_all, width), proj_flat),
                contract_rows(grad_flat, att_flat),
            ],
            axis=1,
        ).astype(jnp.bfloat16),
        "fsdp",
        scatter_dimension=0,
        tiled=True,
    ).astype(jnp.float32)
    gain_sum = jnp.sum(lax.all_gather(gain_acc, "fsdp", axis=0), axis=0)
    return (shard[None], gain_sum[None])


def solution(mesh):
    return jax.shard_map(
        on_device,
        mesh=mesh,
        in_specs=(
            P("section", None, "fsdp", None),
            P(None, "fsdp", None),
            P("section", "fsdp", None),
            P("section", "fsdp"),
        ),
        out_specs=(P("section", "fsdp", None), P("section", None)),
        check_vma=False,
    )
```

```python
import jax
import jax.numpy as jnp
from jax import lax
from jax.sharding import Mesh, PartitionSpec as P

SECTION = ("sh", "sy")
FSDP = ("fx", "fz", "fc")
SH, SY, FX, FZ, FC = 2, 8, 2, 8, 2


def passed_along(value, axis, steps):
    count = SH * SY
    leading, last = (max(0, -steps), min(count, count - steps))
    return lax.ppermute(value, axis, [(source, source + steps) for source in range(leading, last)])


def rope_tables(length, head):
    half_head = head // 2
    position = lax.iota(jnp.float32, length)
    freq = jnp.power(500000.0, -2.0 * lax.iota(jnp.float32, half_head) / head)
    angle = position[:, None] * freq[None, :]
    return (jnp.cos(angle), jnp.sin(angle))


def rotate(value_rows, cosine, sine_table):
    half_head = value_rows.shape[-1] // 2
    first = value_rows[..., :half_head]
    second = value_rows[..., half_head:]
    return jnp.concatenate(
        [first * cosine - second * sine_table, second * cosine + first * sine_table], axis=-1
    )


def unrotate(value_rows, cosine, sine_table):
    half_head = value_rows.shape[-1] // 2
    first = value_rows[..., :half_head]
    second = value_rows[..., half_head:]
    return jnp.concatenate(
        [first * cosine + second * sine_table, second * cosine - first * sine_table], axis=-1
    )


def contract_rows(left, right):
    return lax.dot_general(
        left, right, (((0,), (0,)), ((), ())), preferred_element_type=jnp.float32
    )


def contract_cols(left, right):
    return lax.dot_general(
        left, right, (((1,), (1,)), ((), ())), preferred_element_type=jnp.float32
    )


def on_device(inputs, upstream, weights, gain):
    sections = SH * SY
    here = lax.axis_index("sh") * SY + lax.axis_index("sy")
    micro_count = inputs.shape[1]
    length = inputs.shape[2]
    width = inputs.shape[3]
    head = weights.shape[2] // 4
    rows_here = weights.shape[1]
    groups = FX * FZ * FC

    gain_rows = jnp.zeros((16, weights.shape[2]), jnp.bfloat16)
    gain_rows = lax.dynamic_update_slice(gain_rows, gain[0][None, :], (0, 0))
    packed = jnp.concatenate([weights[0], gain_rows], axis=0)
    staged = lax.all_gather(packed, "fx", axis=0, tiled=True)
    staged = lax.all_gather(staged, "fz", axis=0, tiled=True)
    staged = lax.all_gather(staged, "fc", axis=0, tiled=True)
    gathered = (
        staged.reshape(FC, FZ, FX, rows_here + 16, weights.shape[2])
        .transpose(2, 1, 0, 3, 4)
        .reshape(groups, rows_here + 16, weights.shape[2])
    )
    w_full = gathered[:, :rows_here, :].reshape(groups * rows_here, weights.shape[2])
    gain_full = gathered[:, rows_here, :rows_here].reshape(groups * rows_here)
    wide_gain = gain_full.astype(jnp.float32)
    w_proj = w_full[:, : 3 * head]
    w_back = w_full[:, 3 * head :]

    xfloat = inputs[0].astype(jnp.float32)
    inv_rms = lax.rsqrt(jnp.mean(xfloat * xfloat, axis=-1, keepdims=True) + 1e-05)
    normed = xfloat * inv_rms
    hidden = (normed * wide_gain).astype(jnp.bfloat16)
    proj = jnp.dot(
        hidden.reshape(micro_count * length, width), w_proj, preferred_element_type=jnp.float32
    ).reshape(micro_count, length, 3 * head)
    cosine, sine_table = rope_tables(length, head)
    query_rows = rotate(proj[..., :head], cosine, sine_table).astype(jnp.bfloat16)
    key_rows = rotate(proj[..., head : 2 * head], cosine, sine_table).astype(jnp.bfloat16)
    value_rows = proj[..., 2 * head :].astype(jnp.bfloat16)
    score_scale = head ** (-0.5)
    causal = lax.broadcasted_iota(jnp.int32, (length, length), 0) >= lax.broadcasted_iota(
        jnp.int32, (length, length), 1
    )
    scores = jnp.einsum(
        "mqh,mkh->mqk", query_rows, key_rows, preferred_element_type=jnp.float32
    ) * score_scale
    probs = jax.nn.softmax(jnp.where(causal[None], scores, -1e30), axis=-1)
    probs_b = probs.astype(jnp.bfloat16)
    attended = jnp.einsum(
        "mqk,mkh->mqh", probs_b, value_rows, preferred_element_type=jnp.float32
    ).astype(jnp.bfloat16)

    def tick(tick_no, received, state):
        grad_store, proj_store, gain_acc = state
        micro = tick_no - (sections - 1 - here)
        active = jnp.logical_and(micro >= 0, micro < micro_count)
        clipped = jnp.clip(micro, 0, micro_count - 1)
        slot = jnp.clip(micro, -1, micro_count) + 1
        top_grad = lax.dynamic_index_in_dim(upstream, clipped, 0, keepdims=False)
        grad_in = jnp.where(here == sections - 1, top_grad, received)
        query_m = lax.dynamic_index_in_dim(query_rows, clipped, 0, keepdims=False)
        keys_m = lax.dynamic_index_in_dim(key_rows, clipped, 0, keepdims=False)
        values_m = lax.dynamic_index_in_dim(value_rows, clipped, 0, keepdims=False)
        probs_m = lax.dynamic_index_in_dim(probs, clipped, 0, keepdims=False)
        probs_bm = lax.dynamic_index_in_dim(probs_b, clipped, 0, keepdims=False)
        normed_m = lax.dynamic_index_in_dim(normed, clipped, 0, keepdims=False)
        inv_m = lax.dynamic_index_in_dim(inv_rms, clipped, 0, keepdims=False)
        attention_gradient = jnp.dot(
            grad_in, w_back, preferred_element_type=jnp.float32
        ).astype(jnp.bfloat16)
        probability_gradient = contract_cols(attention_gradient, values_m)
        score_gradient = (
            probs_m
            * (probability_gradient - jnp.sum(probability_gradient * probs_m, axis=-1, keepdims=True))
            * score_scale
        ).astype(jnp.bfloat16)
        query_gradient = jnp.dot(score_gradient, keys_m, preferred_element_type=jnp.float32)
        key_gradient = contract_rows(score_gradient, query_m)
        value_gradient = contract_rows(probs_bm, attention_gradient)
        grad_proj = jnp.concatenate(
            [
                unrotate(query_gradient, cosine, sine_table),
                unrotate(key_gradient, cosine, sine_table),
                value_gradient,
            ],
            axis=-1,
        ).astype(jnp.bfloat16)
        grad_hidden = contract_cols(grad_proj, w_proj)
        gain_term = jnp.sum(grad_hidden * normed_m, axis=0)
        grad_normed = grad_hidden * wide_gain
        grad_x = inv_m * (
            grad_normed - normed_m * jnp.mean(grad_normed * normed_m, axis=-1, keepdims=True)
        )
        grad_out = (grad_in.astype(jnp.float32) + grad_x).astype(jnp.bfloat16)
        grad_store = lax.dynamic_update_index_in_dim(grad_store, grad_in, slot, 0)
        proj_store = lax.dynamic_update_index_in_dim(proj_store, grad_proj, slot, 0)
        gain_acc = gain_acc + jnp.where(active, gain_term, 0.0)
        return grad_out, (grad_store, proj_store, gain_acc)

    def step_loop(tick_no, carry):
        received, state = carry
        sent, state = tick(tick_no, received, state)
        received = passed_along(sent, SECTION, -1)
        return (received, state)

    state_start = (
        jnp.zeros((micro_count + 2, length, width), jnp.bfloat16),
        jnp.zeros((micro_count + 2, length, 3 * head), jnp.bfloat16),
        jnp.zeros((width,), jnp.float32),
    )
    total_ticks = sections + micro_count - 1
    received, state = lax.fori_loop(
        0, total_ticks - 1, step_loop, (jnp.zeros((length, width), jnp.bfloat16), state_start)
    )
    leftover, state = tick(total_ticks - 1, received, state)
    grad_store, proj_store, gain_acc = state
    tokens_all = micro_count * length
    grad_flat = grad_store[1 : micro_count + 1].reshape(tokens_all, width)
    proj_flat = proj_store[1 : micro_count + 1].reshape(tokens_all, 3 * head)
    att_flat = attended.reshape(tokens_all, head)
    def stage_order(rows):
        return (
            rows.reshape(tokens_all, FX, FZ, FC, rows_here)
            .transpose(0, 3, 2, 1, 4)
            .reshape(tokens_all, width)
        )

    terms = jnp.concatenate(
        [
            contract_rows(stage_order(hidden.reshape(tokens_all, width)), proj_flat),
            contract_rows(stage_order(grad_flat), att_flat),
        ],
        axis=1,
    ).astype(jnp.bfloat16)
    cols = terms.shape[1]
    terms = lax.psum_scatter(terms.reshape(FC, -1, cols), "fc", scatter_dimension=0, tiled=True)
    terms = lax.psum_scatter(terms.reshape(FZ, -1, cols), "fz", scatter_dimension=0, tiled=True)
    terms = lax.psum_scatter(terms.reshape(FX, -1, cols), "fx", scatter_dimension=0, tiled=True)
    shard = terms.reshape(rows_here, cols).astype(jnp.float32)
    gain_sum = jnp.sum(lax.all_gather(gain_acc, FSDP, axis=0), axis=0)
    return (shard[None], gain_sum[None])


def solution(mesh):
    global SH, SY, FX, FZ, FC
    sections = mesh.shape["section"]
    groups = mesh.shape["fsdp"]
    SH, SY = 2, sections // 2
    FX, FZ, FC = 2, groups // 4, 2
    sub_mesh = Mesh(
        mesh.devices.reshape(SH, SY, FX, FZ, FC), ("sh", "sy", "fx", "fz", "fc")
    )
    return jax.shard_map(
        on_device,
        mesh=sub_mesh,
        in_specs=(
            P(SECTION, None, FSDP, None),
            P(None, FSDP, None),
            P(SECTION, FSDP, None),
            P(SECTION, FSDP),
        ),
        out_specs=(P(SECTION, FSDP, None), P(SECTION, None)),
        check_vma=False,
    )
```

```python
import jax
import jax.numpy as jnp
from jax import lax
from jax.experimental import pallas as pl
from jax.experimental.pallas import tpu as pltpu
from jax.sharding import Mesh, PartitionSpec as P

SECTION = ("sh", "sy")
FSDP = ("fx", "fz", "fc")
SH, SY, FX, FZ, FC = 2, 8, 2, 8, 2


def passed_along(value, axis, steps):
    count = SH * SY
    leading, last = (max(0, -steps), min(count, count - steps))
    return lax.ppermute(value, axis, [(source, source + steps) for source in range(leading, last)])


def rope_tables(length, head):
    half_head = head // 2
    position = lax.iota(jnp.float32, length)
    freq = jnp.power(500000.0, -2.0 * lax.iota(jnp.float32, half_head) / head)
    angle = position[:, None] * freq[None, :]
    return (jnp.cos(angle), jnp.sin(angle))


def rotate(value_rows, cosine, sine_table):
    half_head = value_rows.shape[-1] // 2
    first = value_rows[..., :half_head]
    second = value_rows[..., half_head:]
    return jnp.concatenate(
        [first * cosine - second * sine_table, second * cosine + first * sine_table], axis=-1
    )


def unrotate(value_rows, cosine, sine_table):
    half_head = value_rows.shape[-1] // 2
    first = value_rows[..., :half_head]
    second = value_rows[..., half_head:]
    return jnp.concatenate(
        [first * cosine + second * sine_table, second * cosine - first * sine_table], axis=-1
    )


def contract_rows(left, right):
    return lax.dot_general(
        left, right, (((0,), (0,)), ((), ())), preferred_element_type=jnp.float32
    )


def contract_cols(left, right):
    return lax.dot_general(
        left, right, (((1,), (1,)), ((), ())), preferred_element_type=jnp.float32
    )


def tick_kernel(
    scal, recv_ref, up_ref, wb_ref, wp_ref, gain_ref, normed_ref, inv_ref, probs_ref, probs_b_ref,
    q_ref, k_ref, v_ref, cos_ref, sin_ref, gstore_in, pstore_in, gacc_ref,
    out_ref, gstore_ref, pstore_ref, gacc_out,
):
    head = q_ref.shape[-1]
    score_scale = head ** (-0.5)
    grad_in = jnp.where(scal[3] == 1, up_ref[...], recv_ref[...])
    ga = jnp.dot(grad_in, wb_ref[...], preferred_element_type=jnp.float32).astype(jnp.bfloat16)
    probs = probs_ref[...]
    gprob = lax.dot_general(
        ga, v_ref[...], (((1,), (1,)), ((), ())), preferred_element_type=jnp.float32
    )
    gs = (probs * (gprob - jnp.sum(gprob * probs, axis=-1, keepdims=True)) * score_scale).astype(
        jnp.bfloat16
    )
    gq = jnp.dot(gs, k_ref[...], preferred_element_type=jnp.float32)
    gk = lax.dot_general(gs, q_ref[...], (((0,), (0,)), ((), ())), preferred_element_type=jnp.float32)
    gv = lax.dot_general(
        probs_b_ref[...], ga, (((0,), (0,)), ((), ())), preferred_element_type=jnp.float32
    )
    cosine = cos_ref[...]
    sine = sin_ref[...]
    gq = gq * cosine + pltpu.roll(gq, head // 2, 1) * sine
    gk = gk * cosine + pltpu.roll(gk, head // 2, 1) * sine
    gp = jnp.concatenate([gq, gk, gv], axis=-1).astype(jnp.bfloat16)
    gh = lax.dot_general(gp, wp_ref[...], (((1,), (1,)), ((), ())), preferred_element_type=jnp.float32)
    normed = normed_ref[...]
    gain_term = jnp.sum(gh * normed, axis=0, keepdims=True)
    gn = gh * gain_ref[...]
    mean = jnp.sum(gn * normed, axis=-1, keepdims=True) * (1.0 / gn.shape[-1])
    gx = inv_ref[...] * (gn - normed * mean)
    out_ref[...] = (grad_in.astype(jnp.float32) + gx).astype(out_ref.dtype)
    gstore_ref[...] = grad_in
    pstore_ref[...] = gp
    gacc_out[...] = gacc_ref[...] + jnp.where(scal[2] == 1, gain_term, 0.0)


def tick_call(scal, recv, upstream, w_back, w_proj, gain_row, normed, inv_rms, probs, probs_b,
              query_rows, key_rows, value_rows, cos2, sin2, grad_store, proj_store, gain_acc):
    micro_count, length, width = normed.shape
    head = query_rows.shape[-1]
    full = lambda shape: pl.BlockSpec(shape, lambda i, s: (0,) * len(shape))
    per_micro = lambda shape: pl.BlockSpec((None,) + shape, lambda i, s: (s[0],) + (0,) * len(shape))
    per_slot = lambda shape: pl.BlockSpec((None,) + shape, lambda i, s: (s[1],) + (0,) * len(shape))
    flops = 2 * length * width * 4 * head * 2
    return pl.pallas_call(
        tick_kernel,
        out_shape=(
            jax.ShapeDtypeStruct((length, width), jnp.bfloat16),
            jax.ShapeDtypeStruct(grad_store.shape, grad_store.dtype),
            jax.ShapeDtypeStruct(proj_store.shape, proj_store.dtype),
            jax.ShapeDtypeStruct(gain_acc.shape, gain_acc.dtype),
        ),
        grid_spec=pltpu.PrefetchScalarGridSpec(
            num_scalar_prefetch=1,
            grid=(1,),
            in_specs=[
                full((length, width)),
                per_micro((length, width)),
                full((width, head)),
                full((width, 3 * head)),
                full((1, width)),
                per_micro((length, width)),
                per_micro((length, 1)),
                per_micro((length, length)),
                per_micro((length, length)),
                per_micro((length, head)),
                per_micro((length, head)),
                per_micro((length, head)),
                full((length, head)),
                full((length, head)),
                pl.BlockSpec(memory_space=pl.ANY),
                pl.BlockSpec(memory_space=pl.ANY),
                full((1, width)),
            ],
            out_specs=[
                full((length, width)),
                per_slot((length, width)),
                per_slot((length, 3 * head)),
                full((1, width)),
            ],
        ),
        input_output_aliases={15: 1, 16: 2, 17: 3},
        cost_estimate=pl.CostEstimate(
            flops=flops, transcendentals=0, bytes_accessed=2 * width * 4 * head + 8 * length * width
        ),
        compiler_params=pltpu.CompilerParams(vmem_limit_bytes=48 * 1024 * 1024),
    )(scal, recv, upstream, w_back, w_proj, gain_row, normed, inv_rms, probs, probs_b,
      query_rows, key_rows, value_rows, cos2, sin2, grad_store, proj_store, gain_acc)


def on_device(inputs, upstream, weights, gain):
    sections = SH * SY
    here = lax.axis_index("sh") * SY + lax.axis_index("sy")
    micro_count = inputs.shape[1]
    length = inputs.shape[2]
    width = inputs.shape[3]
    head = weights.shape[2] // 4
    rows_here = weights.shape[1]
    groups = FX * FZ * FC

    gain_rows = jnp.zeros((16, weights.shape[2]), jnp.bfloat16)
    gain_rows = lax.dynamic_update_slice(gain_rows, gain[0][None, :], (0, 0))
    packed = jnp.concatenate([weights[0], gain_rows], axis=0)
    staged = lax.all_gather(packed, "fx", axis=0, tiled=True)
    staged = lax.all_gather(staged, "fz", axis=0, tiled=True)
    staged = lax.all_gather(staged, "fc", axis=0, tiled=True)
    gathered = (
        staged.reshape(FC, FZ, FX, rows_here + 16, weights.shape[2])
        .transpose(2, 1, 0, 3, 4)
        .reshape(groups, rows_here + 16, weights.shape[2])
    )
    w_full = gathered[:, :rows_here, :].reshape(groups * rows_here, weights.shape[2])
    gain_full = gathered[:, rows_here, :rows_here].reshape(groups * rows_here)
    wide_gain = gain_full.astype(jnp.float32)
    w_proj = w_full[:, : 3 * head]
    w_back = w_full[:, 3 * head :]

    xfloat = inputs[0].astype(jnp.float32)
    inv_rms = lax.rsqrt(jnp.mean(xfloat * xfloat, axis=-1, keepdims=True) + 1e-05)
    normed = xfloat * inv_rms
    hidden = (normed * wide_gain).astype(jnp.bfloat16)
    proj = jnp.dot(
        hidden.reshape(micro_count * length, width), w_proj, preferred_element_type=jnp.float32
    ).reshape(micro_count, length, 3 * head)
    cosine, sine_table = rope_tables(length, head)
    query_rows = rotate(proj[..., :head], cosine, sine_table).astype(jnp.bfloat16)
    key_rows = rotate(proj[..., head : 2 * head], cosine, sine_table).astype(jnp.bfloat16)
    value_rows = proj[..., 2 * head :].astype(jnp.bfloat16)
    score_scale = head ** (-0.5)
    causal = lax.broadcasted_iota(jnp.int32, (length, length), 0) >= lax.broadcasted_iota(
        jnp.int32, (length, length), 1
    )
    scores = jnp.einsum(
        "mqh,mkh->mqk", query_rows, key_rows, preferred_element_type=jnp.float32
    ) * score_scale
    probs = jax.nn.softmax(jnp.where(causal[None], scores, -1e30), axis=-1)
    probs_b = probs.astype(jnp.bfloat16)
    attended = jnp.einsum(
        "mqk,mkh->mqh", probs_b, value_rows, preferred_element_type=jnp.float32
    ).astype(jnp.bfloat16)

    cos2 = jnp.concatenate([cosine, cosine], axis=-1)
    sin2 = jnp.concatenate([sine_table, -sine_table], axis=-1)
    gain_row = wide_gain.reshape(1, width)

    def tick(tick_no, received, state):
        grad_store, proj_store, gain_acc = state
        micro = tick_no - (sections - 1 - here)
        active = jnp.logical_and(micro >= 0, micro < micro_count)
        clipped = jnp.clip(micro, 0, micro_count - 1)
        slot = jnp.clip(micro, -1, micro_count) + 1
        scal = jnp.stack(
            [clipped, slot, active.astype(jnp.int32), (here == sections - 1).astype(jnp.int32)]
        ).astype(jnp.int32)
        grad_out, grad_store, proj_store, gain_acc = tick_call(
            scal, received, upstream, w_back, w_proj, gain_row, normed, inv_rms, probs, probs_b,
            query_rows, key_rows, value_rows, cos2, sin2, grad_store, proj_store, gain_acc.reshape(1, width),
        )
        return grad_out, (grad_store, proj_store, gain_acc.reshape(width))

    def step_loop(tick_no, carry):
        received, state = carry
        sent, state = tick(tick_no, received, state)
        received = passed_along(sent, SECTION, -1)
        return (received, state)

    state_start = (
        jnp.zeros((micro_count + 2, length, width), jnp.bfloat16),
        jnp.zeros((micro_count + 2, length, 3 * head), jnp.bfloat16),
        jnp.zeros((width,), jnp.float32),
    )
    total_ticks = sections + micro_count - 1
    received, state = lax.fori_loop(
        0, total_ticks - 1, step_loop, (jnp.zeros((length, width), jnp.bfloat16), state_start)
    )
    leftover, state = tick(total_ticks - 1, received, state)
    grad_store, proj_store, gain_acc = state
    tokens_all = micro_count * length
    grad_flat = grad_store[1 : micro_count + 1].reshape(tokens_all, width)
    proj_flat = proj_store[1 : micro_count + 1].reshape(tokens_all, 3 * head)
    att_flat = attended.reshape(tokens_all, head)
    def stage_order(rows):
        return (
            rows.reshape(tokens_all, FX, FZ, FC, rows_here)
            .transpose(0, 3, 2, 1, 4)
            .reshape(tokens_all, width)
        )

    terms = jnp.concatenate(
        [
            contract_rows(stage_order(hidden.reshape(tokens_all, width)), proj_flat),
            contract_rows(stage_order(grad_flat), att_flat),
        ],
        axis=1,
    ).astype(jnp.bfloat16)
    cols = terms.shape[1]
    terms = lax.psum_scatter(terms.reshape(FC, -1, cols), "fc", scatter_dimension=0, tiled=True)
    terms = lax.psum_scatter(terms.reshape(FZ, -1, cols), "fz", scatter_dimension=0, tiled=True)
    terms = lax.psum_scatter(terms.reshape(FX, -1, cols), "fx", scatter_dimension=0, tiled=True)
    shard = terms.reshape(rows_here, cols).astype(jnp.float32)
    gain_sum = jnp.sum(lax.all_gather(gain_acc, FSDP, axis=0), axis=0)
    return (shard[None], gain_sum[None])


def solution(mesh):
    global SH, SY, FX, FZ, FC
    sections = mesh.shape["section"]
    groups = mesh.shape["fsdp"]
    SH, SY = 2, sections // 2
    FX, FZ, FC = 2, groups // 4, 2
    sub_mesh = Mesh(
        mesh.devices.reshape(SH, SY, FX, FZ, FC), ("sh", "sy", "fx", "fz", "fc")
    )
    return jax.shard_map(
        on_device,
        mesh=sub_mesh,
        in_specs=(
            P(SECTION, None, FSDP, None),
            P(None, FSDP, None),
            P(SECTION, FSDP, None),
            P(SECTION, FSDP),
        ),
        out_specs=(P(SECTION, FSDP, None), P(SECTION, None)),
        check_vma=False,
    )
```

```python
import jax
import jax.numpy as jnp
from jax import lax
from jax.experimental import pallas as pl
from jax.experimental.pallas import tpu as pltpu
from jax.sharding import Mesh, PartitionSpec as P

SECTION = ("sh", "sy")
FSDP = ("fx", "fz", "fc")
SH, SY, FX, FZ, FC = 2, 8, 2, 8, 2


def passed_along(value, axis, steps):
    count = SH * SY
    leading, last = (max(0, -steps), min(count, count - steps))
    return lax.ppermute(value, axis, [(source, source + steps) for source in range(leading, last)])


def rope_tables(length, head):
    half_head = head // 2
    position = lax.iota(jnp.float32, length)
    freq = jnp.power(500000.0, -2.0 * lax.iota(jnp.float32, half_head) / head)
    angle = position[:, None] * freq[None, :]
    return (jnp.cos(angle), jnp.sin(angle))


def rotate(value_rows, cosine, sine_table):
    half_head = value_rows.shape[-1] // 2
    first = value_rows[..., :half_head]
    second = value_rows[..., half_head:]
    return jnp.concatenate(
        [first * cosine - second * sine_table, second * cosine + first * sine_table], axis=-1
    )


def unrotate(value_rows, cosine, sine_table):
    half_head = value_rows.shape[-1] // 2
    first = value_rows[..., :half_head]
    second = value_rows[..., half_head:]
    return jnp.concatenate(
        [first * cosine + second * sine_table, second * cosine - first * sine_table], axis=-1
    )


def contract_rows(left, right):
    return lax.dot_general(
        left, right, (((0,), (0,)), ((), ())), preferred_element_type=jnp.float32
    )


def contract_cols(left, right):
    return lax.dot_general(
        left, right, (((1,), (1,)), ((), ())), preferred_element_type=jnp.float32
    )


def tick_kernel(
    scal, recv_ref, up_ref, wb_ref, wp_ref, gain_ref, normed_ref, inv_ref, probs_ref, probs_b_ref,
    q_ref, k_ref, v_ref, cos_ref, sin_ref, gstore_in, pstore_in, gacc_ref,
    out_ref, gstore_ref, pstore_ref, gacc_out,
):
    head = q_ref.shape[-1]
    score_scale = head ** (-0.5)
    grad_in = jnp.where(scal[3] == 1, up_ref[...], recv_ref[...])
    ga = jnp.dot(grad_in, wb_ref[...], preferred_element_type=jnp.float32).astype(jnp.bfloat16)
    probs = probs_ref[...]
    gprob = lax.dot_general(
        ga, v_ref[...], (((1,), (1,)), ((), ())), preferred_element_type=jnp.float32
    )
    gs = (probs * (gprob - jnp.sum(gprob * probs, axis=-1, keepdims=True)) * score_scale).astype(
        jnp.bfloat16
    )
    gq = jnp.dot(gs, k_ref[...], preferred_element_type=jnp.float32)
    gk = lax.dot_general(gs, q_ref[...], (((0,), (0,)), ((), ())), preferred_element_type=jnp.float32)
    gv = lax.dot_general(
        probs_b_ref[...], ga, (((0,), (0,)), ((), ())), preferred_element_type=jnp.float32
    )
    cosine = cos_ref[...]
    sine = sin_ref[...]
    gq = gq * cosine + pltpu.roll(gq, head // 2, 1) * sine
    gk = gk * cosine + pltpu.roll(gk, head // 2, 1) * sine
    gp = jnp.concatenate([gq, gk, gv], axis=-1).astype(jnp.bfloat16)
    gh = lax.dot_general(gp, wp_ref[...], (((1,), (1,)), ((), ())), preferred_element_type=jnp.float32)
    normed = normed_ref[...]
    gain_term = jnp.sum(gh * normed, axis=0, keepdims=True)
    gn = gh * gain_ref[...]
    mean = jnp.sum(gn * normed, axis=-1, keepdims=True) * (1.0 / gn.shape[-1])
    gx = inv_ref[...] * (gn - normed * mean)
    out_ref[...] = (grad_in.astype(jnp.float32) + gx).astype(out_ref.dtype)
    gstore_ref[...] = grad_in
    pstore_ref[...] = gp
    gacc_out[...] = gacc_ref[...] + jnp.where(scal[2] == 1, gain_term, 0.0)


def tick_call(scal, recv, upstream, w_back, w_proj, gain_row, normed, inv_rms, probs, probs_b,
              query_rows, key_rows, value_rows, cos2, sin2, grad_store, proj_store, gain_acc):
    micro_count, length, width = normed.shape
    head = query_rows.shape[-1]
    full = lambda shape: pl.BlockSpec(shape, lambda i, s: (0,) * len(shape))
    per_micro = lambda shape: pl.BlockSpec((None,) + shape, lambda i, s: (s[0],) + (0,) * len(shape))
    per_slot = lambda shape: pl.BlockSpec((None,) + shape, lambda i, s: (s[1],) + (0,) * len(shape))
    flops = 2 * length * width * 4 * head * 2
    return pl.pallas_call(
        tick_kernel,
        out_shape=(
            jax.ShapeDtypeStruct((length, width), jnp.bfloat16),
            jax.ShapeDtypeStruct(grad_store.shape, grad_store.dtype),
            jax.ShapeDtypeStruct(proj_store.shape, proj_store.dtype),
            jax.ShapeDtypeStruct(gain_acc.shape, gain_acc.dtype),
        ),
        grid_spec=pltpu.PrefetchScalarGridSpec(
            num_scalar_prefetch=1,
            grid=(1,),
            in_specs=[
                full((length, width)),
                per_micro((length, width)),
                full((width, head)),
                full((width, 3 * head)),
                full((1, width)),
                per_micro((length, width)),
                per_micro((length, 1)),
                per_micro((length, length)),
                per_micro((length, length)),
                per_micro((length, head)),
                per_micro((length, head)),
                per_micro((length, head)),
                full((length, head)),
                full((length, head)),
                pl.BlockSpec(memory_space=pl.ANY),
                pl.BlockSpec(memory_space=pl.ANY),
                full((1, width)),
            ],
            out_specs=[
                full((length, width)),
                per_slot((length, width)),
                per_slot((length, 3 * head)),
                full((1, width)),
            ],
        ),
        input_output_aliases={15: 1, 16: 2, 17: 3},
        cost_estimate=pl.CostEstimate(
            flops=flops, transcendentals=0, bytes_accessed=2 * width * 4 * head + 8 * length * width
        ),
        compiler_params=pltpu.CompilerParams(vmem_limit_bytes=48 * 1024 * 1024),
    )(scal, recv, upstream, w_back, w_proj, gain_row, normed, inv_rms, probs, probs_b,
      query_rows, key_rows, value_rows, cos2, sin2, grad_store, proj_store, gain_acc)


def on_device(inputs, upstream, weights, gain):
    sections = SH * SY
    here = lax.axis_index("sh") * SY + lax.axis_index("sy")
    micro_count = inputs.shape[1]
    length = inputs.shape[2]
    width = inputs.shape[3]
    head = weights.shape[2] // 4
    rows_here = weights.shape[1]
    groups = FX * FZ * FC

    gain_rows = jnp.zeros((16, weights.shape[2]), jnp.bfloat16)
    gain_rows = lax.dynamic_update_slice(gain_rows, gain[0][None, :], (0, 0))
    packed = jnp.concatenate([weights[0], gain_rows], axis=0)
    staged = lax.all_gather(packed, "fx", axis=0, tiled=True)
    staged = lax.all_gather(staged, "fz", axis=0, tiled=True)
    staged = lax.all_gather(staged, "fc", axis=0, tiled=True)
    gathered = (
        staged.reshape(FC, FZ, FX, rows_here + 16, weights.shape[2])
        .transpose(2, 1, 0, 3, 4)
        .reshape(groups, rows_here + 16, weights.shape[2])
    )
    w_full = gathered[:, :rows_here, :].reshape(groups * rows_here, weights.shape[2])
    gain_full = gathered[:, rows_here, :rows_here].reshape(groups * rows_here)
    wide_gain = gain_full.astype(jnp.float32)
    w_proj = w_full[:, : 3 * head]
    w_back = w_full[:, 3 * head :]

    xfloat = inputs[0].astype(jnp.float32)
    inv_rms = lax.rsqrt(jnp.mean(xfloat * xfloat, axis=-1, keepdims=True) + 1e-05)
    normed = xfloat * inv_rms
    hidden = (normed * wide_gain).astype(jnp.bfloat16)
    proj = jnp.dot(
        hidden.reshape(micro_count * length, width), w_proj, preferred_element_type=jnp.float32
    ).reshape(micro_count, length, 3 * head)
    cosine, sine_table = rope_tables(length, head)
    query_rows = rotate(proj[..., :head], cosine, sine_table).astype(jnp.bfloat16)
    key_rows = rotate(proj[..., head : 2 * head], cosine, sine_table).astype(jnp.bfloat16)
    value_rows = proj[..., 2 * head :].astype(jnp.bfloat16)
    score_scale = head ** (-0.5)
    causal = lax.broadcasted_iota(jnp.int32, (length, length), 0) >= lax.broadcasted_iota(
        jnp.int32, (length, length), 1
    )
    scores = jnp.einsum(
        "mqh,mkh->mqk", query_rows, key_rows, preferred_element_type=jnp.float32
    ) * score_scale
    probs = jax.nn.softmax(jnp.where(causal[None], scores, -1e30), axis=-1)
    probs_b = probs.astype(jnp.bfloat16)
    attended = jnp.einsum(
        "mqk,mkh->mqh", probs_b, value_rows, preferred_element_type=jnp.float32
    ).astype(jnp.bfloat16)

    cos2 = jnp.concatenate([cosine, cosine], axis=-1)
    sin2 = jnp.concatenate([sine_table, -sine_table], axis=-1)
    gain_row = wide_gain.reshape(1, width)

    def tick(tick_no, received, state):
        grad_store, proj_store, gain_acc = state
        micro = tick_no - (sections - 1 - here)
        active = jnp.logical_and(micro >= 0, micro < micro_count)
        clipped = jnp.clip(micro, 0, micro_count - 1)
        slot = jnp.clip(micro, -1, micro_count) + 1
        scal = jnp.stack(
            [clipped, slot, active.astype(jnp.int32), (here == sections - 1).astype(jnp.int32)]
        ).astype(jnp.int32)
        grad_out, grad_store, proj_store, gain_acc = tick_call(
            scal, received, upstream, w_back, w_proj, gain_row, normed, inv_rms, probs, probs_b,
            query_rows, key_rows, value_rows, cos2, sin2, grad_store, proj_store, gain_acc.reshape(1, width),
        )
        return grad_out, (grad_store, proj_store, gain_acc.reshape(width))

    def step_loop(tick_no, carry):
        received, state = carry
        sent, state = tick(tick_no, received, state)
        received = passed_along(sent, SECTION, -1)
        return (received, state)

    state_start = (
        jnp.zeros((micro_count + 2, length, width), jnp.bfloat16),
        jnp.zeros((micro_count + 2, length, 3 * head), jnp.bfloat16),
        jnp.zeros((width,), jnp.float32),
    )
    total_ticks = sections + micro_count - 1
    received, state = lax.fori_loop(
        0, total_ticks - 1, step_loop, (jnp.zeros((length, width), jnp.bfloat16), state_start)
    )
    leftover, state = tick(total_ticks - 1, received, state)
    grad_store, proj_store, gain_acc = state
    tokens_all = micro_count * length
    grad_flat = grad_store[1 : micro_count + 1].reshape(tokens_all, width)
    proj_flat = proj_store[1 : micro_count + 1].reshape(tokens_all, 3 * head)
    att_flat = attended.reshape(tokens_all, head)
    def stage_order(rows):
        return (
            rows.reshape(tokens_all, FX, FZ, FC, rows_here)
            .transpose(0, 3, 2, 1, 4)
            .reshape(tokens_all, width)
        )

    terms = jnp.concatenate(
        [
            contract_rows(stage_order(hidden.reshape(tokens_all, width)), proj_flat),
            contract_rows(stage_order(grad_flat), att_flat),
        ],
        axis=1,
    ).astype(jnp.bfloat16)
    cols = terms.shape[1]
    terms = lax.psum_scatter(terms.reshape(FC, -1, cols), "fc", scatter_dimension=0, tiled=True)
    gain_sum = jnp.sum(lax.all_gather(gain_acc, FSDP, axis=0), axis=0)
    terms, gain_sum = lax.optimization_barrier((terms, gain_sum))
    terms = lax.psum_scatter(terms.reshape(FZ, -1, cols), "fz", scatter_dimension=0, tiled=True)
    terms = lax.psum_scatter(terms.reshape(FX, -1, cols), "fx", scatter_dimension=0, tiled=True)
    shard = terms.reshape(rows_here, cols).astype(jnp.float32)
    return (shard[None], gain_sum[None])


def solution(mesh):
    global SH, SY, FX, FZ, FC
    sections = mesh.shape["section"]
    groups = mesh.shape["fsdp"]
    SH, SY = 2, sections // 2
    FX, FZ, FC = 2, groups // 4, 2
    sub_mesh = Mesh(
        mesh.devices.reshape(SH, SY, FX, FZ, FC), ("sh", "sy", "fx", "fz", "fc")
    )
    return jax.shard_map(
        on_device,
        mesh=sub_mesh,
        in_specs=(
            P(SECTION, None, FSDP, None),
            P(None, FSDP, None),
            P(SECTION, FSDP, None),
            P(SECTION, FSDP),
        ),
        out_specs=(P(SECTION, FSDP, None), P(SECTION, None)),
        check_vma=False,
    )
```

```python
import jax
import jax.numpy as jnp
from jax import lax
from jax.experimental import pallas as pl
from jax.experimental.pallas import tpu as pltpu
from jax.sharding import Mesh, PartitionSpec as P

SECTION = ("sh", "sy")
FSDP = ("fx", "fz", "fc")
SH, SY, FX, FZ, FC = 2, 8, 2, 8, 2


def passed_along(value, axis, steps):
    count = SH * SY
    leading, last = (max(0, -steps), min(count, count - steps))
    return lax.ppermute(value, axis, [(source, source + steps) for source in range(leading, last)])


def rope_tables(length, head):
    half_head = head // 2
    position = lax.iota(jnp.float32, length)
    freq = jnp.power(500000.0, -2.0 * lax.iota(jnp.float32, half_head) / head)
    angle = position[:, None] * freq[None, :]
    return (jnp.cos(angle), jnp.sin(angle))


def rotate(value_rows, cosine, sine_table):
    half_head = value_rows.shape[-1] // 2
    first = value_rows[..., :half_head]
    second = value_rows[..., half_head:]
    return jnp.concatenate(
        [first * cosine - second * sine_table, second * cosine + first * sine_table], axis=-1
    )


def unrotate(value_rows, cosine, sine_table):
    half_head = value_rows.shape[-1] // 2
    first = value_rows[..., :half_head]
    second = value_rows[..., half_head:]
    return jnp.concatenate(
        [first * cosine + second * sine_table, second * cosine - first * sine_table], axis=-1
    )


def contract_rows(left, right):
    return lax.dot_general(
        left, right, (((0,), (0,)), ((), ())), preferred_element_type=jnp.float32
    )


def contract_cols(left, right):
    return lax.dot_general(
        left, right, (((1,), (1,)), ((), ())), preferred_element_type=jnp.float32
    )


def tick_kernel(
    scal, recv_ref, up_ref, wb_ref, wp_ref, gain_ref, normed_ref, inv_ref, probs_ref, probs_b_ref,
    q_ref, k_ref, v_ref, cos_ref, sin_ref, gstore_in, pstore_in, gacc_ref,
    out_ref, gstore_ref, pstore_ref, gacc_out,
):
    head = q_ref.shape[-1]
    score_scale = head ** (-0.5)
    grad_in = jnp.where(scal[3] == 1, up_ref[...], recv_ref[...])
    ga = jnp.dot(grad_in, wb_ref[...], preferred_element_type=jnp.float32).astype(jnp.bfloat16)
    probs = probs_ref[...]
    gprob = lax.dot_general(
        ga, v_ref[...], (((1,), (1,)), ((), ())), preferred_element_type=jnp.float32
    )
    gs = (probs * (gprob - jnp.sum(gprob * probs, axis=-1, keepdims=True)) * score_scale).astype(
        jnp.bfloat16
    )
    gq = jnp.dot(gs, k_ref[...], preferred_element_type=jnp.float32)
    gk = lax.dot_general(gs, q_ref[...], (((0,), (0,)), ((), ())), preferred_element_type=jnp.float32)
    gv = lax.dot_general(
        probs_b_ref[...], ga, (((0,), (0,)), ((), ())), preferred_element_type=jnp.float32
    )
    cosine = cos_ref[...]
    sine = sin_ref[...]
    gq = gq * cosine + pltpu.roll(gq, head // 2, 1) * sine
    gk = gk * cosine + pltpu.roll(gk, head // 2, 1) * sine
    gp = jnp.concatenate([gq, gk, gv], axis=-1).astype(jnp.bfloat16)
    gh = lax.dot_general(gp, wp_ref[...], (((1,), (1,)), ((), ())), preferred_element_type=jnp.float32)
    normed = normed_ref[...]
    gain_term = jnp.sum(gh * normed, axis=0, keepdims=True)
    gn = gh * gain_ref[...]
    mean = jnp.sum(gn * normed, axis=-1, keepdims=True) * (1.0 / gn.shape[-1])
    gx = inv_ref[...] * (gn - normed * mean)
    out_ref[...] = (grad_in.astype(jnp.float32) + gx).astype(out_ref.dtype)
    gstore_ref[...] = grad_in
    pstore_ref[...] = gp
    gacc_out[...] = gacc_ref[...] + jnp.where(scal[2] == 1, gain_term, 0.0)


def tick_call(scal, recv, upstream, w_back, w_proj, gain_row, normed, inv_rms, probs, probs_b,
              query_rows, key_rows, value_rows, cos2, sin2, grad_store, proj_store, gain_acc):
    micro_count, length, width = normed.shape
    head = query_rows.shape[-1]
    full = lambda shape: pl.BlockSpec(shape, lambda i, s: (0,) * len(shape))
    per_micro = lambda shape: pl.BlockSpec((None,) + shape, lambda i, s: (s[0],) + (0,) * len(shape))
    per_slot = lambda shape: pl.BlockSpec((None,) + shape, lambda i, s: (s[1],) + (0,) * len(shape))
    flops = 2 * length * width * 4 * head * 2
    return pl.pallas_call(
        tick_kernel,
        out_shape=(
            jax.ShapeDtypeStruct((length, width), jnp.bfloat16),
            jax.ShapeDtypeStruct(grad_store.shape, grad_store.dtype),
            jax.ShapeDtypeStruct(proj_store.shape, proj_store.dtype),
            jax.ShapeDtypeStruct(gain_acc.shape, gain_acc.dtype),
        ),
        grid_spec=pltpu.PrefetchScalarGridSpec(
            num_scalar_prefetch=1,
            grid=(1,),
            in_specs=[
                full((length, width)),
                per_micro((length, width)),
                full((width, head)),
                full((width, 3 * head)),
                full((1, width)),
                per_micro((length, width)),
                per_micro((length, 1)),
                per_micro((length, length)),
                per_micro((length, length)),
                per_micro((length, head)),
                per_micro((length, head)),
                per_micro((length, head)),
                full((length, head)),
                full((length, head)),
                pl.BlockSpec(memory_space=pl.ANY),
                pl.BlockSpec(memory_space=pl.ANY),
                full((1, width)),
            ],
            out_specs=[
                full((length, width)),
                per_slot((length, width)),
                per_slot((length, 3 * head)),
                full((1, width)),
            ],
        ),
        input_output_aliases={15: 1, 16: 2, 17: 3},
        cost_estimate=pl.CostEstimate(
            flops=flops, transcendentals=0, bytes_accessed=2 * width * 4 * head + 8 * length * width
        ),
        compiler_params=pltpu.CompilerParams(vmem_limit_bytes=48 * 1024 * 1024),
    )(scal, recv, upstream, w_back, w_proj, gain_row, normed, inv_rms, probs, probs_b,
      query_rows, key_rows, value_rows, cos2, sin2, grad_store, proj_store, gain_acc)


def on_device(inputs, upstream, weights, gain):
    sections = SH * SY
    here = lax.axis_index("sh") * SY + lax.axis_index("sy")
    micro_count = inputs.shape[1]
    length = inputs.shape[2]
    width = inputs.shape[3]
    head = weights.shape[2] // 4
    rows_here = weights.shape[1]
    groups = FX * FZ * FC

    gain_rows = jnp.zeros((16, weights.shape[2]), jnp.bfloat16)
    gain_rows = lax.dynamic_update_slice(gain_rows, gain[0][None, :], (0, 0))
    packed = jnp.concatenate([weights[0], gain_rows], axis=0)
    staged = lax.all_gather(packed, "fx", axis=0, tiled=True)
    staged = lax.all_gather(staged, "fz", axis=0, tiled=True)
    staged = lax.all_gather(staged, "fc", axis=0, tiled=True)
    gathered = (
        staged.reshape(FC, FZ, FX, rows_here + 16, weights.shape[2])
        .transpose(2, 1, 0, 3, 4)
        .reshape(groups, rows_here + 16, weights.shape[2])
    )
    w_full = gathered[:, :rows_here, :].reshape(groups * rows_here, weights.shape[2])
    gain_full = gathered[:, rows_here, :rows_here].reshape(groups * rows_here)
    wide_gain = gain_full.astype(jnp.float32)
    w_proj = w_full[:, : 3 * head]
    w_back = w_full[:, 3 * head :]

    xfloat = inputs[0].astype(jnp.float32)
    inv_rms = lax.rsqrt(jnp.mean(xfloat * xfloat, axis=-1, keepdims=True) + 1e-05)
    normed = xfloat * inv_rms
    hidden = (normed * wide_gain).astype(jnp.bfloat16)
    proj = jnp.dot(
        hidden.reshape(micro_count * length, width), w_proj, preferred_element_type=jnp.float32
    ).reshape(micro_count, length, 3 * head)
    cosine, sine_table = rope_tables(length, head)
    query_rows = rotate(proj[..., :head], cosine, sine_table).astype(jnp.bfloat16)
    key_rows = rotate(proj[..., head : 2 * head], cosine, sine_table).astype(jnp.bfloat16)
    value_rows = proj[..., 2 * head :].astype(jnp.bfloat16)
    score_scale = head ** (-0.5)
    causal = lax.broadcasted_iota(jnp.int32, (length, length), 0) >= lax.broadcasted_iota(
        jnp.int32, (length, length), 1
    )
    scores = jnp.einsum(
        "mqh,mkh->mqk", query_rows, key_rows, preferred_element_type=jnp.float32
    ) * score_scale
    probs = jax.nn.softmax(jnp.where(causal[None], scores, -1e30), axis=-1)
    probs_b = probs.astype(jnp.bfloat16)
    attended = jnp.einsum(
        "mqk,mkh->mqh", probs_b, value_rows, preferred_element_type=jnp.float32
    ).astype(jnp.bfloat16)

    cos2 = jnp.concatenate([cosine, cosine], axis=-1)
    sin2 = jnp.concatenate([sine_table, -sine_table], axis=-1)
    gain_row = wide_gain.reshape(1, width)

    pairs = micro_count // 2

    def half_tick(period, stream, received, state):
        grad_store, proj_store, gain_acc = state
        pair = period - (sections - 1 - here)
        active = jnp.logical_and(pair >= 0, pair < pairs)
        micro = 2 * pair + stream
        clipped = jnp.clip(micro, 0, micro_count - 1)
        slot = jnp.where(active, micro + 1, jnp.where(pair < 0, 0, micro_count + 1))
        scal = jnp.stack(
            [clipped, slot, active.astype(jnp.int32), (here == sections - 1).astype(jnp.int32)]
        ).astype(jnp.int32)
        grad_out, grad_store, proj_store, gain_acc = tick_call(
            scal, received, upstream, w_back, w_proj, gain_row, normed, inv_rms, probs, probs_b,
            query_rows, key_rows, value_rows, cos2, sin2, grad_store, proj_store, gain_acc.reshape(1, width),
        )
        return grad_out, (grad_store, proj_store, gain_acc.reshape(width))

    def step_loop(period, carry):
        received_a, received_b, state = carry
        sent_a, state = half_tick(period, 0, received_a, state)
        received_a = passed_along(sent_a, SECTION, -1)
        sent_b, state = half_tick(period, 1, received_b, state)
        received_b = passed_along(sent_b, SECTION, -1)
        return (received_a, received_b, state)

    state_start = (
        jnp.zeros((micro_count + 2, length, width), jnp.bfloat16),
        jnp.zeros((micro_count + 2, length, 3 * head), jnp.bfloat16),
        jnp.zeros((width,), jnp.float32),
    )
    total_periods = sections + pairs - 1
    zero_grad = jnp.zeros((length, width), jnp.bfloat16)
    received_a, received_b, state = lax.fori_loop(
        0, total_periods - 1, step_loop, (zero_grad, zero_grad, state_start)
    )
    leftover, state = half_tick(total_periods - 1, 0, received_a, state)
    leftover, state = half_tick(total_periods - 1, 1, received_b, state)
    grad_store, proj_store, gain_acc = state
    tokens_all = micro_count * length
    grad_flat = grad_store[1 : micro_count + 1].reshape(tokens_all, width)
    proj_flat = proj_store[1 : micro_count + 1].reshape(tokens_all, 3 * head)
    att_flat = attended.reshape(tokens_all, head)
    def stage_order(rows):
        return (
            rows.reshape(tokens_all, FX, FZ, FC, rows_here)
            .transpose(0, 3, 2, 1, 4)
            .reshape(tokens_all, width)
        )

    terms = jnp.concatenate(
        [
            contract_rows(stage_order(hidden.reshape(tokens_all, width)), proj_flat),
            contract_rows(stage_order(grad_flat), att_flat),
        ],
        axis=1,
    ).astype(jnp.bfloat16)
    cols = terms.shape[1]
    terms = lax.psum_scatter(terms.reshape(FC, -1, cols), "fc", scatter_dimension=0, tiled=True)
    gain_sum = jnp.sum(lax.all_gather(gain_acc, FSDP, axis=0), axis=0)
    terms, gain_sum = lax.optimization_barrier((terms, gain_sum))
    terms = lax.psum_scatter(terms.reshape(FZ, -1, cols), "fz", scatter_dimension=0, tiled=True)
    terms = lax.psum_scatter(terms.reshape(FX, -1, cols), "fx", scatter_dimension=0, tiled=True)
    shard = terms.reshape(rows_here, cols).astype(jnp.float32)
    return (shard[None], gain_sum[None])


def solution(mesh):
    global SH, SY, FX, FZ, FC
    sections = mesh.shape["section"]
    groups = mesh.shape["fsdp"]
    SH, SY = 2, sections // 2
    FX, FZ, FC = 2, groups // 4, 2
    sub_mesh = Mesh(
        mesh.devices.reshape(SH, SY, FX, FZ, FC), ("sh", "sy", "fx", "fz", "fc")
    )
    return jax.shard_map(
        on_device,
        mesh=sub_mesh,
        in_specs=(
            P(SECTION, None, FSDP, None),
            P(None, FSDP, None),
            P(SECTION, FSDP, None),
            P(SECTION, FSDP),
        ),
        out_specs=(P(SECTION, FSDP, None), P(SECTION, None)),
        check_vma=False,
    )
```

```python
import jax
import jax.numpy as jnp
from jax import lax
from jax.experimental import pallas as pl
from jax.experimental.pallas import tpu as pltpu
from jax.sharding import Mesh, PartitionSpec as P

SECTION = ("sh", "sy")
FSDP = ("fx", "fz", "fc")
SH, SY, FX, FZ, FC = 2, 8, 2, 8, 2


def passed_along(value, axis, steps):
    count = SH * SY
    leading, last = (max(0, -steps), min(count, count - steps))
    return lax.ppermute(value, axis, [(source, source + steps) for source in range(leading, last)])


def rope_tables(length, head):
    half_head = head // 2
    position = lax.iota(jnp.float32, length)
    freq = jnp.power(500000.0, -2.0 * lax.iota(jnp.float32, half_head) / head)
    angle = position[:, None] * freq[None, :]
    return (jnp.cos(angle), jnp.sin(angle))


def rotate(value_rows, cosine, sine_table):
    half_head = value_rows.shape[-1] // 2
    first = value_rows[..., :half_head]
    second = value_rows[..., half_head:]
    return jnp.concatenate(
        [first * cosine - second * sine_table, second * cosine + first * sine_table], axis=-1
    )


def unrotate(value_rows, cosine, sine_table):
    half_head = value_rows.shape[-1] // 2
    first = value_rows[..., :half_head]
    second = value_rows[..., half_head:]
    return jnp.concatenate(
        [first * cosine + second * sine_table, second * cosine - first * sine_table], axis=-1
    )


def contract_rows(left, right):
    return lax.dot_general(
        left, right, (((0,), (0,)), ((), ())), preferred_element_type=jnp.float32
    )


def contract_cols(left, right):
    return lax.dot_general(
        left, right, (((1,), (1,)), ((), ())), preferred_element_type=jnp.float32
    )


def tick_kernel(
    scal, recv_ref, up_ref, wb_ref, wp_ref, gain_ref, normed_ref, inv_ref, probs_ref, probs_b_ref,
    q_ref, k_ref, v_ref, cos_ref, sin_ref, gstore_in, pstore_in, gacc_ref,
    out_ref, gstore_ref, pstore_ref, gacc_out,
):
    head = q_ref.shape[-1]
    score_scale = head ** (-0.5)
    grad_in = jnp.where(scal[3] == 1, up_ref[...], recv_ref[...])
    ga = jnp.dot(grad_in, wb_ref[...], preferred_element_type=jnp.float32).astype(jnp.bfloat16)
    probs = probs_ref[...]
    gprob = lax.dot_general(
        ga, v_ref[...], (((1,), (1,)), ((), ())), preferred_element_type=jnp.float32
    )
    gs = (probs * (gprob - jnp.sum(gprob * probs, axis=-1, keepdims=True)) * score_scale).astype(
        jnp.bfloat16
    )
    gq = jnp.dot(gs, k_ref[...], preferred_element_type=jnp.float32)
    gk = lax.dot_general(gs, q_ref[...], (((0,), (0,)), ((), ())), preferred_element_type=jnp.float32)
    gv = lax.dot_general(
        probs_b_ref[...], ga, (((0,), (0,)), ((), ())), preferred_element_type=jnp.float32
    )
    cosine = cos_ref[...]
    sine = sin_ref[...]
    gq = gq * cosine + pltpu.roll(gq, head // 2, 1) * sine
    gk = gk * cosine + pltpu.roll(gk, head // 2, 1) * sine
    gp = jnp.concatenate([gq, gk, gv], axis=-1).astype(jnp.bfloat16)
    gh = jnp.dot(gp, wp_ref[...], preferred_element_type=jnp.float32)
    normed = normed_ref[...]
    gain_term = jnp.sum(gh * normed, axis=0, keepdims=True)
    gn = gh * gain_ref[...]
    mean = jnp.sum(gn * normed, axis=-1, keepdims=True) * (1.0 / gn.shape[-1])
    gx = inv_ref[...] * (gn - normed * mean)
    out_ref[...] = (grad_in.astype(jnp.float32) + gx).astype(out_ref.dtype)
    gstore_ref[...] = grad_in
    pstore_ref[...] = gp
    gacc_out[...] = gacc_ref[...] + jnp.where(scal[2] == 1, gain_term, 0.0)


def tick_call(scal, recv, upstream, w_back, w_proj, gain_row, normed, inv_rms, probs, probs_b,
              query_rows, key_rows, value_rows, cos2, sin2, grad_store, proj_store, gain_acc):
    micro_count, length, width = normed.shape
    head = query_rows.shape[-1]
    full = lambda shape: pl.BlockSpec(shape, lambda i, s: (0,) * len(shape))
    per_micro = lambda shape: pl.BlockSpec((None,) + shape, lambda i, s: (s[0],) + (0,) * len(shape))
    per_slot = lambda shape: pl.BlockSpec((None,) + shape, lambda i, s: (s[1],) + (0,) * len(shape))
    flops = 2 * length * width * 4 * head * 2
    return pl.pallas_call(
        tick_kernel,
        out_shape=(
            jax.ShapeDtypeStruct((length, width), jnp.bfloat16),
            jax.ShapeDtypeStruct(grad_store.shape, grad_store.dtype),
            jax.ShapeDtypeStruct(proj_store.shape, proj_store.dtype),
            jax.ShapeDtypeStruct(gain_acc.shape, gain_acc.dtype),
        ),
        grid_spec=pltpu.PrefetchScalarGridSpec(
            num_scalar_prefetch=1,
            grid=(1,),
            in_specs=[
                full((length, width)),
                per_micro((length, width)),
                full((width, head)),
                full((3 * head, width)),
                full((1, width)),
                per_micro((length, width)),
                per_micro((length, 1)),
                per_micro((length, length)),
                per_micro((length, length)),
                per_micro((length, head)),
                per_micro((length, head)),
                per_micro((length, head)),
                full((length, head)),
                full((length, head)),
                pl.BlockSpec(memory_space=pl.ANY),
                pl.BlockSpec(memory_space=pl.ANY),
                full((1, width)),
            ],
            out_specs=[
                full((length, width)),
                per_slot((length, width)),
                per_slot((length, 3 * head)),
                full((1, width)),
            ],
        ),
        input_output_aliases={15: 1, 16: 2, 17: 3},
        cost_estimate=pl.CostEstimate(
            flops=flops, transcendentals=0, bytes_accessed=2 * width * 4 * head + 8 * length * width
        ),
        compiler_params=pltpu.CompilerParams(vmem_limit_bytes=48 * 1024 * 1024),
    )(scal, recv, upstream, w_back, w_proj, gain_row, normed, inv_rms, probs, probs_b,
      query_rows, key_rows, value_rows, cos2, sin2, grad_store, proj_store, gain_acc)


def on_device(inputs, upstream, weights, gain):
    sections = SH * SY
    here = lax.axis_index("sh") * SY + lax.axis_index("sy")
    micro_count = inputs.shape[1]
    length = inputs.shape[2]
    width = inputs.shape[3]
    head = weights.shape[2] // 4
    rows_here = weights.shape[1]
    groups = FX * FZ * FC

    gain_rows = jnp.zeros((16, weights.shape[2]), jnp.bfloat16)
    gain_rows = lax.dynamic_update_slice(gain_rows, gain[0][None, :], (0, 0))
    packed = jnp.concatenate([weights[0], gain_rows], axis=0)
    staged = lax.all_gather(packed, "fx", axis=0, tiled=True)
    staged = lax.all_gather(staged, "fz", axis=0, tiled=True)
    staged = lax.all_gather(staged, "fc", axis=0, tiled=True)
    gathered = (
        staged.reshape(FC, FZ, FX, rows_here + 16, weights.shape[2])
        .transpose(2, 1, 0, 3, 4)
        .reshape(groups, rows_here + 16, weights.shape[2])
    )
    w_full = gathered[:, :rows_here, :].reshape(groups * rows_here, weights.shape[2])
    gain_full = gathered[:, rows_here, :rows_here].reshape(groups * rows_here)
    wide_gain = gain_full.astype(jnp.float32)
    w_proj = w_full[:, : 3 * head]
    w_back = w_full[:, 3 * head :]

    xfloat = inputs[0].astype(jnp.float32)
    inv_rms = lax.rsqrt(jnp.mean(xfloat * xfloat, axis=-1, keepdims=True) + 1e-05)
    normed = xfloat * inv_rms
    hidden = (normed * wide_gain).astype(jnp.bfloat16)
    proj = jnp.dot(
        hidden.reshape(micro_count * length, width), w_proj, preferred_element_type=jnp.float32
    ).reshape(micro_count, length, 3 * head)
    cosine, sine_table = rope_tables(length, head)
    query_rows = rotate(proj[..., :head], cosine, sine_table).astype(jnp.bfloat16)
    key_rows = rotate(proj[..., head : 2 * head], cosine, sine_table).astype(jnp.bfloat16)
    value_rows = proj[..., 2 * head :].astype(jnp.bfloat16)
    score_scale = head ** (-0.5)
    causal = lax.broadcasted_iota(jnp.int32, (length, length), 0) >= lax.broadcasted_iota(
        jnp.int32, (length, length), 1
    )
    scores = jnp.einsum(
        "mqh,mkh->mqk", query_rows, key_rows, preferred_element_type=jnp.float32
    ) * score_scale
    probs = jax.nn.softmax(jnp.where(causal[None], scores, -1e30), axis=-1)
    probs_b = probs.astype(jnp.bfloat16)
    attended = jnp.einsum(
        "mqk,mkh->mqh", probs_b, value_rows, preferred_element_type=jnp.float32
    ).astype(jnp.bfloat16)

    cos2 = jnp.concatenate([cosine, cosine], axis=-1)
    sin2 = jnp.concatenate([sine_table, -sine_table], axis=-1)
    gain_row = wide_gain.reshape(1, width)
    w_proj_t = w_proj.T

    def tick(tick_no, received, state):
        grad_store, proj_store, gain_acc = state
        micro = tick_no - (sections - 1 - here)
        active = jnp.logical_and(micro >= 0, micro < micro_count)
        clipped = jnp.clip(micro, 0, micro_count - 1)
        slot = jnp.clip(micro, -1, micro_count) + 1
        scal = jnp.stack(
            [clipped, slot, active.astype(jnp.int32), (here == sections - 1).astype(jnp.int32)]
        ).astype(jnp.int32)
        grad_out, grad_store, proj_store, gain_acc = tick_call(
            scal, received, upstream, w_back, w_proj_t, gain_row, normed, inv_rms, probs, probs_b,
            query_rows, key_rows, value_rows, cos2, sin2, grad_store, proj_store, gain_acc.reshape(1, width),
        )
        return grad_out, (grad_store, proj_store, gain_acc.reshape(width))

    def step_loop(tick_no, carry):
        received, state = carry
        sent, state = tick(tick_no, received, state)
        received = passed_along(sent, SECTION, -1)
        return (received, state)

    state_start = (
        jnp.zeros((micro_count + 2, length, width), jnp.bfloat16),
        jnp.zeros((micro_count + 2, length, 3 * head), jnp.bfloat16),
        jnp.zeros((width,), jnp.float32),
    )
    total_ticks = sections + micro_count - 1
    received, state = lax.fori_loop(
        0, total_ticks - 1, step_loop, (jnp.zeros((length, width), jnp.bfloat16), state_start)
    )
    leftover, state = tick(total_ticks - 1, received, state)
    grad_store, proj_store, gain_acc = state
    tokens_all = micro_count * length
    grad_flat = grad_store[1 : micro_count + 1].reshape(tokens_all, width)
    proj_flat = proj_store[1 : micro_count + 1].reshape(tokens_all, 3 * head)
    att_flat = attended.reshape(tokens_all, head)
    def stage_order(rows):
        return (
            rows.reshape(tokens_all, FX, FZ, FC, rows_here)
            .transpose(0, 3, 2, 1, 4)
            .reshape(tokens_all, width)
        )

    terms = jnp.concatenate(
        [
            contract_rows(stage_order(hidden.reshape(tokens_all, width)), proj_flat),
            contract_rows(stage_order(grad_flat), att_flat),
        ],
        axis=1,
    ).astype(jnp.bfloat16)
    cols = terms.shape[1]
    terms = lax.psum_scatter(terms.reshape(FC, -1, cols), "fc", scatter_dimension=0, tiled=True)
    gain_sum = jnp.sum(lax.all_gather(gain_acc, FSDP, axis=0), axis=0)
    terms, gain_sum = lax.optimization_barrier((terms, gain_sum))
    terms = lax.psum_scatter(terms.reshape(FZ, -1, cols), "fz", scatter_dimension=0, tiled=True)
    terms = lax.psum_scatter(terms.reshape(FX, -1, cols), "fx", scatter_dimension=0, tiled=True)
    shard = terms.reshape(rows_here, cols).astype(jnp.float32)
    return (shard[None], gain_sum[None])


def solution(mesh):
    global SH, SY, FX, FZ, FC
    sections = mesh.shape["section"]
    groups = mesh.shape["fsdp"]
    SH, SY = 2, sections // 2
    FX, FZ, FC = 2, groups // 4, 2
    sub_mesh = Mesh(
        mesh.devices.reshape(SH, SY, FX, FZ, FC), ("sh", "sy", "fx", "fz", "fc")
    )
    return jax.shard_map(
        on_device,
        mesh=sub_mesh,
        in_specs=(
            P(SECTION, None, FSDP, None),
            P(None, FSDP, None),
            P(SECTION, FSDP, None),
            P(SECTION, FSDP),
        ),
        out_specs=(P(SECTION, FSDP, None), P(SECTION, None)),
        check_vma=False,
    )
```

```python
import jax
import jax.numpy as jnp
from jax import lax
from jax.experimental import pallas as pl
from jax.experimental.pallas import tpu as pltpu
from jax.sharding import Mesh, PartitionSpec as P

SECTION = ("sh", "sy")
FSDP = ("fx", "fz", "fc")
SH, SY, FX, FZ, FC = 2, 8, 2, 8, 2


def passed_along(value, axis, steps):
    count = SH * SY
    leading, last = (max(0, -steps), min(count, count - steps))
    return lax.ppermute(value, axis, [(source, source + steps) for source in range(leading, last)])


def rope_tables(length, head):
    half_head = head // 2
    position = lax.iota(jnp.float32, length)
    freq = jnp.power(500000.0, -2.0 * lax.iota(jnp.float32, half_head) / head)
    angle = position[:, None] * freq[None, :]
    return (jnp.cos(angle), jnp.sin(angle))


def rotate(value_rows, cosine, sine_table):
    half_head = value_rows.shape[-1] // 2
    first = value_rows[..., :half_head]
    second = value_rows[..., half_head:]
    return jnp.concatenate(
        [first * cosine - second * sine_table, second * cosine + first * sine_table], axis=-1
    )


def unrotate(value_rows, cosine, sine_table):
    half_head = value_rows.shape[-1] // 2
    first = value_rows[..., :half_head]
    second = value_rows[..., half_head:]
    return jnp.concatenate(
        [first * cosine + second * sine_table, second * cosine - first * sine_table], axis=-1
    )


def contract_rows(left, right):
    return lax.dot_general(
        left, right, (((0,), (0,)), ((), ())), preferred_element_type=jnp.float32
    )


def contract_cols(left, right):
    return lax.dot_general(
        left, right, (((1,), (1,)), ((), ())), preferred_element_type=jnp.float32
    )


def tick_kernel(
    scal, recv_ref, up_ref, wb_ref, wp_ref, gain_ref, normed_ref, inv_ref, probs_ref, probs_b_ref,
    q_ref, k_ref, v_ref, cos_ref, sin_ref, gstore_in, pstore_in, gacc_ref,
    out_ref, gstore_ref, pstore_ref, gacc_out,
):
    head = q_ref.shape[-1]
    score_scale = head ** (-0.5)
    grad_in = jnp.where(scal[3] == 1, up_ref[...], recv_ref[...])
    ga = jnp.dot(grad_in, wb_ref[...], preferred_element_type=jnp.float32).astype(jnp.bfloat16)
    probs = probs_ref[...]
    gprob = lax.dot_general(
        ga, v_ref[...], (((1,), (1,)), ((), ())), preferred_element_type=jnp.float32
    )
    gs = (probs * (gprob - jnp.sum(gprob * probs, axis=-1, keepdims=True)) * score_scale).astype(
        jnp.bfloat16
    )
    gq = jnp.dot(gs, k_ref[...], preferred_element_type=jnp.float32)
    gk = lax.dot_general(gs, q_ref[...], (((0,), (0,)), ((), ())), preferred_element_type=jnp.float32)
    gv = lax.dot_general(
        probs_b_ref[...], ga, (((0,), (0,)), ((), ())), preferred_element_type=jnp.float32
    )
    cosine = cos_ref[...]
    sine = sin_ref[...]
    gq = gq * cosine + pltpu.roll(gq, head // 2, 1) * sine
    gk = gk * cosine + pltpu.roll(gk, head // 2, 1) * sine
    gp = jnp.concatenate([gq, gk, gv], axis=-1).astype(jnp.bfloat16)
    gh = lax.dot_general(gp, wp_ref[...], (((1,), (1,)), ((), ())), preferred_element_type=jnp.float32)
    normed = normed_ref[...]
    gain_term = jnp.sum(gh * normed, axis=0, keepdims=True)
    gn = gh * gain_ref[...]
    mean = jnp.sum(gn * normed, axis=-1, keepdims=True) * (1.0 / gn.shape[-1])
    gx = inv_ref[...] * (gn - normed * mean)
    out_ref[...] = (grad_in.astype(jnp.float32) + gx).astype(out_ref.dtype)
    gstore_ref[...] = grad_in
    pstore_ref[...] = gp
    gacc_out[...] = gacc_ref[...] + jnp.where(scal[2] == 1, gain_term, 0.0)


def tick_call(scal, recv, upstream, w_back, w_proj, gain_row, normed, inv_rms, probs, probs_b,
              query_rows, key_rows, value_rows, cos2, sin2, grad_store, proj_store, gain_acc):
    micro_count, length, width = normed.shape
    head = query_rows.shape[-1]
    full = lambda shape: pl.BlockSpec(shape, lambda i, s: (0,) * len(shape))
    per_micro = lambda shape: pl.BlockSpec((None,) + shape, lambda i, s: (s[0],) + (0,) * len(shape))
    per_slot = lambda shape: pl.BlockSpec((None,) + shape, lambda i, s: (s[1],) + (0,) * len(shape))
    flops = 2 * length * width * 4 * head * 2
    return pl.pallas_call(
        tick_kernel,
        out_shape=(
            jax.ShapeDtypeStruct((length, width), jnp.bfloat16),
            jax.ShapeDtypeStruct(grad_store.shape, grad_store.dtype),
            jax.ShapeDtypeStruct(proj_store.shape, proj_store.dtype),
            jax.ShapeDtypeStruct(gain_acc.shape, gain_acc.dtype),
        ),
        grid_spec=pltpu.PrefetchScalarGridSpec(
            num_scalar_prefetch=1,
            grid=(1,),
            in_specs=[
                full((length, width)),
                per_micro((length, width)),
                full((width, head)),
                full((width, 3 * head)),
                full((1, width)),
                per_micro((length, width)),
                per_micro((length, 1)),
                per_micro((length, length)),
                per_micro((length, length)),
                per_micro((length, head)),
                per_micro((length, head)),
                per_micro((length, head)),
                full((length, head)),
                full((length, head)),
                pl.BlockSpec(memory_space=pl.ANY),
                pl.BlockSpec(memory_space=pl.ANY),
                full((1, width)),
            ],
            out_specs=[
                full((length, width)),
                per_slot((length, width)),
                per_slot((length, 3 * head)),
                full((1, width)),
            ],
        ),
        input_output_aliases={15: 1, 16: 2, 17: 3},
        cost_estimate=pl.CostEstimate(
            flops=flops, transcendentals=0, bytes_accessed=2 * width * 4 * head + 8 * length * width
        ),
        compiler_params=pltpu.CompilerParams(vmem_limit_bytes=48 * 1024 * 1024),
    )(scal, recv, upstream, w_back, w_proj, gain_row, normed, inv_rms, probs, probs_b,
      query_rows, key_rows, value_rows, cos2, sin2, grad_store, proj_store, gain_acc)


def unpack_kernel(rows_ref, gain_ref, wp_ref, wb_ref, gain_out):
    proj_cols = wp_ref.shape[-1]
    block = rows_ref[...]
    wp_ref[...] = block[:, :proj_cols]
    wb_ref[...] = block[:, proj_cols:]
    gain_out[...] = gain_ref[0:1, : gain_out.shape[-1]].astype(jnp.float32)


def unpack_weights(staged, rows_here, head):
    cols = staged.shape[-1]
    groups = FC * FZ * FX
    natural = lambda c, z, x: x * (FZ * FC) + z * FC + c
    return pl.pallas_call(
        unpack_kernel,
        out_shape=(
            jax.ShapeDtypeStruct((groups * rows_here, 3 * head), staged.dtype),
            jax.ShapeDtypeStruct((groups * rows_here, cols - 3 * head), staged.dtype),
            jax.ShapeDtypeStruct((1, groups * rows_here), jnp.float32),
        ),
        grid=(FC, FZ, FX),
        in_specs=[
            pl.BlockSpec((None, None, None, rows_here, cols), lambda c, z, x: (c, z, x, 0, 0)),
            pl.BlockSpec((None, None, None, 16, cols), lambda c, z, x: (c, z, x, rows_here // 16, 0)),
        ],
        out_specs=[
            pl.BlockSpec((rows_here, 3 * head), lambda c, z, x: (natural(c, z, x), 0)),
            pl.BlockSpec((rows_here, cols - 3 * head), lambda c, z, x: (natural(c, z, x), 0)),
            pl.BlockSpec((1, rows_here), lambda c, z, x: (0, natural(c, z, x))),
        ],
    )(staged, staged)


def on_device(inputs, upstream, weights, gain):
    sections = SH * SY
    here = lax.axis_index("sh") * SY + lax.axis_index("sy")
    micro_count = inputs.shape[1]
    length = inputs.shape[2]
    width = inputs.shape[3]
    head = weights.shape[2] // 4
    rows_here = weights.shape[1]
    groups = FX * FZ * FC

    gain_rows = jnp.zeros((16, weights.shape[2]), jnp.bfloat16)
    gain_rows = lax.dynamic_update_slice(gain_rows, gain[0][None, :], (0, 0))
    packed = jnp.concatenate([weights[0], gain_rows], axis=0)
    staged = lax.all_gather(packed, "fx", axis=0, tiled=True)
    staged = lax.all_gather(staged, "fz", axis=0, tiled=True)
    staged = lax.all_gather(staged, "fc", axis=0, tiled=True)
    w_proj, w_back, gain_row = unpack_weights(
        staged.reshape(FC, FZ, FX, rows_here + 16, weights.shape[2]), rows_here, head
    )
    wide_gain = gain_row.reshape(groups * rows_here)

    xfloat = inputs[0].astype(jnp.float32)
    inv_rms = lax.rsqrt(jnp.mean(xfloat * xfloat, axis=-1, keepdims=True) + 1e-05)
    normed = xfloat * inv_rms
    hidden = (normed * wide_gain).astype(jnp.bfloat16)
    proj = jnp.dot(
        hidden.reshape(micro_count * length, width), w_proj, preferred_element_type=jnp.float32
    ).reshape(micro_count, length, 3 * head)
    cosine, sine_table = rope_tables(length, head)
    query_rows = rotate(proj[..., :head], cosine, sine_table).astype(jnp.bfloat16)
    key_rows = rotate(proj[..., head : 2 * head], cosine, sine_table).astype(jnp.bfloat16)
    value_rows = proj[..., 2 * head :].astype(jnp.bfloat16)
    score_scale = head ** (-0.5)
    causal = lax.broadcasted_iota(jnp.int32, (length, length), 0) >= lax.broadcasted_iota(
        jnp.int32, (length, length), 1
    )
    scores = jnp.einsum(
        "mqh,mkh->mqk", query_rows, key_rows, preferred_element_type=jnp.float32
    ) * score_scale
    probs = jax.nn.softmax(jnp.where(causal[None], scores, -1e30), axis=-1)
    probs_b = probs.astype(jnp.bfloat16)
    attended = jnp.einsum(
        "mqk,mkh->mqh", probs_b, value_rows, preferred_element_type=jnp.float32
    ).astype(jnp.bfloat16)

    cos2 = jnp.concatenate([cosine, cosine], axis=-1)
    sin2 = jnp.concatenate([sine_table, -sine_table], axis=-1)

    def tick(tick_no, received, state):
        grad_store, proj_store, gain_acc = state
        micro = tick_no - (sections - 1 - here)
        active = jnp.logical_and(micro >= 0, micro < micro_count)
        clipped = jnp.clip(micro, 0, micro_count - 1)
        slot = jnp.clip(micro, -1, micro_count) + 1
        scal = jnp.stack(
            [clipped, slot, active.astype(jnp.int32), (here == sections - 1).astype(jnp.int32)]
        ).astype(jnp.int32)
        grad_out, grad_store, proj_store, gain_acc = tick_call(
            scal, received, upstream, w_back, w_proj, gain_row, normed, inv_rms, probs, probs_b,
            query_rows, key_rows, value_rows, cos2, sin2, grad_store, proj_store, gain_acc.reshape(1, width),
        )
        return grad_out, (grad_store, proj_store, gain_acc.reshape(width))

    def step_loop(tick_no, carry):
        received, state = carry
        sent, state = tick(tick_no, received, state)
        received = passed_along(sent, SECTION, -1)
        return (received, state)

    state_start = (
        jnp.zeros((micro_count + 2, length, width), jnp.bfloat16),
        jnp.zeros((micro_count + 2, length, 3 * head), jnp.bfloat16),
        jnp.zeros((width,), jnp.float32),
    )
    total_ticks = sections + micro_count - 1
    received, state = lax.fori_loop(
        0, total_ticks - 1, step_loop, (jnp.zeros((length, width), jnp.bfloat16), state_start)
    )
    leftover, state = tick(total_ticks - 1, received, state)
    grad_store, proj_store, gain_acc = state
    tokens_all = micro_count * length
    grad_flat = grad_store[1 : micro_count + 1].reshape(tokens_all, width)
    proj_flat = proj_store[1 : micro_count + 1].reshape(tokens_all, 3 * head)
    att_flat = attended.reshape(tokens_all, head)
    def stage_order(rows):
        return (
            rows.reshape(tokens_all, FX, FZ, FC, rows_here)
            .transpose(0, 3, 2, 1, 4)
            .reshape(tokens_all, width)
        )

    terms = jnp.concatenate(
        [
            contract_rows(stage_order(hidden.reshape(tokens_all, width)), proj_flat),
            contract_rows(stage_order(grad_flat), att_flat),
        ],
        axis=1,
    ).astype(jnp.bfloat16)
    cols = terms.shape[1]
    terms = lax.psum_scatter(terms.reshape(FC, -1, cols), "fc", scatter_dimension=0, tiled=True)
    gain_sum = jnp.sum(lax.all_gather(gain_acc, FSDP, axis=0), axis=0)
    terms, gain_sum = lax.optimization_barrier((terms, gain_sum))
    terms = lax.psum_scatter(terms.reshape(FZ, -1, cols), "fz", scatter_dimension=0, tiled=True)
    terms = lax.psum_scatter(terms.reshape(FX, -1, cols), "fx", scatter_dimension=0, tiled=True)
    shard = terms.reshape(rows_here, cols).astype(jnp.float32)
    return (shard[None], gain_sum[None])


def solution(mesh):
    global SH, SY, FX, FZ, FC
    sections = mesh.shape["section"]
    groups = mesh.shape["fsdp"]
    SH, SY = 2, sections // 2
    FX, FZ, FC = 2, groups // 4, 2
    sub_mesh = Mesh(
        mesh.devices.reshape(SH, SY, FX, FZ, FC), ("sh", "sy", "fx", "fz", "fc")
    )
    return jax.shard_map(
        on_device,
        mesh=sub_mesh,
        in_specs=(
            P(SECTION, None, FSDP, None),
            P(None, FSDP, None),
            P(SECTION, FSDP, None),
            P(SECTION, FSDP),
        ),
        out_specs=(P(SECTION, FSDP, None), P(SECTION, None)),
        check_vma=False,
    )
```

```python
import jax
import jax.numpy as jnp
from jax import lax
from jax.experimental import pallas as pl
from jax.experimental.pallas import tpu as pltpu
from jax.sharding import Mesh, PartitionSpec as P

SECTION = ("sh", "sy")
FSDP = ("fx", "fz", "fc")
SH, SY, FX, FZ, FC = 2, 8, 2, 8, 2


def passed_along(value, axis, steps):
    count = SH * SY
    leading, last = (max(0, -steps), min(count, count - steps))
    return lax.ppermute(value, axis, [(source, source + steps) for source in range(leading, last)])


def rope_tables(length, head):
    half_head = head // 2
    position = lax.iota(jnp.float32, length)
    freq = jnp.power(500000.0, -2.0 * lax.iota(jnp.float32, half_head) / head)
    angle = position[:, None] * freq[None, :]
    return (jnp.cos(angle), jnp.sin(angle))


def rotate(value_rows, cosine, sine_table):
    half_head = value_rows.shape[-1] // 2
    first = value_rows[..., :half_head]
    second = value_rows[..., half_head:]
    return jnp.concatenate(
        [first * cosine - second * sine_table, second * cosine + first * sine_table], axis=-1
    )


def unrotate(value_rows, cosine, sine_table):
    half_head = value_rows.shape[-1] // 2
    first = value_rows[..., :half_head]
    second = value_rows[..., half_head:]
    return jnp.concatenate(
        [first * cosine + second * sine_table, second * cosine - first * sine_table], axis=-1
    )


def contract_rows(left, right):
    return lax.dot_general(
        left, right, (((0,), (0,)), ((), ())), preferred_element_type=jnp.float32
    )


def contract_cols(left, right):
    return lax.dot_general(
        left, right, (((1,), (1,)), ((), ())), preferred_element_type=jnp.float32
    )


def tick_kernel(
    scal, recv_ref, up_ref, wb_ref, wp_ref, gain_ref, normed_ref, inv_ref, probs_ref, probs_b_ref,
    q_ref, k_ref, v_ref, cos_ref, sin_ref, gstore_in, pstore_in, gacc_ref,
    out_ref, gstore_ref, pstore_ref, gacc_out,
):
    head = q_ref.shape[-1]
    score_scale = head ** (-0.5)
    grad_in = jnp.where(scal[3] == 1, up_ref[...], recv_ref[...])
    ga = jnp.dot(grad_in, wb_ref[...], preferred_element_type=jnp.float32).astype(jnp.bfloat16)
    probs = probs_ref[...]
    gprob = lax.dot_general(
        ga, v_ref[...], (((1,), (1,)), ((), ())), preferred_element_type=jnp.float32
    )
    gs = (probs * (gprob - jnp.sum(gprob * probs, axis=-1, keepdims=True)) * score_scale).astype(
        jnp.bfloat16
    )
    gq = jnp.dot(gs, k_ref[...], preferred_element_type=jnp.float32)
    gk = lax.dot_general(gs, q_ref[...], (((0,), (0,)), ((), ())), preferred_element_type=jnp.float32)
    gv = lax.dot_general(
        probs_b_ref[...], ga, (((0,), (0,)), ((), ())), preferred_element_type=jnp.float32
    )
    cosine = cos_ref[...]
    sine = sin_ref[...]
    gq = gq * cosine + pltpu.roll(gq, head // 2, 1) * sine
    gk = gk * cosine + pltpu.roll(gk, head // 2, 1) * sine
    gp = jnp.concatenate([gq, gk, gv], axis=-1).astype(jnp.bfloat16)
    gh = lax.dot_general(gp, wp_ref[...], (((1,), (1,)), ((), ())), preferred_element_type=jnp.float32)
    normed = normed_ref[...]
    gain_term = jnp.sum(gh * normed, axis=0, keepdims=True)
    gn = gh * gain_ref[...]
    mean = jnp.sum(gn * normed, axis=-1, keepdims=True) * (1.0 / gn.shape[-1])
    gx = inv_ref[...] * (gn - normed * mean)
    out_ref[...] = (grad_in.astype(jnp.float32) + gx).astype(out_ref.dtype)
    gstore_ref[...] = grad_in
    pstore_ref[...] = gp
    gacc_out[...] = gacc_ref[...] + jnp.where(scal[2] == 1, gain_term, 0.0)


def tick_call(scal, recv, upstream, w_back, w_proj, gain_row, normed, inv_rms, probs, probs_b,
              query_rows, key_rows, value_rows, cos2, sin2, grad_store, proj_store, gain_acc):
    micro_count, length, width = normed.shape
    head = query_rows.shape[-1]
    full = lambda shape: pl.BlockSpec(shape, lambda i, s: (0,) * len(shape))
    per_micro = lambda shape: pl.BlockSpec((None,) + shape, lambda i, s: (s[0],) + (0,) * len(shape))
    per_slot = lambda shape: pl.BlockSpec((None,) + shape, lambda i, s: (s[1],) + (0,) * len(shape))
    flops = 2 * length * width * 4 * head * 2
    return pl.pallas_call(
        tick_kernel,
        out_shape=(
            jax.ShapeDtypeStruct((length, width), jnp.bfloat16),
            jax.ShapeDtypeStruct(grad_store.shape, grad_store.dtype),
            jax.ShapeDtypeStruct(proj_store.shape, proj_store.dtype),
            jax.ShapeDtypeStruct(gain_acc.shape, gain_acc.dtype),
        ),
        grid_spec=pltpu.PrefetchScalarGridSpec(
            num_scalar_prefetch=1,
            grid=(1,),
            in_specs=[
                full((length, width)),
                per_micro((length, width)),
                full((width, head)),
                full((width, 3 * head)),
                full((1, width)),
                per_micro((length, width)),
                per_micro((length, 1)),
                per_micro((length, length)),
                per_micro((length, length)),
                per_micro((length, head)),
                per_micro((length, head)),
                per_micro((length, head)),
                full((length, head)),
                full((length, head)),
                pl.BlockSpec(memory_space=pl.ANY),
                pl.BlockSpec(memory_space=pl.ANY),
                full((1, width)),
            ],
            out_specs=[
                full((length, width)),
                per_slot((length, width)),
                per_slot((length, 3 * head)),
                full((1, width)),
            ],
        ),
        input_output_aliases={15: 1, 16: 2, 17: 3},
        cost_estimate=pl.CostEstimate(
            flops=flops, transcendentals=0, bytes_accessed=2 * width * 4 * head + 8 * length * width
        ),
        compiler_params=pltpu.CompilerParams(vmem_limit_bytes=48 * 1024 * 1024),
    )(scal, recv, upstream, w_back, w_proj, gain_row, normed, inv_rms, probs, probs_b,
      query_rows, key_rows, value_rows, cos2, sin2, grad_store, proj_store, gain_acc)


def unpack_kernel(rows_ref, gain_ref, wp_ref, wb_ref, gain_out):
    proj_cols = wp_ref.shape[-1]
    block = rows_ref[...]
    wp_ref[...] = block[:, :proj_cols]
    wb_ref[...] = block[:, proj_cols:]
    gain_out[...] = gain_ref[0:1, : gain_out.shape[-1]].astype(jnp.float32)


def unpack_weights(staged, rows_here, head):
    cols = staged.shape[-1]
    groups = FC * FZ * FX
    natural = lambda c, z, x: x * (FZ * FC) + z * FC + c
    return pl.pallas_call(
        unpack_kernel,
        out_shape=(
            jax.ShapeDtypeStruct((groups * rows_here, 3 * head), staged.dtype),
            jax.ShapeDtypeStruct((groups * rows_here, cols - 3 * head), staged.dtype),
            jax.ShapeDtypeStruct((1, groups * rows_here), jnp.float32),
        ),
        grid=(FC, FZ, FX),
        in_specs=[
            pl.BlockSpec((None, None, None, rows_here, cols), lambda c, z, x: (c, z, x, 0, 0)),
            pl.BlockSpec((None, None, None, 16, cols), lambda c, z, x: (c, z, x, rows_here // 16, 0)),
        ],
        out_specs=[
            pl.BlockSpec((rows_here, 3 * head), lambda c, z, x: (natural(c, z, x), 0)),
            pl.BlockSpec((rows_here, cols - 3 * head), lambda c, z, x: (natural(c, z, x), 0)),
            pl.BlockSpec((1, rows_here), lambda c, z, x: (0, natural(c, z, x))),
        ],
    )(staged, staged)


def terms_kernel(hid_ref, g_ref, gp_ref, att_ref, out_ref):
    tokens = hid_ref.shape[0]
    gp = gp_ref[...].reshape(tokens, gp_ref.shape[-1])
    grads = g_ref[...].reshape(tokens, g_ref.shape[-1])
    first = lax.dot_general(hid_ref[...], gp, (((0,), (0,)), ((), ())), preferred_element_type=jnp.float32)
    second = lax.dot_general(grads, att_ref[...], (((0,), (0,)), ((), ())), preferred_element_type=jnp.float32)
    out_ref[...] = jnp.concatenate([first, second], axis=-1).astype(out_ref.dtype)


def weight_terms(hidden_flat, grad_store, proj_store, att_flat, rows_here):
    tokens, width = hidden_flat.shape
    micro_count, length = grad_store.shape[0] - 2, grad_store.shape[1]
    cols = proj_store.shape[-1] + att_flat.shape[-1]
    staged = lambda j: (j % FC) * (FZ * FX) + ((j // FC) % FZ) * FX + j // (FC * FZ)
    return pl.pallas_call(
        terms_kernel,
        out_shape=jax.ShapeDtypeStruct((width, cols), jnp.bfloat16),
        grid=(width // rows_here,),
        in_specs=[
            pl.BlockSpec((tokens, rows_here), lambda j: (0, j)),
            pl.BlockSpec((micro_count, length, rows_here), lambda j: (0, 0, j)),
            pl.BlockSpec((micro_count, length, proj_store.shape[-1]), lambda j: (0, 0, 0)),
            pl.BlockSpec((tokens, att_flat.shape[-1]), lambda j: (0, 0)),
        ],
        out_specs=pl.BlockSpec((rows_here, cols), lambda j: (staged(j), 0)),
    )(hidden_flat, grad_store, proj_store, att_flat)


def on_device(inputs, upstream, weights, gain):
    sections = SH * SY
    here = lax.axis_index("sh") * SY + lax.axis_index("sy")
    micro_count = inputs.shape[1]
    length = inputs.shape[2]
    width = inputs.shape[3]
    head = weights.shape[2] // 4
    rows_here = weights.shape[1]
    groups = FX * FZ * FC

    gain_rows = jnp.zeros((16, weights.shape[2]), jnp.bfloat16)
    gain_rows = lax.dynamic_update_slice(gain_rows, gain[0][None, :], (0, 0))
    packed = jnp.concatenate([weights[0], gain_rows], axis=0)
    staged = lax.all_gather(packed, "fx", axis=0, tiled=True)
    staged = lax.all_gather(staged, "fz", axis=0, tiled=True)
    staged = lax.all_gather(staged, "fc", axis=0, tiled=True)
    w_proj, w_back, gain_row = unpack_weights(
        staged.reshape(FC, FZ, FX, rows_here + 16, weights.shape[2]), rows_here, head
    )
    wide_gain = gain_row.reshape(groups * rows_here)

    xfloat = inputs[0].astype(jnp.float32)
    inv_rms = lax.rsqrt(jnp.mean(xfloat * xfloat, axis=-1, keepdims=True) + 1e-05)
    normed = xfloat * inv_rms
    hidden = (normed * wide_gain).astype(jnp.bfloat16)
    proj = jnp.dot(
        hidden.reshape(micro_count * length, width), w_proj, preferred_element_type=jnp.float32
    ).reshape(micro_count, length, 3 * head)
    cosine, sine_table = rope_tables(length, head)
    query_rows = rotate(proj[..., :head], cosine, sine_table).astype(jnp.bfloat16)
    key_rows = rotate(proj[..., head : 2 * head], cosine, sine_table).astype(jnp.bfloat16)
    value_rows = proj[..., 2 * head :].astype(jnp.bfloat16)
    score_scale = head ** (-0.5)
    causal = lax.broadcasted_iota(jnp.int32, (length, length), 0) >= lax.broadcasted_iota(
        jnp.int32, (length, length), 1
    )
    scores = jnp.einsum(
        "mqh,mkh->mqk", query_rows, key_rows, preferred_element_type=jnp.float32
    ) * score_scale
    probs = jax.nn.softmax(jnp.where(causal[None], scores, -1e30), axis=-1)
    probs_b = probs.astype(jnp.bfloat16)
    attended = jnp.einsum(
        "mqk,mkh->mqh", probs_b, value_rows, preferred_element_type=jnp.float32
    ).astype(jnp.bfloat16)

    cos2 = jnp.concatenate([cosine, cosine], axis=-1)
    sin2 = jnp.concatenate([sine_table, -sine_table], axis=-1)

    def tick(tick_no, received, state):
        grad_store, proj_store, gain_acc = state
        micro = tick_no - (sections - 1 - here)
        active = jnp.logical_and(micro >= 0, micro < micro_count)
        clipped = jnp.clip(micro, 0, micro_count - 1)
        slot = jnp.where(active, micro, jnp.where(micro < 0, micro_count, micro_count + 1))
        scal = jnp.stack(
            [clipped, slot, active.astype(jnp.int32), (here == sections - 1).astype(jnp.int32)]
        ).astype(jnp.int32)
        grad_out, grad_store, proj_store, gain_acc = tick_call(
            scal, received, upstream, w_back, w_proj, gain_row, normed, inv_rms, probs, probs_b,
            query_rows, key_rows, value_rows, cos2, sin2, grad_store, proj_store, gain_acc.reshape(1, width),
        )
        return grad_out, (grad_store, proj_store, gain_acc.reshape(width))

    def step_loop(tick_no, carry):
        received, state = carry
        sent, state = tick(tick_no, received, state)
        received = passed_along(sent, SECTION, -1)
        return (received, state)

    state_start = (
        jnp.zeros((micro_count + 2, length, width), jnp.bfloat16),
        jnp.zeros((micro_count + 2, length, 3 * head), jnp.bfloat16),
        jnp.zeros((width,), jnp.float32),
    )
    total_ticks = sections + micro_count - 1
    received, state = lax.fori_loop(
        0, total_ticks - 1, step_loop, (jnp.zeros((length, width), jnp.bfloat16), state_start)
    )
    leftover, state = tick(total_ticks - 1, received, state)
    grad_store, proj_store, gain_acc = state
    tokens_all = micro_count * length
    terms = weight_terms(
        hidden.reshape(tokens_all, width), grad_store, proj_store,
        attended.reshape(tokens_all, head), rows_here,
    )
    cols = terms.shape[1]
    terms = lax.psum_scatter(terms.reshape(FC, -1, cols), "fc", scatter_dimension=0, tiled=True)
    gain_sum = jnp.sum(lax.all_gather(gain_acc, FSDP, axis=0), axis=0)
    terms, gain_sum = lax.optimization_barrier((terms, gain_sum))
    terms = lax.psum_scatter(terms.reshape(FZ, -1, cols), "fz", scatter_dimension=0, tiled=True)
    terms = lax.psum_scatter(terms.reshape(FX, -1, cols), "fx", scatter_dimension=0, tiled=True)
    shard = terms.reshape(rows_here, cols).astype(jnp.float32)
    return (shard[None], gain_sum[None])


def solution(mesh):
    global SH, SY, FX, FZ, FC
    sections = mesh.shape["section"]
    groups = mesh.shape["fsdp"]
    SH, SY = 2, sections // 2
    FX, FZ, FC = 2, groups // 4, 2
    sub_mesh = Mesh(
        mesh.devices.reshape(SH, SY, FX, FZ, FC), ("sh", "sy", "fx", "fz", "fc")
    )
    return jax.shard_map(
        on_device,
        mesh=sub_mesh,
        in_specs=(
            P(SECTION, None, FSDP, None),
            P(None, FSDP, None),
            P(SECTION, FSDP, None),
            P(SECTION, FSDP),
        ),
        out_specs=(P(SECTION, FSDP, None), P(SECTION, None)),
        check_vma=False,
    )
```

```python
import jax
import jax.numpy as jnp
from jax import lax
from jax.experimental import pallas as pl
from jax.experimental.pallas import tpu as pltpu
from jax.sharding import Mesh, PartitionSpec as P

SECTION = ("sh", "sy")
FSDP = ("fx", "fz", "fc")
SH, SY, FX, FZ, FC = 2, 8, 2, 8, 2


def passed_along(value, axis, steps):
    count = SH * SY
    leading, last = (max(0, -steps), min(count, count - steps))
    return lax.ppermute(value, axis, [(source, source + steps) for source in range(leading, last)])


def rope_tables(length, head):
    half_head = head // 2
    position = lax.iota(jnp.float32, length)
    freq = jnp.power(500000.0, -2.0 * lax.iota(jnp.float32, half_head) / head)
    angle = position[:, None] * freq[None, :]
    return (jnp.cos(angle), jnp.sin(angle))


def rotate(value_rows, cosine, sine_table):
    half_head = value_rows.shape[-1] // 2
    first = value_rows[..., :half_head]
    second = value_rows[..., half_head:]
    return jnp.concatenate(
        [first * cosine - second * sine_table, second * cosine + first * sine_table], axis=-1
    )


def unrotate(value_rows, cosine, sine_table):
    half_head = value_rows.shape[-1] // 2
    first = value_rows[..., :half_head]
    second = value_rows[..., half_head:]
    return jnp.concatenate(
        [first * cosine + second * sine_table, second * cosine - first * sine_table], axis=-1
    )


def contract_rows(left, right):
    return lax.dot_general(
        left, right, (((0,), (0,)), ((), ())), preferred_element_type=jnp.float32
    )


def contract_cols(left, right):
    return lax.dot_general(
        left, right, (((1,), (1,)), ((), ())), preferred_element_type=jnp.float32
    )


def tick_kernel(
    scal, recv_ref, up_ref, wb_ref, wp_ref, gain_ref, normed_ref, inv_ref, probs_ref, probs_b_ref,
    q_ref, k_ref, v_ref, cos_ref, sin_ref, gstore_in, pstore_in, gacc_ref,
    out_ref, gstore_ref, pstore_ref, gacc_out,
):
    head = q_ref.shape[-1]
    score_scale = head ** (-0.5)
    grad_in = jnp.where(scal[3] == 1, up_ref[...], recv_ref[...])
    ga = jnp.dot(grad_in, wb_ref[...], preferred_element_type=jnp.float32).astype(jnp.bfloat16)
    probs = probs_ref[...]
    gprob = lax.dot_general(
        ga, v_ref[...], (((1,), (1,)), ((), ())), preferred_element_type=jnp.float32
    )
    gs = (probs * (gprob - jnp.sum(gprob * probs, axis=-1, keepdims=True)) * score_scale).astype(
        jnp.bfloat16
    )
    gq = jnp.dot(gs, k_ref[...], preferred_element_type=jnp.float32)
    gk = lax.dot_general(gs, q_ref[...], (((0,), (0,)), ((), ())), preferred_element_type=jnp.float32)
    gv = lax.dot_general(
        probs_b_ref[...], ga, (((0,), (0,)), ((), ())), preferred_element_type=jnp.float32
    )
    cosine = cos_ref[...]
    sine = sin_ref[...]
    gq = gq * cosine + pltpu.roll(gq, head // 2, 1) * sine
    gk = gk * cosine + pltpu.roll(gk, head // 2, 1) * sine
    gp = jnp.concatenate([gq, gk, gv], axis=-1).astype(jnp.bfloat16)
    gh = lax.dot_general(gp, wp_ref[...], (((1,), (1,)), ((), ())), preferred_element_type=jnp.float32)
    normed = normed_ref[...]
    gain_term = jnp.sum(gh * normed, axis=0, keepdims=True)
    gn = gh * gain_ref[...]
    mean = jnp.sum(gn * normed, axis=-1, keepdims=True) * (1.0 / gn.shape[-1])
    gx = inv_ref[...] * (gn - normed * mean)
    out_ref[...] = (grad_in.astype(jnp.float32) + gx).astype(out_ref.dtype)
    gstore_ref[...] = grad_in
    pstore_ref[...] = gp
    gacc_out[...] = gacc_ref[...] + jnp.where(scal[2] == 1, gain_term, 0.0)


def tick_call(scal, recv, upstream, w_back, w_proj, gain_row, normed, inv_rms, probs, probs_b,
              query_rows, key_rows, value_rows, cos2, sin2, grad_store, proj_store, gain_acc):
    micro_count, length, width = normed.shape
    head = query_rows.shape[-1]
    full = lambda shape: pl.BlockSpec(shape, lambda i, s: (0,) * len(shape))
    per_micro = lambda shape: pl.BlockSpec((None,) + shape, lambda i, s: (s[0],) + (0,) * len(shape))
    per_slot = lambda shape: pl.BlockSpec((None,) + shape, lambda i, s: (s[1],) + (0,) * len(shape))
    flops = 2 * length * width * 4 * head * 2
    return pl.pallas_call(
        tick_kernel,
        out_shape=(
            jax.ShapeDtypeStruct((length, width), jnp.bfloat16),
            jax.ShapeDtypeStruct(grad_store.shape, grad_store.dtype),
            jax.ShapeDtypeStruct(proj_store.shape, proj_store.dtype),
            jax.ShapeDtypeStruct(gain_acc.shape, gain_acc.dtype),
        ),
        grid_spec=pltpu.PrefetchScalarGridSpec(
            num_scalar_prefetch=1,
            grid=(1,),
            in_specs=[
                full((length, width)),
                per_micro((length, width)),
                full((width, head)),
                full((width, 3 * head)),
                full((1, width)),
                per_micro((length, width)),
                per_micro((length, 1)),
                per_micro((length, length)),
                per_micro((length, length)),
                per_micro((length, head)),
                per_micro((length, head)),
                per_micro((length, head)),
                full((length, head)),
                full((length, head)),
                pl.BlockSpec(memory_space=pl.ANY),
                pl.BlockSpec(memory_space=pl.ANY),
                full((1, width)),
            ],
            out_specs=[
                full((length, width)),
                per_slot((length, width)),
                per_slot((length, 3 * head)),
                full((1, width)),
            ],
        ),
        input_output_aliases={15: 1, 16: 2, 17: 3},
        cost_estimate=pl.CostEstimate(
            flops=flops, transcendentals=0, bytes_accessed=2 * width * 4 * head + 8 * length * width
        ),
        compiler_params=pltpu.CompilerParams(vmem_limit_bytes=48 * 1024 * 1024),
    )(scal, recv, upstream, w_back, w_proj, gain_row, normed, inv_rms, probs, probs_b,
      query_rows, key_rows, value_rows, cos2, sin2, grad_store, proj_store, gain_acc)


def unpack_kernel(rows_ref, gain_ref, wp_ref, wb_ref, gain_out):
    proj_cols = wp_ref.shape[-1]
    block = rows_ref[...]
    wp_ref[...] = block[:, :proj_cols]
    wb_ref[...] = block[:, proj_cols:]
    gain_out[...] = gain_ref[0:1, : gain_out.shape[-1]].astype(jnp.float32)


def unpack_weights(staged, rows_here, head):
    cols = staged.shape[-1]
    groups = FC * FZ * FX
    natural = lambda c, z, x: x * (FZ * FC) + z * FC + c
    return pl.pallas_call(
        unpack_kernel,
        out_shape=(
            jax.ShapeDtypeStruct((groups * rows_here, 3 * head), staged.dtype),
            jax.ShapeDtypeStruct((groups * rows_here, cols - 3 * head), staged.dtype),
            jax.ShapeDtypeStruct((1, groups * rows_here), jnp.float32),
        ),
        grid=(FC, FZ, FX),
        in_specs=[
            pl.BlockSpec((None, None, None, rows_here, cols), lambda c, z, x: (c, z, x, 0, 0)),
            pl.BlockSpec((None, None, None, 16, cols), lambda c, z, x: (c, z, x, rows_here // 16, 0)),
        ],
        out_specs=[
            pl.BlockSpec((rows_here, 3 * head), lambda c, z, x: (natural(c, z, x), 0)),
            pl.BlockSpec((rows_here, cols - 3 * head), lambda c, z, x: (natural(c, z, x), 0)),
            pl.BlockSpec((1, rows_here), lambda c, z, x: (0, natural(c, z, x))),
        ],
    )(staged, staged)


def terms_kernel(hid_ref, g_ref, gp_ref, att_ref, out_ref):
    tokens = hid_ref.shape[0]
    gp = gp_ref[...].reshape(tokens, gp_ref.shape[-1])
    grads = g_ref[...].reshape(tokens, g_ref.shape[-1])
    first = lax.dot_general(hid_ref[...], gp, (((0,), (0,)), ((), ())), preferred_element_type=jnp.float32)
    second = lax.dot_general(grads, att_ref[...], (((0,), (0,)), ((), ())), preferred_element_type=jnp.float32)
    out_ref[...] = jnp.concatenate([first, second], axis=-1).astype(out_ref.dtype)


def weight_terms(hidden_flat, grad_store, proj_store, att_flat, rows_here):
    tokens, width = hidden_flat.shape
    micro_count, length = grad_store.shape[0] - 2, grad_store.shape[1]
    cols = proj_store.shape[-1] + att_flat.shape[-1]
    staged = lambda j: (j % FC) * (FZ * FX) + ((j // FC) % FZ) * FX + j // (FC * FZ)
    return pl.pallas_call(
        terms_kernel,
        out_shape=jax.ShapeDtypeStruct((width, cols), jnp.bfloat16),
        grid=(width // rows_here,),
        in_specs=[
            pl.BlockSpec((tokens, rows_here), lambda j: (0, j)),
            pl.BlockSpec((micro_count, length, rows_here), lambda j: (0, 0, j)),
            pl.BlockSpec((micro_count, length, proj_store.shape[-1]), lambda j: (0, 0, 0)),
            pl.BlockSpec((tokens, att_flat.shape[-1]), lambda j: (0, 0)),
        ],
        out_specs=pl.BlockSpec((rows_here, cols), lambda j: (staged(j), 0)),
    )(hidden_flat, grad_store, proj_store, att_flat)


def on_device(inputs, upstream, weights, gain):
    sections = SH * SY
    here = lax.axis_index("sh") * SY + lax.axis_index("sy")
    micro_count = inputs.shape[1]
    length = inputs.shape[2]
    width = inputs.shape[3]
    head = weights.shape[2] // 4
    rows_here = weights.shape[1]
    groups = FX * FZ * FC

    gain_rows = jnp.zeros((16, weights.shape[2]), jnp.bfloat16)
    gain_rows = lax.dynamic_update_slice(gain_rows, gain[0][None, :], (0, 0))
    packed = jnp.concatenate([weights[0], gain_rows], axis=0)
    staged = lax.all_gather(packed, "fx", axis=0, tiled=True)
    staged = lax.all_gather(staged, "fz", axis=0, tiled=True)
    staged = lax.all_gather(staged, "fc", axis=0, tiled=True)
    w_proj, w_back, gain_row = unpack_weights(
        staged.reshape(FC, FZ, FX, rows_here + 16, weights.shape[2]), rows_here, head
    )
    wide_gain = gain_row.reshape(groups * rows_here)

    xfloat = inputs[0].astype(jnp.float32)
    inv_rms = lax.rsqrt(jnp.mean(xfloat * xfloat, axis=-1, keepdims=True) + 1e-05)
    normed = xfloat * inv_rms
    hidden = (normed * wide_gain).astype(jnp.bfloat16)
    proj = jnp.dot(
        hidden.reshape(micro_count * length, width), w_proj, preferred_element_type=jnp.float32
    ).reshape(micro_count, length, 3 * head)
    cosine, sine_table = rope_tables(length, head)
    query_rows = rotate(proj[..., :head], cosine, sine_table).astype(jnp.bfloat16)
    key_rows = rotate(proj[..., head : 2 * head], cosine, sine_table).astype(jnp.bfloat16)
    value_rows = proj[..., 2 * head :].astype(jnp.bfloat16)
    score_scale = head ** (-0.5)
    causal = lax.broadcasted_iota(jnp.int32, (length, length), 0) >= lax.broadcasted_iota(
        jnp.int32, (length, length), 1
    )
    scores = jnp.einsum(
        "mqh,mkh->mqk", query_rows, key_rows, preferred_element_type=jnp.float32
    ) * score_scale
    probs = jax.nn.softmax(jnp.where(causal[None], scores, -1e30), axis=-1)
    probs_b = probs.astype(jnp.bfloat16)
    attended = jnp.einsum(
        "mqk,mkh->mqh", probs_b, value_rows, preferred_element_type=jnp.float32
    ).astype(jnp.bfloat16)

    cos2 = jnp.concatenate([cosine, cosine], axis=-1)
    sin2 = jnp.concatenate([sine_table, -sine_table], axis=-1)

    def tick(tick_no, received, state):
        grad_store, proj_store, gain_acc = state
        micro = tick_no - (sections - 1 - here)
        active = jnp.logical_and(micro >= 0, micro < micro_count)
        clipped = jnp.clip(micro, 0, micro_count - 1)
        slot = jnp.where(active, micro, jnp.where(micro < 0, micro_count, micro_count + 1))
        scal = jnp.stack(
            [clipped, slot, active.astype(jnp.int32), (here == sections - 1).astype(jnp.int32)]
        ).astype(jnp.int32)
        grad_out, grad_store, proj_store, gain_acc = tick_call(
            scal, received, upstream, w_back, w_proj, gain_row, normed, inv_rms, probs, probs_b,
            query_rows, key_rows, value_rows, cos2, sin2, grad_store, proj_store, gain_acc.reshape(1, width),
        )
        return grad_out, (grad_store, proj_store, gain_acc.reshape(width))

    def step_loop(tick_no, carry):
        received, state = carry
        sent, state = tick(tick_no, received, state)
        received = passed_along(sent, SECTION, -1)
        return (received, state)

    state_start = (
        jnp.zeros((micro_count + 2, length, width), jnp.bfloat16),
        jnp.zeros((micro_count + 2, length, 3 * head), jnp.bfloat16),
        jnp.zeros((width,), jnp.float32),
    )
    total_ticks = sections + micro_count - 1
    received, state = lax.fori_loop(
        0, total_ticks - 1, step_loop, (jnp.zeros((length, width), jnp.bfloat16), state_start)
    )
    leftover, state = tick(total_ticks - 1, received, state)
    grad_store, proj_store, gain_acc = state
    tokens_all = micro_count * length
    terms = weight_terms(
        hidden.reshape(tokens_all, width), grad_store, proj_store,
        attended.reshape(tokens_all, head), rows_here,
    )
    cols = terms.shape[1]
    terms = lax.psum_scatter(terms.reshape(FC, -1, cols), "fc", scatter_dimension=0, tiled=True)
    terms = lax.psum_scatter(terms.reshape(FZ, -1, cols), "fz", scatter_dimension=0, tiled=True)
    gain_sum = jnp.sum(lax.all_gather(gain_acc, FSDP, axis=0), axis=0)
    terms, gain_sum = lax.optimization_barrier((terms, gain_sum))
    terms = lax.psum_scatter(terms.reshape(FX, -1, cols), "fx", scatter_dimension=0, tiled=True)
    shard = terms.reshape(rows_here, cols).astype(jnp.float32)
    return (shard[None], gain_sum[None])


def solution(mesh):
    global SH, SY, FX, FZ, FC
    sections = mesh.shape["section"]
    groups = mesh.shape["fsdp"]
    SH, SY = 2, sections // 2
    FX, FZ, FC = 2, groups // 4, 2
    sub_mesh = Mesh(
        mesh.devices.reshape(SH, SY, FX, FZ, FC), ("sh", "sy", "fx", "fz", "fc")
    )
    return jax.shard_map(
        on_device,
        mesh=sub_mesh,
        in_specs=(
            P(SECTION, None, FSDP, None),
            P(None, FSDP, None),
            P(SECTION, FSDP, None),
            P(SECTION, FSDP),
        ),
        out_specs=(P(SECTION, FSDP, None), P(SECTION, None)),
        check_vma=False,
    )
```

```python
import jax
import jax.numpy as jnp
from jax import lax
from jax.experimental import pallas as pl
from jax.experimental.pallas import tpu as pltpu
from jax.sharding import Mesh, PartitionSpec as P

SECTION = ("sh", "sy")
FSDP = ("fx", "fz", "fc")
SH, SY, FX, FZ, FC = 2, 8, 2, 8, 2


def passed_along(value, axis, steps):
    count = SH * SY
    leading, last = (max(0, -steps), min(count, count - steps))
    return lax.ppermute(value, axis, [(source, source + steps) for source in range(leading, last)])


def rope_tables(length, head):
    half_head = head // 2
    position = lax.iota(jnp.float32, length)
    freq = jnp.power(500000.0, -2.0 * lax.iota(jnp.float32, half_head) / head)
    angle = position[:, None] * freq[None, :]
    return (jnp.cos(angle), jnp.sin(angle))


def rotate(value_rows, cosine, sine_table):
    half_head = value_rows.shape[-1] // 2
    first = value_rows[..., :half_head]
    second = value_rows[..., half_head:]
    return jnp.concatenate(
        [first * cosine - second * sine_table, second * cosine + first * sine_table], axis=-1
    )


def unrotate(value_rows, cosine, sine_table):
    half_head = value_rows.shape[-1] // 2
    first = value_rows[..., :half_head]
    second = value_rows[..., half_head:]
    return jnp.concatenate(
        [first * cosine + second * sine_table, second * cosine - first * sine_table], axis=-1
    )


def contract_rows(left, right):
    return lax.dot_general(
        left, right, (((0,), (0,)), ((), ())), preferred_element_type=jnp.float32
    )


def contract_cols(left, right):
    return lax.dot_general(
        left, right, (((1,), (1,)), ((), ())), preferred_element_type=jnp.float32
    )


def tick_kernel(
    scal, recv_ref, up_ref, wb_ref, wp_ref, gain_ref, normed_ref, inv_ref, probs_ref, probs_b_ref,
    q_ref, k_ref, v_ref, cos_ref, sin_ref, gstore_in, pstore_in, gacc_ref,
    out_ref, gstore_ref, pstore_ref, gacc_out,
):
    head = q_ref.shape[-1]
    score_scale = head ** (-0.5)
    grad_in = jnp.where(scal[3] == 1, up_ref[...], recv_ref[...])
    ga = jnp.dot(grad_in, wb_ref[...], preferred_element_type=jnp.float32).astype(jnp.bfloat16)
    probs = probs_ref[...]
    gprob = lax.dot_general(
        ga, v_ref[...], (((1,), (1,)), ((), ())), preferred_element_type=jnp.float32
    )
    gs = (probs * (gprob - jnp.sum(gprob * probs, axis=-1, keepdims=True)) * score_scale).astype(
        jnp.bfloat16
    )
    gq = jnp.dot(gs, k_ref[...], preferred_element_type=jnp.float32)
    gk = lax.dot_general(gs, q_ref[...], (((0,), (0,)), ((), ())), preferred_element_type=jnp.float32)
    gv = lax.dot_general(
        probs_b_ref[...], ga, (((0,), (0,)), ((), ())), preferred_element_type=jnp.float32
    )
    cosine = cos_ref[...]
    sine = sin_ref[...]
    gq = gq * cosine + pltpu.roll(gq, head // 2, 1) * sine
    gk = gk * cosine + pltpu.roll(gk, head // 2, 1) * sine
    gp = jnp.concatenate([gq, gk, gv], axis=-1).astype(jnp.bfloat16)
    gh = lax.dot_general(gp, wp_ref[...], (((1,), (1,)), ((), ())), preferred_element_type=jnp.float32)
    normed = normed_ref[...]
    gain_term = jnp.sum(gh * normed, axis=0, keepdims=True)
    gn = gh * gain_ref[...]
    mean = jnp.sum(gn * normed, axis=-1, keepdims=True) * (1.0 / gn.shape[-1])
    gx = inv_ref[...] * (gn - normed * mean)
    out_ref[...] = (grad_in.astype(jnp.float32) + gx).astype(out_ref.dtype)
    gstore_ref[...] = grad_in
    pstore_ref[...] = gp
    gacc_out[...] = gacc_ref[...] + jnp.where(scal[2] == 1, gain_term, 0.0)


def tick_call(scal, recv, upstream, w_back, w_proj, gain_row, normed, inv_rms, probs, probs_b,
              query_rows, key_rows, value_rows, cos2, sin2, grad_store, proj_store, gain_acc):
    micro_count, length, width = normed.shape
    head = query_rows.shape[-1]
    full = lambda shape: pl.BlockSpec(shape, lambda i, s: (0,) * len(shape))
    per_micro = lambda shape: pl.BlockSpec((None,) + shape, lambda i, s: (s[0],) + (0,) * len(shape))
    per_slot = lambda shape: pl.BlockSpec((None,) + shape, lambda i, s: (s[1],) + (0,) * len(shape))
    flops = 2 * length * width * 4 * head * 2
    return pl.pallas_call(
        tick_kernel,
        out_shape=(
            jax.ShapeDtypeStruct((length, width), jnp.bfloat16),
            jax.ShapeDtypeStruct(grad_store.shape, grad_store.dtype),
            jax.ShapeDtypeStruct(proj_store.shape, proj_store.dtype),
            jax.ShapeDtypeStruct(gain_acc.shape, gain_acc.dtype),
        ),
        grid_spec=pltpu.PrefetchScalarGridSpec(
            num_scalar_prefetch=1,
            grid=(1,),
            in_specs=[
                full((length, width)),
                per_micro((length, width)),
                full((width, head)),
                full((width, 3 * head)),
                full((1, width)),
                per_micro((length, width)),
                per_micro((length, 1)),
                per_micro((length, length)),
                per_micro((length, length)),
                per_micro((length, head)),
                per_micro((length, head)),
                per_micro((length, head)),
                full((length, head)),
                full((length, head)),
                pl.BlockSpec(memory_space=pl.ANY),
                pl.BlockSpec(memory_space=pl.ANY),
                full((1, width)),
            ],
            out_specs=[
                full((length, width)),
                per_slot((length, width)),
                per_slot((length, 3 * head)),
                full((1, width)),
            ],
        ),
        input_output_aliases={15: 1, 16: 2, 17: 3},
        cost_estimate=pl.CostEstimate(
            flops=flops, transcendentals=0, bytes_accessed=2 * width * 4 * head + 8 * length * width
        ),
        compiler_params=pltpu.CompilerParams(vmem_limit_bytes=48 * 1024 * 1024),
    )(scal, recv, upstream, w_back, w_proj, gain_row, normed, inv_rms, probs, probs_b,
      query_rows, key_rows, value_rows, cos2, sin2, grad_store, proj_store, gain_acc)


def unpack_kernel(rows_ref, gain_ref, wp_ref, wb_ref, gain_out):
    proj_cols = wp_ref.shape[-1]
    rows = rows_ref.shape[1]
    for core in range(rows_ref.shape[0]):
        block = rows_ref[core]
        wp_ref[core * rows : (core + 1) * rows, :] = block[:, :proj_cols]
        wb_ref[core * rows : (core + 1) * rows, :] = block[:, proj_cols:]
        gain_out[core : core + 1, :] = gain_ref[core, 0:1, : gain_out.shape[-1]].astype(jnp.float32)


def unpack_weights(staged, rows_here, head):
    cols = staged.shape[-1]
    groups = FC * FZ * FX
    return pl.pallas_call(
        unpack_kernel,
        out_shape=(
            jax.ShapeDtypeStruct((groups * rows_here, 3 * head), staged.dtype),
            jax.ShapeDtypeStruct((groups * rows_here, cols - 3 * head), staged.dtype),
            jax.ShapeDtypeStruct((FX * FZ, FC, rows_here), jnp.float32),
        ),
        grid=(FX, FZ),
        in_specs=[
            pl.BlockSpec((FC, None, None, rows_here, cols), lambda x, z: (0, z, x, 0, 0)),
            pl.BlockSpec((FC, None, None, 16, cols), lambda x, z: (0, z, x, rows_here // 16, 0)),
        ],
        out_specs=[
            pl.BlockSpec((FC * rows_here, 3 * head), lambda x, z: (x * FZ + z, 0)),
            pl.BlockSpec((FC * rows_here, cols - 3 * head), lambda x, z: (x * FZ + z, 0)),
            pl.BlockSpec((None, FC, rows_here), lambda x, z: (x * FZ + z, 0, 0)),
        ],
    )(staged, staged)

def terms_kernel(hid_ref, g_ref, gp_ref, att_ref, out_ref):
    tokens = hid_ref.shape[0]
    gp = gp_ref[...].reshape(tokens, gp_ref.shape[-1])
    grads = g_ref[...].reshape(tokens, g_ref.shape[-1])
    first = lax.dot_general(hid_ref[...], gp, (((0,), (0,)), ((), ())), preferred_element_type=jnp.float32)
    second = lax.dot_general(grads, att_ref[...], (((0,), (0,)), ((), ())), preferred_element_type=jnp.float32)
    out_ref[...] = jnp.concatenate([first, second], axis=-1).astype(out_ref.dtype)


def weight_terms(hidden_flat, grad_store, proj_store, att_flat, rows_here):
    tokens, width = hidden_flat.shape
    micro_count, length = grad_store.shape[0] - 2, grad_store.shape[1]
    cols = proj_store.shape[-1] + att_flat.shape[-1]
    staged = lambda j: (j % FC) * (FZ * FX) + ((j // FC) % FZ) * FX + j // (FC * FZ)
    return pl.pallas_call(
        terms_kernel,
        out_shape=jax.ShapeDtypeStruct((width, cols), jnp.bfloat16),
        grid=(width // rows_here,),
        in_specs=[
            pl.BlockSpec((tokens, rows_here), lambda j: (0, j)),
            pl.BlockSpec((micro_count, length, rows_here), lambda j: (0, 0, j)),
            pl.BlockSpec((micro_count, length, proj_store.shape[-1]), lambda j: (0, 0, 0)),
            pl.BlockSpec((tokens, att_flat.shape[-1]), lambda j: (0, 0)),
        ],
        out_specs=pl.BlockSpec((rows_here, cols), lambda j: (staged(j), 0)),
    )(hidden_flat, grad_store, proj_store, att_flat)


def on_device(inputs, upstream, weights, gain):
    sections = SH * SY
    here = lax.axis_index("sh") * SY + lax.axis_index("sy")
    micro_count = inputs.shape[1]
    length = inputs.shape[2]
    width = inputs.shape[3]
    head = weights.shape[2] // 4
    rows_here = weights.shape[1]
    groups = FX * FZ * FC

    gain_rows = jnp.zeros((16, weights.shape[2]), jnp.bfloat16)
    gain_rows = lax.dynamic_update_slice(gain_rows, gain[0][None, :], (0, 0))
    packed = jnp.concatenate([weights[0], gain_rows], axis=0)
    staged = lax.all_gather(packed, "fx", axis=0, tiled=True)
    staged = lax.all_gather(staged, "fz", axis=0, tiled=True)
    staged = lax.all_gather(staged, "fc", axis=0, tiled=True)
    w_proj, w_back, gain_row = unpack_weights(
        staged.reshape(FC, FZ, FX, rows_here + 16, weights.shape[2]), rows_here, head
    )
    gain_row = gain_row.reshape(1, groups * rows_here)
    wide_gain = gain_row.reshape(groups * rows_here)

    xfloat = inputs[0].astype(jnp.float32)
    inv_rms = lax.rsqrt(jnp.mean(xfloat * xfloat, axis=-1, keepdims=True) + 1e-05)
    normed = xfloat * inv_rms
    hidden = (normed * wide_gain).astype(jnp.bfloat16)
    proj = jnp.dot(
        hidden.reshape(micro_count * length, width), w_proj, preferred_element_type=jnp.float32
    ).reshape(micro_count, length, 3 * head)
    cosine, sine_table = rope_tables(length, head)
    query_rows = rotate(proj[..., :head], cosine, sine_table).astype(jnp.bfloat16)
    key_rows = rotate(proj[..., head : 2 * head], cosine, sine_table).astype(jnp.bfloat16)
    value_rows = proj[..., 2 * head :].astype(jnp.bfloat16)
    score_scale = head ** (-0.5)
    causal = lax.broadcasted_iota(jnp.int32, (length, length), 0) >= lax.broadcasted_iota(
        jnp.int32, (length, length), 1
    )
    scores = jnp.einsum(
        "mqh,mkh->mqk", query_rows, key_rows, preferred_element_type=jnp.float32
    ) * score_scale
    probs = jax.nn.softmax(jnp.where(causal[None], scores, -1e30), axis=-1)
    probs_b = probs.astype(jnp.bfloat16)
    attended = jnp.einsum(
        "mqk,mkh->mqh", probs_b, value_rows, preferred_element_type=jnp.float32
    ).astype(jnp.bfloat16)

    cos2 = jnp.concatenate([cosine, cosine], axis=-1)
    sin2 = jnp.concatenate([sine_table, -sine_table], axis=-1)

    def tick(tick_no, received, state):
        grad_store, proj_store, gain_acc = state
        micro = tick_no - (sections - 1 - here)
        active = jnp.logical_and(micro >= 0, micro < micro_count)
        clipped = jnp.clip(micro, 0, micro_count - 1)
        slot = jnp.where(active, micro, jnp.where(micro < 0, micro_count, micro_count + 1))
        scal = jnp.stack(
            [clipped, slot, active.astype(jnp.int32), (here == sections - 1).astype(jnp.int32)]
        ).astype(jnp.int32)
        grad_out, grad_store, proj_store, gain_acc = tick_call(
            scal, received, upstream, w_back, w_proj, gain_row, normed, inv_rms, probs, probs_b,
            query_rows, key_rows, value_rows, cos2, sin2, grad_store, proj_store, gain_acc.reshape(1, width),
        )
        return grad_out, (grad_store, proj_store, gain_acc.reshape(width))

    def step_loop(tick_no, carry):
        received, state = carry
        sent, state = tick(tick_no, received, state)
        received = passed_along(sent, SECTION, -1)
        return (received, state)

    state_start = (
        jnp.zeros((micro_count + 2, length, width), jnp.bfloat16),
        jnp.zeros((micro_count + 2, length, 3 * head), jnp.bfloat16),
        jnp.zeros((width,), jnp.float32),
    )
    total_ticks = sections + micro_count - 1
    received, state = lax.fori_loop(
        0, total_ticks - 1, step_loop, (jnp.zeros((length, width), jnp.bfloat16), state_start)
    )
    leftover, state = tick(total_ticks - 1, received, state)
    grad_store, proj_store, gain_acc = state
    tokens_all = micro_count * length
    terms = weight_terms(
        hidden.reshape(tokens_all, width), grad_store, proj_store,
        attended.reshape(tokens_all, head), rows_here,
    )
    cols = terms.shape[1]
    terms = lax.psum_scatter(terms.reshape(FC, -1, cols), "fc", scatter_dimension=0, tiled=True)
    terms = lax.psum_scatter(terms.reshape(FZ, -1, cols), "fz", scatter_dimension=0, tiled=True)
    gain_sum = jnp.sum(lax.all_gather(gain_acc, FSDP, axis=0), axis=0)
    terms, gain_sum = lax.optimization_barrier((terms, gain_sum))
    terms = lax.psum_scatter(terms.reshape(FX, -1, cols), "fx", scatter_dimension=0, tiled=True)
    shard = terms.reshape(rows_here, cols).astype(jnp.float32)
    return (shard[None], gain_sum[None])


def solution(mesh):
    global SH, SY, FX, FZ, FC
    sections = mesh.shape["section"]
    groups = mesh.shape["fsdp"]
    SH, SY = 2, sections // 2
    FX, FZ, FC = 2, groups // 4, 2
    sub_mesh = Mesh(
        mesh.devices.reshape(SH, SY, FX, FZ, FC), ("sh", "sy", "fx", "fz", "fc")
    )
    return jax.shard_map(
        on_device,
        mesh=sub_mesh,
        in_specs=(
            P(SECTION, None, FSDP, None),
            P(None, FSDP, None),
            P(SECTION, FSDP, None),
            P(SECTION, FSDP),
        ),
        out_specs=(P(SECTION, FSDP, None), P(SECTION, None)),
        check_vma=False,
    )
```

```python
import jax
import jax.numpy as jnp
from jax import lax
from jax.experimental import pallas as pl
from jax.experimental.pallas import tpu as pltpu
from jax.sharding import Mesh, PartitionSpec as P

SECTION = ("sh", "sy")
FSDP = ("fx", "fz", "fc")
SH, SY, FX, FZ, FC = 2, 8, 2, 8, 2


def passed_along(value, axis, steps):
    count = SH * SY
    leading, last = (max(0, -steps), min(count, count - steps))
    return lax.ppermute(value, axis, [(source, source + steps) for source in range(leading, last)])


def rope_tables(length, head):
    half_head = head // 2
    position = lax.iota(jnp.float32, length)
    freq = jnp.power(500000.0, -2.0 * lax.iota(jnp.float32, half_head) / head)
    angle = position[:, None] * freq[None, :]
    return (jnp.cos(angle), jnp.sin(angle))


def rotate(value_rows, cosine, sine_table):
    half_head = value_rows.shape[-1] // 2
    first = value_rows[..., :half_head]
    second = value_rows[..., half_head:]
    return jnp.concatenate(
        [first * cosine - second * sine_table, second * cosine + first * sine_table], axis=-1
    )


def unrotate(value_rows, cosine, sine_table):
    half_head = value_rows.shape[-1] // 2
    first = value_rows[..., :half_head]
    second = value_rows[..., half_head:]
    return jnp.concatenate(
        [first * cosine + second * sine_table, second * cosine - first * sine_table], axis=-1
    )


def contract_rows(left, right):
    return lax.dot_general(
        left, right, (((0,), (0,)), ((), ())), preferred_element_type=jnp.float32
    )


def contract_cols(left, right):
    return lax.dot_general(
        left, right, (((1,), (1,)), ((), ())), preferred_element_type=jnp.float32
    )


def tick_kernel(
    scal, recv_ref, up_ref, wb_ref, wp_ref, gain_ref, normed_ref, inv_ref, probs_ref, probs_b_ref,
    q_ref, k_ref, v_ref, cos_ref, sin_ref, gstore_in, pstore_in, gacc_ref,
    out_ref, gstore_ref, pstore_ref, gacc_out,
):
    head = q_ref.shape[-1]
    score_scale = head ** (-0.5)
    grad_in = jnp.where(scal[3] == 1, up_ref[...], recv_ref[...])
    ga = jnp.dot(grad_in, wb_ref[...], preferred_element_type=jnp.float32).astype(jnp.bfloat16)
    probs = probs_ref[...]
    gprob = lax.dot_general(
        ga, v_ref[...], (((1,), (1,)), ((), ())), preferred_element_type=jnp.float32
    )
    gs = (probs * (gprob - jnp.sum(gprob * probs, axis=-1, keepdims=True)) * score_scale).astype(
        jnp.bfloat16
    )
    gq = jnp.dot(gs, k_ref[...], preferred_element_type=jnp.float32)
    gk = lax.dot_general(gs, q_ref[...], (((0,), (0,)), ((), ())), preferred_element_type=jnp.float32)
    gv = lax.dot_general(
        probs_b_ref[...], ga, (((0,), (0,)), ((), ())), preferred_element_type=jnp.float32
    )
    cosine = cos_ref[...]
    sine = sin_ref[...]
    gq = gq * cosine + pltpu.roll(gq, head // 2, 1) * sine
    gk = gk * cosine + pltpu.roll(gk, head // 2, 1) * sine
    gp = jnp.concatenate([gq, gk, gv], axis=-1).astype(jnp.bfloat16)
    gh = lax.dot_general(gp, wp_ref[...], (((1,), (1,)), ((), ())), preferred_element_type=jnp.float32)
    normed = normed_ref[...]
    gain_term = jnp.sum(gh * normed, axis=0, keepdims=True)
    gn = gh * gain_ref[...]
    mean = jnp.sum(gn * normed, axis=-1, keepdims=True) * (1.0 / gn.shape[-1])
    gx = inv_ref[...] * (gn - normed * mean)
    out_ref[...] = (grad_in.astype(jnp.float32) + gx).astype(out_ref.dtype)
    gstore_ref[...] = grad_in
    pstore_ref[...] = gp
    gacc_out[...] = gacc_ref[...] + jnp.where(scal[2] == 1, gain_term, 0.0)


def tick_call(scal, recv, upstream, w_back, w_proj, gain_row, normed, inv_rms, probs, probs_b,
              query_rows, key_rows, value_rows, cos2, sin2, grad_store, proj_store, gain_acc):
    micro_count, length, width = normed.shape
    head = query_rows.shape[-1]
    full = lambda shape: pl.BlockSpec(shape, lambda i, s: (0,) * len(shape))
    per_micro = lambda shape: pl.BlockSpec((None,) + shape, lambda i, s: (s[0],) + (0,) * len(shape))
    per_slot = lambda shape: pl.BlockSpec((None,) + shape, lambda i, s: (s[1],) + (0,) * len(shape))
    flops = 2 * length * width * 4 * head * 2
    return pl.pallas_call(
        tick_kernel,
        out_shape=(
            jax.ShapeDtypeStruct((length, width), jnp.bfloat16),
            jax.ShapeDtypeStruct(grad_store.shape, grad_store.dtype),
            jax.ShapeDtypeStruct(proj_store.shape, proj_store.dtype),
            jax.ShapeDtypeStruct(gain_acc.shape, gain_acc.dtype),
        ),
        grid_spec=pltpu.PrefetchScalarGridSpec(
            num_scalar_prefetch=1,
            grid=(1,),
            in_specs=[
                full((length, width)),
                per_micro((length, width)),
                full((width, head)),
                full((width, 3 * head)),
                full((1, width)),
                per_micro((length, width)),
                per_micro((length, 1)),
                per_micro((length, length)),
                per_micro((length, length)),
                per_micro((length, head)),
                per_micro((length, head)),
                per_micro((length, head)),
                full((length, head)),
                full((length, head)),
                pl.BlockSpec(memory_space=pl.ANY),
                pl.BlockSpec(memory_space=pl.ANY),
                full((1, width)),
            ],
            out_specs=[
                full((length, width)),
                per_slot((length, width)),
                per_slot((length, 3 * head)),
                full((1, width)),
            ],
        ),
        input_output_aliases={15: 1, 16: 2, 17: 3},
        cost_estimate=pl.CostEstimate(
            flops=flops, transcendentals=0, bytes_accessed=2 * width * 4 * head + 8 * length * width
        ),
        compiler_params=pltpu.CompilerParams(vmem_limit_bytes=48 * 1024 * 1024),
    )(scal, recv, upstream, w_back, w_proj, gain_row, normed, inv_rms, probs, probs_b,
      query_rows, key_rows, value_rows, cos2, sin2, grad_store, proj_store, gain_acc)


def unpack_kernel(rows_ref, gain_ref, wp_ref, wb_ref, gain_out):
    proj_cols = wp_ref.shape[-1]
    rows = rows_ref.shape[1]
    for core in range(rows_ref.shape[0]):
        block = rows_ref[core]
        wp_ref[core * rows : (core + 1) * rows, :] = block[:, :proj_cols]
        wb_ref[core * rows : (core + 1) * rows, :] = block[:, proj_cols:]
        gain_out[core : core + 1, :] = gain_ref[core, 0:1, : gain_out.shape[-1]].astype(jnp.float32)


def unpack_weights(staged, rows_here, head):
    cols = staged.shape[-1]
    groups = FC * FZ * FX
    return pl.pallas_call(
        unpack_kernel,
        out_shape=(
            jax.ShapeDtypeStruct((groups * rows_here, 3 * head), staged.dtype),
            jax.ShapeDtypeStruct((groups * rows_here, cols - 3 * head), staged.dtype),
            jax.ShapeDtypeStruct((FX * FZ, FC, rows_here), jnp.float32),
        ),
        grid=(FX, FZ),
        in_specs=[
            pl.BlockSpec((FC, None, None, rows_here, cols), lambda x, z: (0, z, x, 0, 0)),
            pl.BlockSpec((FC, None, None, 16, cols), lambda x, z: (0, z, x, rows_here // 16, 0)),
        ],
        out_specs=[
            pl.BlockSpec((FC * rows_here, 3 * head), lambda x, z: (x * FZ + z, 0)),
            pl.BlockSpec((FC * rows_here, cols - 3 * head), lambda x, z: (x * FZ + z, 0)),
            pl.BlockSpec((None, FC, rows_here), lambda x, z: (x * FZ + z, 0, 0)),
        ],
    )(staged, staged)

def terms_kernel(hid_ref, g_ref, gp_ref, att_ref, out_ref):
    tokens = hid_ref.shape[0]
    rows = out_ref.shape[1]
    gp = gp_ref[...].reshape(tokens, gp_ref.shape[-1])
    grads = g_ref[...].reshape(tokens, g_ref.shape[-1])
    att = att_ref[...]
    for core in range(out_ref.shape[0]):
        cut = slice(core * rows, (core + 1) * rows)
        first = lax.dot_general(
            hid_ref[:, cut], gp, (((0,), (0,)), ((), ())), preferred_element_type=jnp.float32
        )
        second = lax.dot_general(
            grads[:, cut], att, (((0,), (0,)), ((), ())), preferred_element_type=jnp.float32
        )
        out_ref[core] = jnp.concatenate([first, second], axis=-1).astype(out_ref.dtype)


def weight_terms(hidden_flat, grad_store, proj_store, att_flat, rows_here):
    tokens, width = hidden_flat.shape
    micro_count, length = grad_store.shape[0] - 2, grad_store.shape[1]
    cols = proj_store.shape[-1] + att_flat.shape[-1]
    both = FC * rows_here
    out = pl.pallas_call(
        terms_kernel,
        out_shape=jax.ShapeDtypeStruct((FC, FZ * FX, rows_here, cols), jnp.bfloat16),
        grid=(FX, FZ),
        in_specs=[
            pl.BlockSpec((tokens, both), lambda x, z: (0, x * FZ + z)),
            pl.BlockSpec((micro_count, length, both), lambda x, z: (0, 0, x * FZ + z)),
            pl.BlockSpec((micro_count, length, proj_store.shape[-1]), lambda x, z: (0, 0, 0)),
            pl.BlockSpec((tokens, att_flat.shape[-1]), lambda x, z: (0, 0)),
        ],
        out_specs=pl.BlockSpec((FC, None, rows_here, cols), lambda x, z: (0, z * FX + x, 0, 0)),
    )(hidden_flat, grad_store, proj_store, att_flat)
    return out.reshape(width, cols)

def on_device(inputs, upstream, weights, gain):
    sections = SH * SY
    here = lax.axis_index("sh") * SY + lax.axis_index("sy")
    micro_count = inputs.shape[1]
    length = inputs.shape[2]
    width = inputs.shape[3]
    head = weights.shape[2] // 4
    rows_here = weights.shape[1]
    groups = FX * FZ * FC

    gain_rows = jnp.zeros((16, weights.shape[2]), jnp.bfloat16)
    gain_rows = lax.dynamic_update_slice(gain_rows, gain[0][None, :], (0, 0))
    packed = jnp.concatenate([weights[0], gain_rows], axis=0)
    staged = lax.all_gather(packed, "fx", axis=0, tiled=True)
    staged = lax.all_gather(staged, "fz", axis=0, tiled=True)
    staged = lax.all_gather(staged, "fc", axis=0, tiled=True)
    w_proj, w_back, gain_row = unpack_weights(
        staged.reshape(FC, FZ, FX, rows_here + 16, weights.shape[2]), rows_here, head
    )
    gain_row = gain_row.reshape(1, groups * rows_here)
    wide_gain = gain_row.reshape(groups * rows_here)

    xfloat = inputs[0].astype(jnp.float32)
    inv_rms = lax.rsqrt(jnp.mean(xfloat * xfloat, axis=-1, keepdims=True) + 1e-05)
    normed = xfloat * inv_rms
    hidden = (normed * wide_gain).astype(jnp.bfloat16)
    proj = jnp.dot(
        hidden.reshape(micro_count * length, width), w_proj, preferred_element_type=jnp.float32
    ).reshape(micro_count, length, 3 * head)
    cosine, sine_table = rope_tables(length, head)
    query_rows = rotate(proj[..., :head], cosine, sine_table).astype(jnp.bfloat16)
    key_rows = rotate(proj[..., head : 2 * head], cosine, sine_table).astype(jnp.bfloat16)
    value_rows = proj[..., 2 * head :].astype(jnp.bfloat16)
    score_scale = head ** (-0.5)
    causal = lax.broadcasted_iota(jnp.int32, (length, length), 0) >= lax.broadcasted_iota(
        jnp.int32, (length, length), 1
    )
    scores = jnp.einsum(
        "mqh,mkh->mqk", query_rows, key_rows, preferred_element_type=jnp.float32
    ) * score_scale
    probs = jax.nn.softmax(jnp.where(causal[None], scores, -1e30), axis=-1)
    probs_b = probs.astype(jnp.bfloat16)
    attended = jnp.einsum(
        "mqk,mkh->mqh", probs_b, value_rows, preferred_element_type=jnp.float32
    ).astype(jnp.bfloat16)

    cos2 = jnp.concatenate([cosine, cosine], axis=-1)
    sin2 = jnp.concatenate([sine_table, -sine_table], axis=-1)

    def tick(tick_no, received, state):
        grad_store, proj_store, gain_acc = state
        micro = tick_no - (sections - 1 - here)
        active = jnp.logical_and(micro >= 0, micro < micro_count)
        clipped = jnp.clip(micro, 0, micro_count - 1)
        slot = jnp.where(active, micro, jnp.where(micro < 0, micro_count, micro_count + 1))
        scal = jnp.stack(
            [clipped, slot, active.astype(jnp.int32), (here == sections - 1).astype(jnp.int32)]
        ).astype(jnp.int32)
        grad_out, grad_store, proj_store, gain_acc = tick_call(
            scal, received, upstream, w_back, w_proj, gain_row, normed, inv_rms, probs, probs_b,
            query_rows, key_rows, value_rows, cos2, sin2, grad_store, proj_store, gain_acc.reshape(1, width),
        )
        return grad_out, (grad_store, proj_store, gain_acc.reshape(width))

    def step_loop(tick_no, carry):
        received, state = carry
        sent, state = tick(tick_no, received, state)
        received = passed_along(sent, SECTION, -1)
        return (received, state)

    state_start = (
        jnp.zeros((micro_count + 2, length, width), jnp.bfloat16),
        jnp.zeros((micro_count + 2, length, 3 * head), jnp.bfloat16),
        jnp.zeros((width,), jnp.float32),
    )
    total_ticks = sections + micro_count - 1
    received, state = lax.fori_loop(
        0, total_ticks - 1, step_loop, (jnp.zeros((length, width), jnp.bfloat16), state_start)
    )
    leftover, state = tick(total_ticks - 1, received, state)
    grad_store, proj_store, gain_acc = state
    tokens_all = micro_count * length
    terms = weight_terms(
        hidden.reshape(tokens_all, width), grad_store, proj_store,
        attended.reshape(tokens_all, head), rows_here,
    )
    cols = terms.shape[1]
    terms = lax.psum_scatter(terms.reshape(FC, -1, cols), "fc", scatter_dimension=0, tiled=True)
    terms = lax.psum_scatter(terms.reshape(FZ, -1, cols), "fz", scatter_dimension=0, tiled=True)
    gain_sum = jnp.sum(lax.all_gather(gain_acc, FSDP, axis=0), axis=0)
    terms, gain_sum = lax.optimization_barrier((terms, gain_sum))
    terms = lax.psum_scatter(terms.reshape(FX, -1, cols), "fx", scatter_dimension=0, tiled=True)
    shard = terms.reshape(rows_here, cols).astype(jnp.float32)
    return (shard[None], gain_sum[None])


def solution(mesh):
    global SH, SY, FX, FZ, FC
    sections = mesh.shape["section"]
    groups = mesh.shape["fsdp"]
    SH, SY = 2, sections // 2
    FX, FZ, FC = 2, groups // 4, 2
    sub_mesh = Mesh(
        mesh.devices.reshape(SH, SY, FX, FZ, FC), ("sh", "sy", "fx", "fz", "fc")
    )
    return jax.shard_map(
        on_device,
        mesh=sub_mesh,
        in_specs=(
            P(SECTION, None, FSDP, None),
            P(None, FSDP, None),
            P(SECTION, FSDP, None),
            P(SECTION, FSDP),
        ),
        out_specs=(P(SECTION, FSDP, None), P(SECTION, None)),
        check_vma=False,
    )
```

```python
import jax
import jax.numpy as jnp
from jax import lax
from jax.experimental import pallas as pl
from jax.experimental.pallas import tpu as pltpu
from jax.sharding import Mesh, PartitionSpec as P

SECTION = ("sh", "sy")
FSDP = ("fx", "fz", "fc")
SH, SY, FX, FZ, FC = 2, 8, 2, 8, 2


def passed_along(value, axis, steps):
    count = SH * SY
    leading, last = (max(0, -steps), min(count, count - steps))
    return lax.ppermute(value, axis, [(source, source + steps) for source in range(leading, last)])


def rope_tables(length, head):
    half_head = head // 2
    position = lax.iota(jnp.float32, length)
    freq = jnp.power(500000.0, -2.0 * lax.iota(jnp.float32, half_head) / head)
    angle = position[:, None] * freq[None, :]
    return (jnp.cos(angle), jnp.sin(angle))


def rotate(value_rows, cosine, sine_table):
    half_head = value_rows.shape[-1] // 2
    first = value_rows[..., :half_head]
    second = value_rows[..., half_head:]
    return jnp.concatenate(
        [first * cosine - second * sine_table, second * cosine + first * sine_table], axis=-1
    )


def unrotate(value_rows, cosine, sine_table):
    half_head = value_rows.shape[-1] // 2
    first = value_rows[..., :half_head]
    second = value_rows[..., half_head:]
    return jnp.concatenate(
        [first * cosine + second * sine_table, second * cosine - first * sine_table], axis=-1
    )


def contract_rows(left, right):
    return lax.dot_general(
        left, right, (((0,), (0,)), ((), ())), preferred_element_type=jnp.float32
    )


def contract_cols(left, right):
    return lax.dot_general(
        left, right, (((1,), (1,)), ((), ())), preferred_element_type=jnp.float32
    )


def tick_kernel(
    scal, recv_ref, up_ref, wb_ref, wp_ref, gain_ref, normed_ref, inv_ref, probs_ref, probs_b_ref,
    q_ref, k_ref, v_ref, cos_ref, sin_ref, gstore_in, pstore_in, gacc_ref,
    out_ref, gstore_ref, pstore_ref, gacc_out,
):
    head = q_ref.shape[-1]
    score_scale = head ** (-0.5)
    grad_in = jnp.where(scal[3] == 1, up_ref[...], recv_ref[...])
    ga = jnp.dot(grad_in, wb_ref[...], preferred_element_type=jnp.float32).astype(jnp.bfloat16)
    probs = probs_ref[...]
    gprob = lax.dot_general(
        ga, v_ref[...], (((1,), (1,)), ((), ())), preferred_element_type=jnp.float32
    )
    gs = (probs * (gprob - jnp.sum(gprob * probs, axis=-1, keepdims=True)) * score_scale).astype(
        jnp.bfloat16
    )
    gq = jnp.dot(gs, k_ref[...], preferred_element_type=jnp.float32)
    gk = lax.dot_general(gs, q_ref[...], (((0,), (0,)), ((), ())), preferred_element_type=jnp.float32)
    gv = lax.dot_general(
        probs_b_ref[...], ga, (((0,), (0,)), ((), ())), preferred_element_type=jnp.float32
    )
    cosine = cos_ref[...]
    sine = sin_ref[...]
    gq = gq * cosine + pltpu.roll(gq, head // 2, 1) * sine
    gk = gk * cosine + pltpu.roll(gk, head // 2, 1) * sine
    gp = jnp.concatenate([gq, gk, gv], axis=-1).astype(jnp.bfloat16)
    gh = lax.dot_general(gp, wp_ref[...], (((1,), (1,)), ((), ())), preferred_element_type=jnp.float32)
    normed = normed_ref[...]
    gain_term = jnp.sum(gh * normed, axis=0, keepdims=True)
    gn = gh * gain_ref[...]
    mean = jnp.sum(gn * normed, axis=-1, keepdims=True) * (1.0 / gn.shape[-1])
    gx = inv_ref[...] * (gn - normed * mean)
    out_ref[...] = (grad_in.astype(jnp.float32) + gx).astype(out_ref.dtype)
    gstore_ref[...] = grad_in
    pstore_ref[...] = gp
    gacc_out[...] = gacc_ref[...] + jnp.where(scal[2] == 1, gain_term, 0.0)


def tick_call(scal, recv, upstream, w_back, w_proj, gain_row, normed, inv_rms, probs, probs_b,
              query_rows, key_rows, value_rows, cos2, sin2, grad_store, proj_store, gain_acc):
    micro_count, length, width = normed.shape
    head = query_rows.shape[-1]
    full = lambda shape: pl.BlockSpec(shape, lambda i, s: (0,) * len(shape))
    per_micro = lambda shape: pl.BlockSpec((None,) + shape, lambda i, s: (s[0],) + (0,) * len(shape))
    per_slot = lambda shape: pl.BlockSpec((None,) + shape, lambda i, s: (s[1],) + (0,) * len(shape))
    flops = 2 * length * width * 4 * head * 2
    return pl.pallas_call(
        tick_kernel,
        out_shape=(
            jax.ShapeDtypeStruct((length, width), jnp.bfloat16),
            jax.ShapeDtypeStruct(grad_store.shape, grad_store.dtype),
            jax.ShapeDtypeStruct(proj_store.shape, proj_store.dtype),
            jax.ShapeDtypeStruct(gain_acc.shape, gain_acc.dtype),
        ),
        grid_spec=pltpu.PrefetchScalarGridSpec(
            num_scalar_prefetch=1,
            grid=(1,),
            in_specs=[
                full((length, width)),
                per_micro((length, width)),
                full((width, head)),
                full((width, 3 * head)),
                full((1, width)),
                per_micro((length, width)),
                per_micro((length, 1)),
                per_micro((length, length)),
                per_micro((length, length)),
                per_micro((length, head)),
                per_micro((length, head)),
                per_micro((length, head)),
                full((length, head)),
                full((length, head)),
                pl.BlockSpec(memory_space=pl.ANY),
                pl.BlockSpec(memory_space=pl.ANY),
                full((1, width)),
            ],
            out_specs=[
                full((length, width)),
                per_slot((length, width)),
                per_slot((length, 3 * head)),
                full((1, width)),
            ],
        ),
        input_output_aliases={15: 1, 16: 2, 17: 3},
        cost_estimate=pl.CostEstimate(
            flops=flops, transcendentals=0, bytes_accessed=2 * width * 4 * head + 8 * length * width
        ),
        compiler_params=pltpu.CompilerParams(vmem_limit_bytes=48 * 1024 * 1024),
    )(scal, recv, upstream, w_back, w_proj, gain_row, normed, inv_rms, probs, probs_b,
      query_rows, key_rows, value_rows, cos2, sin2, grad_store, proj_store, gain_acc)


def unpack_kernel(rows_ref, gain_ref, wp_ref, wb_ref, gain_out):
    proj_cols = wp_ref.shape[-1]
    rows = rows_ref.shape[2]
    fc, fz = rows_ref.shape[0], rows_ref.shape[1]
    for z in range(fz):
        for core in range(fc):
            at = z * fc + core
            block = rows_ref[core, z]
            wp_ref[at * rows : (at + 1) * rows, :] = block[:, :proj_cols]
            wb_ref[at * rows : (at + 1) * rows, :] = block[:, proj_cols:]
            gain_out[at : at + 1, :] = gain_ref[core, z, 0:1, : gain_out.shape[-1]].astype(jnp.float32)


def unpack_weights(staged, rows_here, head):
    cols = staged.shape[-1]
    groups = FC * FZ * FX
    span = FC * FZ
    return pl.pallas_call(
        unpack_kernel,
        out_shape=(
            jax.ShapeDtypeStruct((groups * rows_here, 3 * head), staged.dtype),
            jax.ShapeDtypeStruct((groups * rows_here, cols - 3 * head), staged.dtype),
            jax.ShapeDtypeStruct((FX, span, rows_here), jnp.float32),
        ),
        grid=(FX,),
        in_specs=[
            pl.BlockSpec((FC, FZ, None, rows_here, cols), lambda x: (0, 0, x, 0, 0)),
            pl.BlockSpec((FC, FZ, None, 16, cols), lambda x: (0, 0, x, rows_here // 16, 0)),
        ],
        out_specs=[
            pl.BlockSpec((span * rows_here, 3 * head), lambda x: (x, 0)),
            pl.BlockSpec((span * rows_here, cols - 3 * head), lambda x: (x, 0)),
            pl.BlockSpec((None, span, rows_here), lambda x: (x, 0, 0)),
        ],
    )(staged, staged)

def terms_kernel(hid_ref, g_ref, gp_ref, att_ref, out_ref):
    tokens = hid_ref.shape[0]
    rows = out_ref.shape[1]
    gp = gp_ref[...].reshape(tokens, gp_ref.shape[-1])
    grads = g_ref[...].reshape(tokens, g_ref.shape[-1])
    att = att_ref[...]
    for core in range(out_ref.shape[0]):
        cut = slice(core * rows, (core + 1) * rows)
        first = lax.dot_general(
            hid_ref[:, cut], gp, (((0,), (0,)), ((), ())), preferred_element_type=jnp.float32
        )
        second = lax.dot_general(
            grads[:, cut], att, (((0,), (0,)), ((), ())), preferred_element_type=jnp.float32
        )
        out_ref[core] = jnp.concatenate([first, second], axis=-1).astype(out_ref.dtype)


def weight_terms(hidden_flat, grad_store, proj_store, att_flat, rows_here):
    tokens, width = hidden_flat.shape
    micro_count, length = grad_store.shape[0] - 2, grad_store.shape[1]
    cols = proj_store.shape[-1] + att_flat.shape[-1]
    both = FC * rows_here
    out = pl.pallas_call(
        terms_kernel,
        out_shape=jax.ShapeDtypeStruct((FC, FZ * FX, rows_here, cols), jnp.bfloat16),
        grid=(FX, FZ),
        in_specs=[
            pl.BlockSpec((tokens, both), lambda x, z: (0, x * FZ + z)),
            pl.BlockSpec((micro_count, length, both), lambda x, z: (0, 0, x * FZ + z)),
            pl.BlockSpec((micro_count, length, proj_store.shape[-1]), lambda x, z: (0, 0, 0)),
            pl.BlockSpec((tokens, att_flat.shape[-1]), lambda x, z: (0, 0)),
        ],
        out_specs=pl.BlockSpec((FC, None, rows_here, cols), lambda x, z: (0, z * FX + x, 0, 0)),
    )(hidden_flat, grad_store, proj_store, att_flat)
    return out.reshape(width, cols)

def on_device(inputs, upstream, weights, gain):
    sections = SH * SY
    here = lax.axis_index("sh") * SY + lax.axis_index("sy")
    micro_count = inputs.shape[1]
    length = inputs.shape[2]
    width = inputs.shape[3]
    head = weights.shape[2] // 4
    rows_here = weights.shape[1]
    groups = FX * FZ * FC

    gain_rows = jnp.zeros((16, weights.shape[2]), jnp.bfloat16)
    gain_rows = lax.dynamic_update_slice(gain_rows, gain[0][None, :], (0, 0))
    packed = jnp.concatenate([weights[0], gain_rows], axis=0)
    staged = lax.all_gather(packed, "fx", axis=0, tiled=True)
    staged = lax.all_gather(staged, "fz", axis=0, tiled=True)
    staged = lax.all_gather(staged, "fc", axis=0, tiled=True)
    w_proj, w_back, gain_row = unpack_weights(
        staged.reshape(FC, FZ, FX, rows_here + 16, weights.shape[2]), rows_here, head
    )
    gain_row = gain_row.reshape(1, groups * rows_here)
    wide_gain = gain_row.reshape(groups * rows_here)

    xfloat = inputs[0].astype(jnp.float32)
    inv_rms = lax.rsqrt(jnp.mean(xfloat * xfloat, axis=-1, keepdims=True) + 1e-05)
    normed = xfloat * inv_rms
    hidden = (normed * wide_gain).astype(jnp.bfloat16)
    proj = jnp.dot(
        hidden.reshape(micro_count * length, width), w_proj, preferred_element_type=jnp.float32
    ).reshape(micro_count, length, 3 * head)
    cosine, sine_table = rope_tables(length, head)
    query_rows = rotate(proj[..., :head], cosine, sine_table).astype(jnp.bfloat16)
    key_rows = rotate(proj[..., head : 2 * head], cosine, sine_table).astype(jnp.bfloat16)
    value_rows = proj[..., 2 * head :].astype(jnp.bfloat16)
    score_scale = head ** (-0.5)
    causal = lax.broadcasted_iota(jnp.int32, (length, length), 0) >= lax.broadcasted_iota(
        jnp.int32, (length, length), 1
    )
    scores = jnp.einsum(
        "mqh,mkh->mqk", query_rows, key_rows, preferred_element_type=jnp.float32
    ) * score_scale
    probs = jax.nn.softmax(jnp.where(causal[None], scores, -1e30), axis=-1)
    probs_b = probs.astype(jnp.bfloat16)
    attended = jnp.einsum(
        "mqk,mkh->mqh", probs_b, value_rows, preferred_element_type=jnp.float32
    ).astype(jnp.bfloat16)

    cos2 = jnp.concatenate([cosine, cosine], axis=-1)
    sin2 = jnp.concatenate([sine_table, -sine_table], axis=-1)

    def tick(tick_no, received, state):
        grad_store, proj_store, gain_acc = state
        micro = tick_no - (sections - 1 - here)
        active = jnp.logical_and(micro >= 0, micro < micro_count)
        clipped = jnp.clip(micro, 0, micro_count - 1)
        slot = jnp.where(active, micro, jnp.where(micro < 0, micro_count, micro_count + 1))
        scal = jnp.stack(
            [clipped, slot, active.astype(jnp.int32), (here == sections - 1).astype(jnp.int32)]
        ).astype(jnp.int32)
        grad_out, grad_store, proj_store, gain_acc = tick_call(
            scal, received, upstream, w_back, w_proj, gain_row, normed, inv_rms, probs, probs_b,
            query_rows, key_rows, value_rows, cos2, sin2, grad_store, proj_store, gain_acc.reshape(1, width),
        )
        return grad_out, (grad_store, proj_store, gain_acc.reshape(width))

    def step_loop(tick_no, carry):
        received, state = carry
        sent, state = tick(tick_no, received, state)
        received = passed_along(sent, SECTION, -1)
        return (received, state)

    state_start = (
        jnp.zeros((micro_count + 2, length, width), jnp.bfloat16),
        jnp.zeros((micro_count + 2, length, 3 * head), jnp.bfloat16),
        jnp.zeros((width,), jnp.float32),
    )
    total_ticks = sections + micro_count - 1
    received, state = lax.fori_loop(
        0, total_ticks - 1, step_loop, (jnp.zeros((length, width), jnp.bfloat16), state_start)
    )
    leftover, state = tick(total_ticks - 1, received, state)
    grad_store, proj_store, gain_acc = state
    tokens_all = micro_count * length
    terms = weight_terms(
        hidden.reshape(tokens_all, width), grad_store, proj_store,
        attended.reshape(tokens_all, head), rows_here,
    )
    cols = terms.shape[1]
    terms = lax.psum_scatter(terms.reshape(FC, -1, cols), "fc", scatter_dimension=0, tiled=True)
    terms = lax.psum_scatter(terms.reshape(FZ, -1, cols), "fz", scatter_dimension=0, tiled=True)
    gain_sum = jnp.sum(lax.all_gather(gain_acc, FSDP, axis=0), axis=0)
    terms, gain_sum = lax.optimization_barrier((terms, gain_sum))
    terms = lax.psum_scatter(terms.reshape(FX, -1, cols), "fx", scatter_dimension=0, tiled=True)
    shard = terms.reshape(rows_here, cols).astype(jnp.float32)
    return (shard[None], gain_sum[None])


def solution(mesh):
    global SH, SY, FX, FZ, FC
    sections = mesh.shape["section"]
    groups = mesh.shape["fsdp"]
    SH, SY = 2, sections // 2
    FX, FZ, FC = 2, groups // 4, 2
    sub_mesh = Mesh(
        mesh.devices.reshape(SH, SY, FX, FZ, FC), ("sh", "sy", "fx", "fz", "fc")
    )
    return jax.shard_map(
        on_device,
        mesh=sub_mesh,
        in_specs=(
            P(SECTION, None, FSDP, None),
            P(None, FSDP, None),
            P(SECTION, FSDP, None),
            P(SECTION, FSDP),
        ),
        out_specs=(P(SECTION, FSDP, None), P(SECTION, None)),
        check_vma=False,
    )
```

```python
import jax
import jax.numpy as jnp
from jax import lax
from jax.experimental import pallas as pl
from jax.experimental.pallas import tpu as pltpu
from jax.sharding import Mesh, PartitionSpec as P

SECTION = ("sh", "sy")
FSDP = ("fx", "fz", "fc")
SH, SY, FX, FZ, FC = 2, 8, 2, 8, 2


def passed_along(value, axis, steps):
    count = SH * SY
    leading, last = (max(0, -steps), min(count, count - steps))
    return lax.ppermute(value, axis, [(source, source + steps) for source in range(leading, last)])


def rope_tables(length, head):
    half_head = head // 2
    position = lax.iota(jnp.float32, length)
    freq = jnp.power(500000.0, -2.0 * lax.iota(jnp.float32, half_head) / head)
    angle = position[:, None] * freq[None, :]
    return (jnp.cos(angle), jnp.sin(angle))


def rotate(value_rows, cosine, sine_table):
    half_head = value_rows.shape[-1] // 2
    first = value_rows[..., :half_head]
    second = value_rows[..., half_head:]
    return jnp.concatenate(
        [first * cosine - second * sine_table, second * cosine + first * sine_table], axis=-1
    )


def unrotate(value_rows, cosine, sine_table):
    half_head = value_rows.shape[-1] // 2
    first = value_rows[..., :half_head]
    second = value_rows[..., half_head:]
    return jnp.concatenate(
        [first * cosine + second * sine_table, second * cosine - first * sine_table], axis=-1
    )


def contract_rows(left, right):
    return lax.dot_general(
        left, right, (((0,), (0,)), ((), ())), preferred_element_type=jnp.float32
    )


def contract_cols(left, right):
    return lax.dot_general(
        left, right, (((1,), (1,)), ((), ())), preferred_element_type=jnp.float32
    )


def tick_kernel(
    scal, recv_ref, up_ref, wb_ref, wp_ref, gain_ref, normed_ref, inv_ref, probs_ref, probs_b_ref,
    q_ref, k_ref, v_ref, cos_ref, sin_ref, gstore_in, pstore_in, gacc_ref,
    out_ref, gstore_ref, pstore_ref, gacc_out,
):
    head = q_ref.shape[-1]
    score_scale = head ** (-0.5)
    grad_in = jnp.where(scal[3] == 1, up_ref[...], recv_ref[...])
    ga = jnp.dot(grad_in, wb_ref[...], preferred_element_type=jnp.float32).astype(jnp.bfloat16)
    probs = probs_ref[...]
    gprob = lax.dot_general(
        ga, v_ref[...], (((1,), (1,)), ((), ())), preferred_element_type=jnp.float32
    )
    gs = (probs * (gprob - jnp.sum(gprob * probs, axis=-1, keepdims=True)) * score_scale).astype(
        jnp.bfloat16
    )
    gq = jnp.dot(gs, k_ref[...], preferred_element_type=jnp.float32)
    gk = lax.dot_general(gs, q_ref[...], (((0,), (0,)), ((), ())), preferred_element_type=jnp.float32)
    gv = lax.dot_general(
        probs_b_ref[...], ga, (((0,), (0,)), ((), ())), preferred_element_type=jnp.float32
    )
    cosine = cos_ref[...]
    sine = sin_ref[...]
    gq = gq * cosine + pltpu.roll(gq, head // 2, 1) * sine
    gk = gk * cosine + pltpu.roll(gk, head // 2, 1) * sine
    gp = jnp.concatenate([gq, gk, gv], axis=-1).astype(jnp.bfloat16)
    gh = lax.dot_general(gp, wp_ref[...], (((1,), (1,)), ((), ())), preferred_element_type=jnp.float32)
    normed = normed_ref[...]
    gain_term = jnp.sum(gh * normed, axis=0, keepdims=True)
    gn = gh * gain_ref[...]
    mean = jnp.sum(gn * normed, axis=-1, keepdims=True) * (1.0 / gn.shape[-1])
    gx = inv_ref[...] * (gn - normed * mean)
    out_ref[...] = (grad_in.astype(jnp.float32) + gx).astype(out_ref.dtype)
    gstore_ref[...] = grad_in
    pstore_ref[...] = gp
    gacc_out[...] = gacc_ref[...] + jnp.where(scal[2] == 1, gain_term, 0.0)


def tick_call(scal, recv, upstream, w_back, w_proj, gain_row, normed, inv_rms, probs, probs_b,
              query_rows, key_rows, value_rows, cos2, sin2, grad_store, proj_store, gain_acc):
    micro_count, length, width = normed.shape
    head = query_rows.shape[-1]
    full = lambda shape: pl.BlockSpec(shape, lambda i, s: (0,) * len(shape))
    per_micro = lambda shape: pl.BlockSpec((None,) + shape, lambda i, s: (s[0],) + (0,) * len(shape))
    per_slot = lambda shape: pl.BlockSpec((None,) + shape, lambda i, s: (s[1],) + (0,) * len(shape))
    flops = 2 * length * width * 4 * head * 2
    return pl.pallas_call(
        tick_kernel,
        out_shape=(
            jax.ShapeDtypeStruct((length, width), jnp.bfloat16),
            jax.ShapeDtypeStruct(grad_store.shape, grad_store.dtype),
            jax.ShapeDtypeStruct(proj_store.shape, proj_store.dtype),
            jax.ShapeDtypeStruct(gain_acc.shape, gain_acc.dtype),
        ),
        grid_spec=pltpu.PrefetchScalarGridSpec(
            num_scalar_prefetch=1,
            grid=(1,),
            in_specs=[
                full((length, width)),
                per_micro((length, width)),
                full((width, head)),
                full((width, 3 * head)),
                full((1, width)),
                per_micro((length, width)),
                per_micro((length, 1)),
                per_micro((length, length)),
                per_micro((length, length)),
                per_micro((length, head)),
                per_micro((length, head)),
                per_micro((length, head)),
                full((length, head)),
                full((length, head)),
                pl.BlockSpec(memory_space=pl.ANY),
                pl.BlockSpec(memory_space=pl.ANY),
                full((1, width)),
            ],
            out_specs=[
                full((length, width)),
                per_slot((length, width)),
                per_slot((length, 3 * head)),
                full((1, width)),
            ],
        ),
        input_output_aliases={15: 1, 16: 2, 17: 3},
        cost_estimate=pl.CostEstimate(
            flops=flops, transcendentals=0, bytes_accessed=2 * width * 4 * head + 8 * length * width
        ),
        compiler_params=pltpu.CompilerParams(vmem_limit_bytes=48 * 1024 * 1024),
    )(scal, recv, upstream, w_back, w_proj, gain_row, normed, inv_rms, probs, probs_b,
      query_rows, key_rows, value_rows, cos2, sin2, grad_store, proj_store, gain_acc)


def unpack_kernel(rows_ref, gain_ref, wp_ref, wb_ref, gain_out):
    proj_cols = wp_ref.shape[-1]
    rows = rows_ref.shape[2]
    fc, fz = rows_ref.shape[0], rows_ref.shape[1]
    for z in range(fz):
        for core in range(fc):
            at = z * fc + core
            block = rows_ref[core, z]
            wp_ref[at * rows : (at + 1) * rows, :] = block[:, :proj_cols]
            wb_ref[at * rows : (at + 1) * rows, :] = block[:, proj_cols:]
            gain_out[at : at + 1, :] = gain_ref[core, z, 0:1, : gain_out.shape[-1]].astype(jnp.float32)


def unpack_weights(staged, rows_here, head):
    cols = staged.shape[-1]
    groups = FC * FZ * FX
    span = FC * FZ
    return pl.pallas_call(
        unpack_kernel,
        out_shape=(
            jax.ShapeDtypeStruct((groups * rows_here, 3 * head), staged.dtype),
            jax.ShapeDtypeStruct((groups * rows_here, cols - 3 * head), staged.dtype),
            jax.ShapeDtypeStruct((FX, span, rows_here), jnp.float32),
        ),
        grid=(FX,),
        in_specs=[
            pl.BlockSpec((FC, FZ, None, rows_here, cols), lambda x: (0, 0, x, 0, 0)),
            pl.BlockSpec((FC, FZ, None, 16, cols), lambda x: (0, 0, x, rows_here // 16, 0)),
        ],
        out_specs=[
            pl.BlockSpec((span * rows_here, 3 * head), lambda x: (x, 0)),
            pl.BlockSpec((span * rows_here, cols - 3 * head), lambda x: (x, 0)),
            pl.BlockSpec((None, span, rows_here), lambda x: (x, 0, 0)),
        ],
    )(staged, staged)

def terms_kernel(hid_ref, g_ref, gp_ref, att_ref, out_ref):
    tokens = hid_ref.shape[0]
    fc, fz, rows = out_ref.shape[0], out_ref.shape[1], out_ref.shape[2]
    gp = gp_ref[...].reshape(tokens, gp_ref.shape[-1])
    grads = g_ref[...].reshape(tokens, g_ref.shape[-1])
    att = att_ref[...]
    for z in range(fz):
        for core in range(fc):
            at = z * fc + core
            cut = slice(at * rows, (at + 1) * rows)
            first = lax.dot_general(
                hid_ref[:, cut], gp, (((0,), (0,)), ((), ())), preferred_element_type=jnp.float32
            )
            second = lax.dot_general(
                grads[:, cut], att, (((0,), (0,)), ((), ())), preferred_element_type=jnp.float32
            )
            out_ref[core, z] = jnp.concatenate([first, second], axis=-1).astype(out_ref.dtype)


def weight_terms(hidden_flat, grad_store, proj_store, att_flat, rows_here):
    tokens, width = hidden_flat.shape
    micro_count, length = grad_store.shape[0] - 2, grad_store.shape[1]
    cols = proj_store.shape[-1] + att_flat.shape[-1]
    span = FC * FZ * rows_here
    out = pl.pallas_call(
        terms_kernel,
        out_shape=jax.ShapeDtypeStruct((FC, FZ, FX, rows_here, cols), jnp.bfloat16),
        grid=(FX,),
        in_specs=[
            pl.BlockSpec((tokens, span), lambda x: (0, x)),
            pl.BlockSpec((micro_count, length, span), lambda x: (0, 0, x)),
            pl.BlockSpec((micro_count, length, proj_store.shape[-1]), lambda x: (0, 0, 0)),
            pl.BlockSpec((tokens, att_flat.shape[-1]), lambda x: (0, 0)),
        ],
        out_specs=pl.BlockSpec((FC, FZ, None, rows_here, cols), lambda x: (0, 0, x, 0, 0)),
    )(hidden_flat, grad_store, proj_store, att_flat)
    return out.reshape(width, cols)

def on_device(inputs, upstream, weights, gain):
    sections = SH * SY
    here = lax.axis_index("sh") * SY + lax.axis_index("sy")
    micro_count = inputs.shape[1]
    length = inputs.shape[2]
    width = inputs.shape[3]
    head = weights.shape[2] // 4
    rows_here = weights.shape[1]
    groups = FX * FZ * FC

    gain_rows = jnp.zeros((16, weights.shape[2]), jnp.bfloat16)
    gain_rows = lax.dynamic_update_slice(gain_rows, gain[0][None, :], (0, 0))
    packed = jnp.concatenate([weights[0], gain_rows], axis=0)
    staged = lax.all_gather(packed, "fx", axis=0, tiled=True)
    staged = lax.all_gather(staged, "fz", axis=0, tiled=True)
    staged = lax.all_gather(staged, "fc", axis=0, tiled=True)
    w_proj, w_back, gain_row = unpack_weights(
        staged.reshape(FC, FZ, FX, rows_here + 16, weights.shape[2]), rows_here, head
    )
    gain_row = gain_row.reshape(1, groups * rows_here)
    wide_gain = gain_row.reshape(groups * rows_here)

    xfloat = inputs[0].astype(jnp.float32)
    inv_rms = lax.rsqrt(jnp.mean(xfloat * xfloat, axis=-1, keepdims=True) + 1e-05)
    normed = xfloat * inv_rms
    hidden = (normed * wide_gain).astype(jnp.bfloat16)
    proj = jnp.dot(
        hidden.reshape(micro_count * length, width), w_proj, preferred_element_type=jnp.float32
    ).reshape(micro_count, length, 3 * head)
    cosine, sine_table = rope_tables(length, head)
    query_rows = rotate(proj[..., :head], cosine, sine_table).astype(jnp.bfloat16)
    key_rows = rotate(proj[..., head : 2 * head], cosine, sine_table).astype(jnp.bfloat16)
    value_rows = proj[..., 2 * head :].astype(jnp.bfloat16)
    score_scale = head ** (-0.5)
    causal = lax.broadcasted_iota(jnp.int32, (length, length), 0) >= lax.broadcasted_iota(
        jnp.int32, (length, length), 1
    )
    scores = jnp.einsum(
        "mqh,mkh->mqk", query_rows, key_rows, preferred_element_type=jnp.float32
    ) * score_scale
    probs = jax.nn.softmax(jnp.where(causal[None], scores, -1e30), axis=-1)
    probs_b = probs.astype(jnp.bfloat16)
    attended = jnp.einsum(
        "mqk,mkh->mqh", probs_b, value_rows, preferred_element_type=jnp.float32
    ).astype(jnp.bfloat16)

    cos2 = jnp.concatenate([cosine, cosine], axis=-1)
    sin2 = jnp.concatenate([sine_table, -sine_table], axis=-1)

    def tick(tick_no, received, state):
        grad_store, proj_store, gain_acc = state
        micro = tick_no - (sections - 1 - here)
        active = jnp.logical_and(micro >= 0, micro < micro_count)
        clipped = jnp.clip(micro, 0, micro_count - 1)
        slot = jnp.where(active, micro, jnp.where(micro < 0, micro_count, micro_count + 1))
        scal = jnp.stack(
            [clipped, slot, active.astype(jnp.int32), (here == sections - 1).astype(jnp.int32)]
        ).astype(jnp.int32)
        grad_out, grad_store, proj_store, gain_acc = tick_call(
            scal, received, upstream, w_back, w_proj, gain_row, normed, inv_rms, probs, probs_b,
            query_rows, key_rows, value_rows, cos2, sin2, grad_store, proj_store, gain_acc.reshape(1, width),
        )
        return grad_out, (grad_store, proj_store, gain_acc.reshape(width))

    def step_loop(tick_no, carry):
        received, state = carry
        sent, state = tick(tick_no, received, state)
        received = passed_along(sent, SECTION, -1)
        return (received, state)

    state_start = (
        jnp.zeros((micro_count + 2, length, width), jnp.bfloat16),
        jnp.zeros((micro_count + 2, length, 3 * head), jnp.bfloat16),
        jnp.zeros((width,), jnp.float32),
    )
    total_ticks = sections + micro_count - 1
    received, state = lax.fori_loop(
        0, total_ticks - 1, step_loop, (jnp.zeros((length, width), jnp.bfloat16), state_start)
    )
    leftover, state = tick(total_ticks - 1, received, state)
    grad_store, proj_store, gain_acc = state
    tokens_all = micro_count * length
    terms = weight_terms(
        hidden.reshape(tokens_all, width), grad_store, proj_store,
        attended.reshape(tokens_all, head), rows_here,
    )
    cols = terms.shape[1]
    terms = lax.psum_scatter(terms.reshape(FC, -1, cols), "fc", scatter_dimension=0, tiled=True)
    terms = lax.psum_scatter(terms.reshape(FZ, -1, cols), "fz", scatter_dimension=0, tiled=True)
    gain_sum = jnp.sum(lax.all_gather(gain_acc, FSDP, axis=0), axis=0)
    terms, gain_sum = lax.optimization_barrier((terms, gain_sum))
    terms = lax.psum_scatter(terms.reshape(FX, -1, cols), "fx", scatter_dimension=0, tiled=True)
    shard = terms.reshape(rows_here, cols).astype(jnp.float32)
    return (shard[None], gain_sum[None])


def solution(mesh):
    global SH, SY, FX, FZ, FC
    sections = mesh.shape["section"]
    groups = mesh.shape["fsdp"]
    SH, SY = 2, sections // 2
    FX, FZ, FC = 2, groups // 4, 2
    sub_mesh = Mesh(
        mesh.devices.reshape(SH, SY, FX, FZ, FC), ("sh", "sy", "fx", "fz", "fc")
    )
    return jax.shard_map(
        on_device,
        mesh=sub_mesh,
        in_specs=(
            P(SECTION, None, FSDP, None),
            P(None, FSDP, None),
            P(SECTION, FSDP, None),
            P(SECTION, FSDP),
        ),
        out_specs=(P(SECTION, FSDP, None), P(SECTION, None)),
        check_vma=False,
    )
```

```python
import jax
import jax.numpy as jnp
from jax import lax
from jax.experimental import pallas as pl
from jax.experimental.pallas import tpu as pltpu
from jax.sharding import Mesh, PartitionSpec as P

SECTION = ("sh", "sy")
FSDP = ("fx", "fz", "fc")
SH, SY, FX, FZ, FC = 2, 8, 2, 8, 2


def passed_along(value, axis, steps):
    count = SH * SY
    leading, last = (max(0, -steps), min(count, count - steps))
    return lax.ppermute(value, axis, [(source, source + steps) for source in range(leading, last)])


def rope_tables(length, head):
    half_head = head // 2
    position = lax.iota(jnp.float32, length)
    freq = jnp.power(500000.0, -2.0 * lax.iota(jnp.float32, half_head) / head)
    angle = position[:, None] * freq[None, :]
    return (jnp.cos(angle), jnp.sin(angle))


def rotate(value_rows, cosine, sine_table):
    half_head = value_rows.shape[-1] // 2
    first = value_rows[..., :half_head]
    second = value_rows[..., half_head:]
    return jnp.concatenate(
        [first * cosine - second * sine_table, second * cosine + first * sine_table], axis=-1
    )


def unrotate(value_rows, cosine, sine_table):
    half_head = value_rows.shape[-1] // 2
    first = value_rows[..., :half_head]
    second = value_rows[..., half_head:]
    return jnp.concatenate(
        [first * cosine + second * sine_table, second * cosine - first * sine_table], axis=-1
    )


def contract_rows(left, right):
    return lax.dot_general(
        left, right, (((0,), (0,)), ((), ())), preferred_element_type=jnp.float32
    )


def contract_cols(left, right):
    return lax.dot_general(
        left, right, (((1,), (1,)), ((), ())), preferred_element_type=jnp.float32
    )


def tick_kernel(
    scal, recv_ref, up_ref, wb_ref, wp_ref, gain_ref, normed_ref, inv_ref, probs_ref, probs_b_ref,
    q_ref, k_ref, v_ref, cos_ref, sin_ref, gstore_in, pstore_in, gacc_ref,
    out_ref, gstore_ref, pstore_ref, gacc_out,
):
    head = q_ref.shape[-1]
    score_scale = head ** (-0.5)
    grad_in = jnp.where(scal[3] == 1, up_ref[...], recv_ref[...])
    ga = jnp.dot(grad_in, wb_ref[...], preferred_element_type=jnp.float32).astype(jnp.bfloat16)
    probs = probs_ref[...]
    gprob = lax.dot_general(
        ga, v_ref[...], (((1,), (1,)), ((), ())), preferred_element_type=jnp.float32
    )
    gs = (probs * (gprob - jnp.sum(gprob * probs, axis=-1, keepdims=True)) * score_scale).astype(
        jnp.bfloat16
    )
    gq = jnp.dot(gs, k_ref[...], preferred_element_type=jnp.float32)
    gk = lax.dot_general(gs, q_ref[...], (((0,), (0,)), ((), ())), preferred_element_type=jnp.float32)
    gv = lax.dot_general(
        probs_b_ref[...], ga, (((0,), (0,)), ((), ())), preferred_element_type=jnp.float32
    )
    cosine = cos_ref[...]
    sine = sin_ref[...]
    gq = gq * cosine + pltpu.roll(gq, head // 2, 1) * sine
    gk = gk * cosine + pltpu.roll(gk, head // 2, 1) * sine
    gp = jnp.concatenate([gq, gk, gv], axis=-1).astype(jnp.bfloat16)
    gh = lax.dot_general(gp, wp_ref[...], (((1,), (1,)), ((), ())), preferred_element_type=jnp.float32)
    normed = normed_ref[...]
    gain_term = jnp.sum(gh * normed, axis=0, keepdims=True)
    gn = gh * gain_ref[...]
    mean = jnp.sum(gn * normed, axis=-1, keepdims=True) * (1.0 / gn.shape[-1])
    gx = inv_ref[...] * (gn - normed * mean)
    out_ref[...] = (grad_in.astype(jnp.float32) + gx).astype(out_ref.dtype)
    gstore_ref[...] = grad_in
    pstore_ref[...] = gp
    gacc_out[...] = gacc_ref[...] + jnp.where(scal[2] == 1, gain_term, 0.0)


def tick_call(scal, recv, upstream, w_back, w_proj, gain_row, normed, inv_rms, probs, probs_b,
              query_rows, key_rows, value_rows, cos2, sin2, grad_store, proj_store, gain_acc):
    micro_count, length, width = normed.shape
    head = query_rows.shape[-1]
    full = lambda shape: pl.BlockSpec(shape, lambda i, s: (0,) * len(shape))
    per_micro = lambda shape: pl.BlockSpec((None,) + shape, lambda i, s: (s[0],) + (0,) * len(shape))
    per_slot = lambda shape: pl.BlockSpec((None,) + shape, lambda i, s: (s[1],) + (0,) * len(shape))
    flops = 2 * length * width * 4 * head * 2
    return pl.pallas_call(
        tick_kernel,
        out_shape=(
            jax.ShapeDtypeStruct((length, width), jnp.bfloat16),
            jax.ShapeDtypeStruct(grad_store.shape, grad_store.dtype),
            jax.ShapeDtypeStruct(proj_store.shape, proj_store.dtype),
            jax.ShapeDtypeStruct(gain_acc.shape, gain_acc.dtype),
        ),
        grid_spec=pltpu.PrefetchScalarGridSpec(
            num_scalar_prefetch=1,
            grid=(1,),
            in_specs=[
                full((length, width)),
                per_micro((length, width)),
                full((width, head)),
                full((width, 3 * head)),
                full((1, width)),
                per_micro((length, width)),
                per_micro((length, 1)),
                per_micro((length, length)),
                per_micro((length, length)),
                per_micro((length, head)),
                per_micro((length, head)),
                per_micro((length, head)),
                full((length, head)),
                full((length, head)),
                pl.BlockSpec(memory_space=pl.ANY),
                pl.BlockSpec(memory_space=pl.ANY),
                full((1, width)),
            ],
            out_specs=[
                full((length, width)),
                per_slot((length, width)),
                per_slot((length, 3 * head)),
                full((1, width)),
            ],
        ),
        input_output_aliases={15: 1, 16: 2, 17: 3},
        cost_estimate=pl.CostEstimate(
            flops=flops, transcendentals=0, bytes_accessed=2 * width * 4 * head + 8 * length * width
        ),
        compiler_params=pltpu.CompilerParams(vmem_limit_bytes=48 * 1024 * 1024),
    )(scal, recv, upstream, w_back, w_proj, gain_row, normed, inv_rms, probs, probs_b,
      query_rows, key_rows, value_rows, cos2, sin2, grad_store, proj_store, gain_acc)


def unpack_kernel(rows_ref, gain_ref, wp_ref, wb_ref, gain_out):
    proj_cols = wp_ref.shape[-1]
    rows = rows_ref.shape[2]
    fc, fz = rows_ref.shape[0], rows_ref.shape[1]
    for z in range(fz):
        for core in range(fc):
            at = z * fc + core
            block = rows_ref[core, z]
            wp_ref[at * rows : (at + 1) * rows, :] = block[:, :proj_cols]
            wb_ref[at * rows : (at + 1) * rows, :] = block[:, proj_cols:]
            gain_out[at : at + 1, :] = gain_ref[core, z, 0:1, : gain_out.shape[-1]].astype(jnp.float32)


def unpack_weights(staged, rows_here, head):
    cols = staged.shape[-1]
    groups = FC * FZ * FX
    span = FC * FZ
    return pl.pallas_call(
        unpack_kernel,
        out_shape=(
            jax.ShapeDtypeStruct((groups * rows_here, 3 * head), staged.dtype),
            jax.ShapeDtypeStruct((groups * rows_here, cols - 3 * head), staged.dtype),
            jax.ShapeDtypeStruct((FX, span, rows_here), jnp.float32),
        ),
        grid=(FX,),
        in_specs=[
            pl.BlockSpec((FC, FZ, None, rows_here, cols), lambda x: (0, 0, x, 0, 0)),
            pl.BlockSpec((FC, FZ, None, 16, cols), lambda x: (0, 0, x, rows_here // 16, 0)),
        ],
        out_specs=[
            pl.BlockSpec((span * rows_here, 3 * head), lambda x: (x, 0)),
            pl.BlockSpec((span * rows_here, cols - 3 * head), lambda x: (x, 0)),
            pl.BlockSpec((None, span, rows_here), lambda x: (x, 0, 0)),
        ],
    )(staged, staged)

def terms_kernel(hid_ref, g_ref, gp_ref, att_ref, out_ref):
    tokens = hid_ref.shape[0]
    fc, fz, rows = out_ref.shape[0], out_ref.shape[1], out_ref.shape[2]
    gp = gp_ref[...].reshape(tokens, gp_ref.shape[-1])
    grads = g_ref[...].reshape(tokens, g_ref.shape[-1])
    att = att_ref[...]
    for z in range(fz):
        for core in range(fc):
            at = z * fc + core
            cut = slice(at * rows, (at + 1) * rows)
            first = lax.dot_general(
                hid_ref[:, cut], gp, (((0,), (0,)), ((), ())), preferred_element_type=jnp.float32
            )
            second = lax.dot_general(
                grads[:, cut], att, (((0,), (0,)), ((), ())), preferred_element_type=jnp.float32
            )
            out_ref[core, z] = jnp.concatenate([first, second], axis=-1).astype(out_ref.dtype)


def weight_terms(hidden_flat, grad_store, proj_store, att_flat, rows_here):
    tokens, width = hidden_flat.shape
    micro_count, length = grad_store.shape[0] - 2, grad_store.shape[1]
    cols = proj_store.shape[-1] + att_flat.shape[-1]
    span = FC * FZ * rows_here
    out = pl.pallas_call(
        terms_kernel,
        out_shape=jax.ShapeDtypeStruct((FC, FZ, FX, rows_here, cols), jnp.bfloat16),
        grid=(FX,),
        in_specs=[
            pl.BlockSpec((tokens, span), lambda x: (0, x)),
            pl.BlockSpec((micro_count, length, span), lambda x: (0, 0, x)),
            pl.BlockSpec((micro_count, length, proj_store.shape[-1]), lambda x: (0, 0, 0)),
            pl.BlockSpec((tokens, att_flat.shape[-1]), lambda x: (0, 0)),
        ],
        out_specs=pl.BlockSpec((FC, FZ, None, rows_here, cols), lambda x: (0, 0, x, 0, 0)),
    )(hidden_flat, grad_store, proj_store, att_flat)
    return out.reshape(width, cols)

def on_device(inputs, upstream, weights, gain):
    sections = SH * SY
    here = lax.axis_index("sh") * SY + lax.axis_index("sy")
    micro_count = inputs.shape[1]
    length = inputs.shape[2]
    width = inputs.shape[3]
    head = weights.shape[2] // 4
    rows_here = weights.shape[1]
    groups = FX * FZ * FC

    gain_rows = jnp.zeros((16, weights.shape[2]), jnp.bfloat16)
    gain_rows = lax.dynamic_update_slice(gain_rows, gain[0][None, :], (0, 0))
    packed = jnp.concatenate([weights[0], gain_rows], axis=0)
    staged = lax.all_gather(packed, "fx", axis=0, tiled=True)
    staged = lax.all_gather(staged, "fz", axis=0, tiled=True)
    staged = lax.all_gather(staged, "fc", axis=0, tiled=True)
    w_proj, w_back, gain_row = unpack_weights(
        staged.reshape(FC, FZ, FX, rows_here + 16, weights.shape[2]), rows_here, head
    )
    gain_row = gain_row.reshape(1, groups * rows_here)
    wide_gain = gain_row.reshape(groups * rows_here)

    xfloat = inputs[0].astype(jnp.float32)
    inv_rms = lax.rsqrt(jnp.mean(xfloat * xfloat, axis=-1, keepdims=True) + 1e-05)
    normed = xfloat * inv_rms
    hidden = (normed * wide_gain).astype(jnp.bfloat16)
    proj = jnp.dot(
        hidden.reshape(micro_count * length, width), w_proj, preferred_element_type=jnp.float32
    ).reshape(micro_count, length, 3 * head)
    cosine, sine_table = rope_tables(length, head)
    query_rows = rotate(proj[..., :head], cosine, sine_table).astype(jnp.bfloat16)
    key_rows = rotate(proj[..., head : 2 * head], cosine, sine_table).astype(jnp.bfloat16)
    value_rows = proj[..., 2 * head :].astype(jnp.bfloat16)
    score_scale = head ** (-0.5)
    causal = lax.broadcasted_iota(jnp.int32, (length, length), 0) >= lax.broadcasted_iota(
        jnp.int32, (length, length), 1
    )
    scores = jnp.einsum(
        "mqh,mkh->mqk", query_rows, key_rows, preferred_element_type=jnp.float32
    ) * score_scale
    probs = jax.nn.softmax(jnp.where(causal[None], scores, -1e30), axis=-1)
    probs_b = probs.astype(jnp.bfloat16)
    attended = jnp.einsum(
        "mqk,mkh->mqh", probs_b, value_rows, preferred_element_type=jnp.float32
    ).astype(jnp.bfloat16)

    cos2 = jnp.concatenate([cosine, cosine], axis=-1)
    sin2 = jnp.concatenate([sine_table, -sine_table], axis=-1)

    def tick(tick_no, received, state):
        grad_store, proj_store, gain_acc = state
        micro = tick_no - (sections - 1 - here)
        active = jnp.logical_and(micro >= 0, micro < micro_count)
        clipped = jnp.clip(micro, 0, micro_count - 1)
        slot = jnp.where(active, micro, jnp.where(micro < 0, micro_count, micro_count + 1))
        scal = jnp.stack(
            [clipped, slot, active.astype(jnp.int32), (here == sections - 1).astype(jnp.int32)]
        ).astype(jnp.int32)
        grad_out, grad_store, proj_store, gain_acc = tick_call(
            scal, received, upstream, w_back, w_proj, gain_row, normed, inv_rms, probs, probs_b,
            query_rows, key_rows, value_rows, cos2, sin2, grad_store, proj_store, gain_acc.reshape(1, width),
        )
        return grad_out, (grad_store, proj_store, gain_acc.reshape(width))

    def step_loop(tick_no, carry):
        received, state = carry
        sent, state = tick(tick_no, received, state)
        received = passed_along(sent, SECTION, -1)
        return (received, state)

    state_start = (
        jnp.zeros((micro_count + 2, length, width), jnp.bfloat16),
        jnp.zeros((micro_count + 2, length, 3 * head), jnp.bfloat16),
        jnp.zeros((width,), jnp.float32),
    )
    total_ticks = sections + micro_count - 1
    received, state = lax.fori_loop(
        0, total_ticks - 1, step_loop, (jnp.zeros((length, width), jnp.bfloat16), state_start)
    )
    leftover, state = tick(total_ticks - 1, received, state)
    grad_store, proj_store, gain_acc = state
    tokens_all = micro_count * length
    terms = weight_terms(
        hidden.reshape(tokens_all, width), grad_store, proj_store,
        attended.reshape(tokens_all, head), rows_here,
    )
    cols = terms.shape[1]
    terms = lax.psum_scatter(terms.reshape(FC, -1, cols), "fc", scatter_dimension=0, tiled=True)
    terms = lax.psum_scatter(terms.reshape(FZ, -1, cols), "fz", scatter_dimension=0, tiled=True)
    gain_sum = gain_acc
    for axis in ("fc", "fz", "fx"):
        gain_sum = jnp.sum(lax.all_gather(gain_sum, axis, axis=0), axis=0)
    terms, gain_sum = lax.optimization_barrier((terms, gain_sum))
    terms = lax.psum_scatter(terms.reshape(FX, -1, cols), "fx", scatter_dimension=0, tiled=True)
    shard = terms.reshape(rows_here, cols).astype(jnp.float32)
    return (shard[None], gain_sum[None])


def solution(mesh):
    global SH, SY, FX, FZ, FC
    sections = mesh.shape["section"]
    groups = mesh.shape["fsdp"]
    SH, SY = 2, sections // 2
    FX, FZ, FC = 2, groups // 4, 2
    sub_mesh = Mesh(
        mesh.devices.reshape(SH, SY, FX, FZ, FC), ("sh", "sy", "fx", "fz", "fc")
    )
    return jax.shard_map(
        on_device,
        mesh=sub_mesh,
        in_specs=(
            P(SECTION, None, FSDP, None),
            P(None, FSDP, None),
            P(SECTION, FSDP, None),
            P(SECTION, FSDP),
        ),
        out_specs=(P(SECTION, FSDP, None), P(SECTION, None)),
        check_vma=False,
    )
```

```python
import jax
import jax.numpy as jnp
from jax import lax
from jax.experimental import pallas as pl
from jax.experimental.pallas import tpu as pltpu
from jax.sharding import Mesh, PartitionSpec as P

SECTION = ("sh", "sy")
FSDP = ("fx", "fz", "fc")
SH, SY, FX, FZ, FC = 2, 8, 2, 8, 2


def passed_along(value, axis, steps):
    count = SH * SY
    leading, last = (max(0, -steps), min(count, count - steps))
    return lax.ppermute(value, axis, [(source, source + steps) for source in range(leading, last)])


def rope_tables(length, head):
    half_head = head // 2
    position = lax.iota(jnp.float32, length)
    freq = jnp.power(500000.0, -2.0 * lax.iota(jnp.float32, half_head) / head)
    angle = position[:, None] * freq[None, :]
    return (jnp.cos(angle), jnp.sin(angle))


def rotate(value_rows, cosine, sine_table):
    half_head = value_rows.shape[-1] // 2
    first = value_rows[..., :half_head]
    second = value_rows[..., half_head:]
    return jnp.concatenate(
        [first * cosine - second * sine_table, second * cosine + first * sine_table], axis=-1
    )


def unrotate(value_rows, cosine, sine_table):
    half_head = value_rows.shape[-1] // 2
    first = value_rows[..., :half_head]
    second = value_rows[..., half_head:]
    return jnp.concatenate(
        [first * cosine + second * sine_table, second * cosine - first * sine_table], axis=-1
    )


def contract_rows(left, right):
    return lax.dot_general(
        left, right, (((0,), (0,)), ((), ())), preferred_element_type=jnp.float32
    )


def contract_cols(left, right):
    return lax.dot_general(
        left, right, (((1,), (1,)), ((), ())), preferred_element_type=jnp.float32
    )


def tick_kernel(
    scal, recv_ref, up_ref, wb_ref, wp_ref, gain_ref, normed_ref, inv_ref, probs_ref, probs_b_ref,
    q_ref, k_ref, v_ref, cos_ref, sin_ref, gstore_in, pstore_in, gacc_ref,
    out_ref, gstore_ref, pstore_ref, gacc_out, wp_vmem, wp_sem,
):
    wp_copy = pltpu.make_async_copy(wp_ref, wp_vmem, wp_sem)
    wp_copy.start()
    head = q_ref.shape[-1]
    score_scale = head ** (-0.5)
    grad_in = jnp.where(scal[3] == 1, up_ref[...], recv_ref[...])
    ga = jnp.dot(grad_in, wb_ref[...], preferred_element_type=jnp.float32).astype(jnp.bfloat16)
    probs = probs_ref[...]
    gprob = lax.dot_general(
        ga, v_ref[...], (((1,), (1,)), ((), ())), preferred_element_type=jnp.float32
    )
    gs = (probs * (gprob - jnp.sum(gprob * probs, axis=-1, keepdims=True)) * score_scale).astype(
        jnp.bfloat16
    )
    gq = jnp.dot(gs, k_ref[...], preferred_element_type=jnp.float32)
    gk = lax.dot_general(gs, q_ref[...], (((0,), (0,)), ((), ())), preferred_element_type=jnp.float32)
    gv = lax.dot_general(
        probs_b_ref[...], ga, (((0,), (0,)), ((), ())), preferred_element_type=jnp.float32
    )
    cosine = cos_ref[...]
    sine = sin_ref[...]
    gq = gq * cosine + pltpu.roll(gq, head // 2, 1) * sine
    gk = gk * cosine + pltpu.roll(gk, head // 2, 1) * sine
    gp = jnp.concatenate([gq, gk, gv], axis=-1).astype(jnp.bfloat16)
    wp_copy.wait()
    gh = lax.dot_general(gp, wp_vmem[...], (((1,), (1,)), ((), ())), preferred_element_type=jnp.float32)
    normed = normed_ref[...]
    gain_term = jnp.sum(gh * normed, axis=0, keepdims=True)
    gn = gh * gain_ref[...]
    mean = jnp.sum(gn * normed, axis=-1, keepdims=True) * (1.0 / gn.shape[-1])
    gx = inv_ref[...] * (gn - normed * mean)
    out_ref[...] = (grad_in.astype(jnp.float32) + gx).astype(out_ref.dtype)
    gstore_ref[...] = grad_in
    pstore_ref[...] = gp
    gacc_out[...] = gacc_ref[...] + jnp.where(scal[2] == 1, gain_term, 0.0)


def tick_call(scal, recv, upstream, w_back, w_proj, gain_row, normed, inv_rms, probs, probs_b,
              query_rows, key_rows, value_rows, cos2, sin2, grad_store, proj_store, gain_acc):
    micro_count, length, width = normed.shape
    head = query_rows.shape[-1]
    full = lambda shape: pl.BlockSpec(shape, lambda i, s: (0,) * len(shape))
    per_micro = lambda shape: pl.BlockSpec((None,) + shape, lambda i, s: (s[0],) + (0,) * len(shape))
    per_slot = lambda shape: pl.BlockSpec((None,) + shape, lambda i, s: (s[1],) + (0,) * len(shape))
    flops = 2 * length * width * 4 * head * 2
    return pl.pallas_call(
        tick_kernel,
        out_shape=(
            jax.ShapeDtypeStruct((length, width), jnp.bfloat16),
            jax.ShapeDtypeStruct(grad_store.shape, grad_store.dtype),
            jax.ShapeDtypeStruct(proj_store.shape, proj_store.dtype),
            jax.ShapeDtypeStruct(gain_acc.shape, gain_acc.dtype),
        ),
        grid_spec=pltpu.PrefetchScalarGridSpec(
            num_scalar_prefetch=1,
            grid=(1,),
            in_specs=[
                full((length, width)),
                per_micro((length, width)),
                full((width, head)),
                pl.BlockSpec(memory_space=pl.ANY),
                full((1, width)),
                per_micro((length, width)),
                per_micro((length, 1)),
                per_micro((length, length)),
                per_micro((length, length)),
                per_micro((length, head)),
                per_micro((length, head)),
                per_micro((length, head)),
                full((length, head)),
                full((length, head)),
                pl.BlockSpec(memory_space=pl.ANY),
                pl.BlockSpec(memory_space=pl.ANY),
                full((1, width)),
            ],
            out_specs=[
                full((length, width)),
                per_slot((length, width)),
                per_slot((length, 3 * head)),
                full((1, width)),
            ],
            scratch_shapes=[
                pltpu.VMEM((width, 3 * head), w_proj.dtype),
                pltpu.SemaphoreType.DMA(()),
            ],
        ),
        input_output_aliases={15: 1, 16: 2, 17: 3},
        cost_estimate=pl.CostEstimate(
            flops=flops, transcendentals=0, bytes_accessed=2 * width * 4 * head + 8 * length * width
        ),
        compiler_params=pltpu.CompilerParams(vmem_limit_bytes=48 * 1024 * 1024),
    )(scal, recv, upstream, w_back, w_proj, gain_row, normed, inv_rms, probs, probs_b,
      query_rows, key_rows, value_rows, cos2, sin2, grad_store, proj_store, gain_acc)


def unpack_kernel(rows_ref, gain_ref, wp_ref, wb_ref, gain_out):
    proj_cols = wp_ref.shape[-1]
    rows = rows_ref.shape[2]
    fc, fz = rows_ref.shape[0], rows_ref.shape[1]
    for z in range(fz):
        for core in range(fc):
            at = z * fc + core
            block = rows_ref[core, z]
            wp_ref[at * rows : (at + 1) * rows, :] = block[:, :proj_cols]
            wb_ref[at * rows : (at + 1) * rows, :] = block[:, proj_cols:]
            gain_out[at : at + 1, :] = gain_ref[core, z, 0:1, : gain_out.shape[-1]].astype(jnp.float32)


def unpack_weights(staged, rows_here, head):
    cols = staged.shape[-1]
    groups = FC * FZ * FX
    span = FC * FZ
    return pl.pallas_call(
        unpack_kernel,
        out_shape=(
            jax.ShapeDtypeStruct((groups * rows_here, 3 * head), staged.dtype),
            jax.ShapeDtypeStruct((groups * rows_here, cols - 3 * head), staged.dtype),
            jax.ShapeDtypeStruct((FX, span, rows_here), jnp.float32),
        ),
        grid=(FX,),
        in_specs=[
            pl.BlockSpec((FC, FZ, None, rows_here, cols), lambda x: (0, 0, x, 0, 0)),
            pl.BlockSpec((FC, FZ, None, 16, cols), lambda x: (0, 0, x, rows_here // 16, 0)),
        ],
        out_specs=[
            pl.BlockSpec((span * rows_here, 3 * head), lambda x: (x, 0)),
            pl.BlockSpec((span * rows_here, cols - 3 * head), lambda x: (x, 0)),
            pl.BlockSpec((None, span, rows_here), lambda x: (x, 0, 0)),
        ],
    )(staged, staged)

def terms_kernel(hid_ref, g_ref, gp_ref, att_ref, out_ref):
    tokens = hid_ref.shape[0]
    fc, fz, rows = out_ref.shape[0], out_ref.shape[1], out_ref.shape[2]
    gp = gp_ref[...].reshape(tokens, gp_ref.shape[-1])
    grads = g_ref[...].reshape(tokens, g_ref.shape[-1])
    att = att_ref[...]
    for z in range(fz):
        for core in range(fc):
            at = z * fc + core
            cut = slice(at * rows, (at + 1) * rows)
            first = lax.dot_general(
                hid_ref[:, cut], gp, (((0,), (0,)), ((), ())), preferred_element_type=jnp.float32
            )
            second = lax.dot_general(
                grads[:, cut], att, (((0,), (0,)), ((), ())), preferred_element_type=jnp.float32
            )
            out_ref[core, z] = jnp.concatenate([first, second], axis=-1).astype(out_ref.dtype)


def weight_terms(hidden_flat, grad_store, proj_store, att_flat, rows_here):
    tokens, width = hidden_flat.shape
    micro_count, length = grad_store.shape[0] - 2, grad_store.shape[1]
    cols = proj_store.shape[-1] + att_flat.shape[-1]
    span = FC * FZ * rows_here
    out = pl.pallas_call(
        terms_kernel,
        out_shape=jax.ShapeDtypeStruct((FC, FZ, FX, rows_here, cols), jnp.bfloat16),
        grid=(FX,),
        in_specs=[
            pl.BlockSpec((tokens, span), lambda x: (0, x)),
            pl.BlockSpec((micro_count, length, span), lambda x: (0, 0, x)),
            pl.BlockSpec((micro_count, length, proj_store.shape[-1]), lambda x: (0, 0, 0)),
            pl.BlockSpec((tokens, att_flat.shape[-1]), lambda x: (0, 0)),
        ],
        out_specs=pl.BlockSpec((FC, FZ, None, rows_here, cols), lambda x: (0, 0, x, 0, 0)),
    )(hidden_flat, grad_store, proj_store, att_flat)
    return out.reshape(width, cols)

def on_device(inputs, upstream, weights, gain):
    sections = SH * SY
    here = lax.axis_index("sh") * SY + lax.axis_index("sy")
    micro_count = inputs.shape[1]
    length = inputs.shape[2]
    width = inputs.shape[3]
    head = weights.shape[2] // 4
    rows_here = weights.shape[1]
    groups = FX * FZ * FC

    gain_rows = jnp.zeros((16, weights.shape[2]), jnp.bfloat16)
    gain_rows = lax.dynamic_update_slice(gain_rows, gain[0][None, :], (0, 0))
    packed = jnp.concatenate([weights[0], gain_rows], axis=0)
    staged = lax.all_gather(packed, "fx", axis=0, tiled=True)
    staged = lax.all_gather(staged, "fz", axis=0, tiled=True)
    staged = lax.all_gather(staged, "fc", axis=0, tiled=True)
    w_proj, w_back, gain_row = unpack_weights(
        staged.reshape(FC, FZ, FX, rows_here + 16, weights.shape[2]), rows_here, head
    )
    gain_row = gain_row.reshape(1, groups * rows_here)
    wide_gain = gain_row.reshape(groups * rows_here)

    xfloat = inputs[0].astype(jnp.float32)
    inv_rms = lax.rsqrt(jnp.mean(xfloat * xfloat, axis=-1, keepdims=True) + 1e-05)
    normed = xfloat * inv_rms
    hidden = (normed * wide_gain).astype(jnp.bfloat16)
    proj = jnp.dot(
        hidden.reshape(micro_count * length, width), w_proj, preferred_element_type=jnp.float32
    ).reshape(micro_count, length, 3 * head)
    cosine, sine_table = rope_tables(length, head)
    query_rows = rotate(proj[..., :head], cosine, sine_table).astype(jnp.bfloat16)
    key_rows = rotate(proj[..., head : 2 * head], cosine, sine_table).astype(jnp.bfloat16)
    value_rows = proj[..., 2 * head :].astype(jnp.bfloat16)
    score_scale = head ** (-0.5)
    causal = lax.broadcasted_iota(jnp.int32, (length, length), 0) >= lax.broadcasted_iota(
        jnp.int32, (length, length), 1
    )
    scores = jnp.einsum(
        "mqh,mkh->mqk", query_rows, key_rows, preferred_element_type=jnp.float32
    ) * score_scale
    probs = jax.nn.softmax(jnp.where(causal[None], scores, -1e30), axis=-1)
    probs_b = probs.astype(jnp.bfloat16)
    attended = jnp.einsum(
        "mqk,mkh->mqh", probs_b, value_rows, preferred_element_type=jnp.float32
    ).astype(jnp.bfloat16)

    cos2 = jnp.concatenate([cosine, cosine], axis=-1)
    sin2 = jnp.concatenate([sine_table, -sine_table], axis=-1)

    def tick(tick_no, received, state):
        grad_store, proj_store, gain_acc = state
        micro = tick_no - (sections - 1 - here)
        active = jnp.logical_and(micro >= 0, micro < micro_count)
        clipped = jnp.clip(micro, 0, micro_count - 1)
        slot = jnp.where(active, micro, jnp.where(micro < 0, micro_count, micro_count + 1))
        scal = jnp.stack(
            [clipped, slot, active.astype(jnp.int32), (here == sections - 1).astype(jnp.int32)]
        ).astype(jnp.int32)
        grad_out, grad_store, proj_store, gain_acc = tick_call(
            scal, received, upstream, w_back, w_proj, gain_row, normed, inv_rms, probs, probs_b,
            query_rows, key_rows, value_rows, cos2, sin2, grad_store, proj_store, gain_acc.reshape(1, width),
        )
        return grad_out, (grad_store, proj_store, gain_acc.reshape(width))

    def step_loop(tick_no, carry):
        received, state = carry
        sent, state = tick(tick_no, received, state)
        received = passed_along(sent, SECTION, -1)
        return (received, state)

    state_start = (
        jnp.zeros((micro_count + 2, length, width), jnp.bfloat16),
        jnp.zeros((micro_count + 2, length, 3 * head), jnp.bfloat16),
        jnp.zeros((width,), jnp.float32),
    )
    total_ticks = sections + micro_count - 1
    received, state = lax.fori_loop(
        0, total_ticks - 1, step_loop, (jnp.zeros((length, width), jnp.bfloat16), state_start)
    )
    leftover, state = tick(total_ticks - 1, received, state)
    grad_store, proj_store, gain_acc = state
    tokens_all = micro_count * length
    terms = weight_terms(
        hidden.reshape(tokens_all, width), grad_store, proj_store,
        attended.reshape(tokens_all, head), rows_here,
    )
    cols = terms.shape[1]
    terms = lax.psum_scatter(terms.reshape(FC, -1, cols), "fc", scatter_dimension=0, tiled=True)
    terms = lax.psum_scatter(terms.reshape(FZ, -1, cols), "fz", scatter_dimension=0, tiled=True)
    gain_sum = jnp.sum(lax.all_gather(gain_acc, FSDP, axis=0), axis=0)
    terms, gain_sum = lax.optimization_barrier((terms, gain_sum))
    terms = lax.psum_scatter(terms.reshape(FX, -1, cols), "fx", scatter_dimension=0, tiled=True)
    shard = terms.reshape(rows_here, cols).astype(jnp.float32)
    return (shard[None], gain_sum[None])


def solution(mesh):
    global SH, SY, FX, FZ, FC
    sections = mesh.shape["section"]
    groups = mesh.shape["fsdp"]
    SH, SY = 2, sections // 2
    FX, FZ, FC = 2, groups // 4, 2
    sub_mesh = Mesh(
        mesh.devices.reshape(SH, SY, FX, FZ, FC), ("sh", "sy", "fx", "fz", "fc")
    )
    return jax.shard_map(
        on_device,
        mesh=sub_mesh,
        in_specs=(
            P(SECTION, None, FSDP, None),
            P(None, FSDP, None),
            P(SECTION, FSDP, None),
            P(SECTION, FSDP),
        ),
        out_specs=(P(SECTION, FSDP, None), P(SECTION, None)),
        check_vma=False,
    )
```
